32 devices in a mesh: task: 4 (over x, core), feat: 8 (over z, y).
Axes of the slice: x: 2, y: 2, z: 4, core: 2. Of those that a mesh axis runs over, the one named last changes fastest.
Arguments:
- tokens: bfloat16 [8, 512, 8, 512], P('task', None, 'feat'), may hold values from -6 to 6
- cotangent: bfloat16 [8, 512, 8, 512], P('task', None, 'feat'), may hold values from -6 to 6
- counts: int32 [8], P('task'), may hold values from 51 to 512, as said below
- sample_gain: bfloat16 [512], P('feat'), may hold values from 0.25 to 1.75
- sample_shift: bfloat16 [512], P('feat'), may hold values from -2 to 2
- sample_project: bfloat16 [512, 1536], P('feat'), may hold values from -0.25 to 0.25
- sample_merge: bfloat16 [512, 512], P('feat'), may hold values from -1.5 to 1.5
- feature_gain: bfloat16 [512], P('feat'), may hold values from 0.25 to 1.75
- feature_shift: bfloat16 [512], P('feat'), may hold values from -2 to 2
- feature_project: bfloat16 [512, 1536], P('feat'), may hold values from -0.25 to 0.25
- feature_merge: bfloat16 [512, 512], P('feat'), may hold values from -1 to 1
- dense_gain: bfloat16 [512], P('feat'), may hold values from 0.25 to 1.75
- dense_shift: bfloat16 [512], P('feat'), may hold values from -2 to 2
- dense_expand: bfloat16 [512, 2048], P('feat'), may hold values from -0.25 to 0.25
- expand_bias: bfloat16 [2048], P('feat'), may hold values from -3 to 3
- dense_shrink: bfloat16 [2048, 512], P('feat'), may hold values from -0.125 to 0.125
- shrink_bias: bfloat16 [512], P('feat'), may hold values from -2 to 2
Outputs:
- layer_out: bfloat16 [8, 512, 8, 512], P('task', None, 'feat')
- input_grad: float32 [8, 512, 8, 512], P('task', None, 'feat')
- sample_gain_grad: float32 [512], P('feat')
- sample_shift_grad: float32 [512], P('feat')
- sample_project_grad: float32 [512, 1536], P('feat')
- sample_merge_grad: float32 [512, 512], P('feat')
- feature_gain_grad: float32 [512], P('feat')
- feature_shift_grad: float32 [512], P('feat')
- feature_project_grad: float32 [512, 1536], P('feat')
- feature_merge_grad: float32 [512, 512], P('feat')
- dense_gain_grad: float32 [512], P('feat')
- dense_shift_grad: float32 [512], P('feat')
- dense_expand_grad: float32 [512, 2048], P('feat')
- expand_bias_grad: float32 [2048], P('feat')
- dense_shrink_grad: float32 [2048, 512], P('feat')
- shrink_bias_grad: float32 [512], P('feat')
The draws below stay inside these ranges and needn't reach their ends.
Inputs may be any that keep to these rules, and one draw needn't show every extreme that they name: `counts`: some task has exactly 512 live samples and some exactly 51.
All inputs are finite; a program needn't handle non-finite values.
Results may differ from the reference program's by a relative error of at most 0.023.
Values may be sent and summed in bfloat16 or wider, within the bound.
A program may use at most 192 MiB of HBM per device.

```python
import jax
import jax.numpy as jnp
from jax import lax

D = 512
HEADS = 8
FF = 2048
SAMPLES = 512
LEAST = 51
TASKS = 8
FEATURES = 8


def draw_counts(key, part):
    values = jax.random.randint(jax.random.fold_in(key, 11), (TASKS,), LEAST, SAMPLES + 1)
    order = jax.random.permutation(jax.random.fold_in(key, 12), TASKS)
    values = values.at[order[0]].set(SAMPLES)
    values = values.at[order[1]].set(LEAST)
    return values.astype(jnp.int32)


def block_scale(rng, shape, split, low, top_value):
    gain = 1.0
    for axis_at, shards_of in split:
        draws = jax.random.uniform(jax.random.fold_in(jax.random.fold_in(rng, 6), axis_at), (shards_of,), jnp.float32, low / len(split), top_value / len(split))
        gain = gain * jnp.repeat(jnp.exp(draws), shape[axis_at] // shards_of).reshape((-1,) + (1,) * (len(shape) - 1 - axis_at))
    return gain


def bell_draw(key, extent, scale, reach, cuts=(), kind=jnp.bfloat16):
    gain = block_scale(key, extent, cuts, -0.22, 0.18) if cuts else 1.0
    drawn = jax.random.normal(key, extent, jnp.float32) * scale * gain
    return jnp.minimum(jnp.maximum(drawn, -reach), reach).astype(kind)


def setup_inputs(seed: int = 0) -> dict:
    streams_of = jax.random.split(jax.random.key(seed), 18)
    return {
        "tokens": bell_draw(streams_of[0], (TASKS, SAMPLES, FEATURES, D), 1.0, 6.0, ((0, 4), (2, 8))),
        "cotangent": bell_draw(streams_of[1], (TASKS, SAMPLES, FEATURES, D), 1.0, 6.0, ((0, 4), (2, 8))),
        "counts": draw_counts(jax.random.fold_in(streams_of[17], 71), 0),
        "sample_gain": jnp.clip(1.0 + 0.15 * jax.random.normal(streams_of[3], (D,), jnp.float32), 0.25, 1.75).astype(jnp.bfloat16),
        "sample_shift": bell_draw(streams_of[4], (D,), 0.3, 2.0, ((0, 8),)),
        "sample_project": bell_draw(streams_of[5], (D, 3 * D), D ** -0.5, 0.25, ((0, 8),)),
        "sample_merge": bell_draw(streams_of[6], (D, D), (D // 32) ** -0.5, 1.5, ((0, 8),)),
        "feature_gain": jnp.clip(1.0 + 0.15 * jax.random.normal(streams_of[7], (D,), jnp.float32), 0.25, 1.75).astype(jnp.bfloat16),
        "feature_shift": bell_draw(streams_of[8], (D,), 0.3, 2.0, ((0, 8),)),
        "feature_project": bell_draw(streams_of[9], (D, 3 * D), D ** -0.5, 0.25, ((0, 8),)),
        "feature_merge": bell_draw(streams_of[10], (D, D), (D // 16) ** -0.5, 1.0, ((0, 8),)),
        "dense_gain": jnp.clip(1.0 + 0.15 * jax.random.normal(streams_of[11], (D,), jnp.float32), 0.25, 1.75).astype(jnp.bfloat16),
        "dense_shift": bell_draw(streams_of[12], (D,), 0.3, 2.0, ((0, 8),)),
        "dense_expand": bell_draw(streams_of[13], (D, FF), D ** -0.5, 0.25, ((0, 8),)),
        "expand_bias": bell_draw(streams_of[14], (FF,), 0.5, 3.0, ((0, 8),)),
        "dense_shrink": bell_draw(streams_of[15], (FF, D), FF ** -0.5, 0.125, ((0, 8),)),
        "shrink_bias": bell_draw(streams_of[16], (D,), 0.3, 2.0, ((0, 8),)),
    }


norm_eps = 1e-05
masked_score = -1e+30
highest = lax.Precision.HIGHEST

@jax.custom_vjp
def low(v):
    return lax.optimization_barrier(v.astype(jnp.bfloat16)).astype(jnp.float32)

@jax.custom_vjp
def low_back(v):
    return v

def low_keep(v):
    return (low(v), None)

def low_pass(kept, grad):
    return (grad,)

def back_keep(v):
    return (v, None)

def back_low(kept, grad):
    return (low(grad),)
low.defvjp(low_keep, low_pass)
low_back.defvjp(back_keep, back_low)

def layer_norm(values, norm_gain, norm_shift):
    center = values - lax.optimization_barrier(jnp.mean(values, axis=-1, keepdims=True))
    spread = lax.optimization_barrier(jnp.mean(center * center, axis=-1, keepdims=True))
    return center * lax.rsqrt(spread + norm_eps) * norm_gain + norm_shift

def multiply(row_data, weight):
    flattened = row_data.reshape(-1, row_data.shape[-1])
    result = jnp.dot(flattened, weight, precision=highest, preferred_element_type=jnp.float32)
    return result.reshape(row_data.shape[:-1] + (weight.shape[1],))

def attention(triple, key_live):
    batches, length = (triple.shape[0], triple.shape[1])
    pieces = triple.reshape(batches, length, 3, HEADS, D // HEADS)
    query_rows, key_rows, value_rows = (pieces[:, :, 0], pieces[:, :, 1], pieces[:, :, 2])
    scaling = (D // HEADS) ** (-0.5)
    scores = jnp.einsum('blhe,bmhe->bhlm', query_rows, key_rows, precision=highest) * scaling
    scores = low_back(scores)
    scores = jnp.where(key_live[:, None, None, :] > 0, scores, masked_score)
    chances = low(jax.nn.softmax(scores, axis=-1))
    mixture = jnp.einsum('bhlm,bmhe->blhe', chances, value_rows, precision=highest)
    return mixture.reshape(batches, length, D)

def task_forward(source, live_mask, weights):
    gain_one, shift_one, project_one, merge_one, gain_two, shift_two, project_two, merge_two, gain_three, shift_three, expand, bias_in, shrink, bias_out = weights
    keep_mask = live_mask[:, None, None]
    normed = low(layer_norm(source, gain_one, shift_one))
    triple = low(low_back(multiply(normed, project_one)))

    def one_feature(column):
        return attention(column[None], live_mask[None])[0]
    mixture = lax.map(jax.checkpoint(one_feature), jnp.swapaxes(triple, 0, 1))
    mixture = low(low_back(jnp.swapaxes(mixture, 0, 1)))
    hidden_one = source + keep_mask * low_back(multiply(mixture, merge_one))
    normed = low(layer_norm(hidden_one, gain_two, shift_two))
    triple = low(low_back(multiply(normed, project_two)))
    mixture = low(low_back(attention(triple, jnp.ones(triple.shape[:2], jnp.float32))))
    hidden_two = hidden_one + keep_mask * low_back(multiply(mixture, merge_two))
    normed = low(layer_norm(hidden_two, gain_three, shift_three))
    expanded = low_back(multiply(normed, expand) + bias_in)
    activated = low(jax.nn.gelu(expanded))
    return hidden_two + keep_mask * low_back(multiply(activated, shrink) + bias_out)

def reference(tokens, cotangent, counts, sample_gain, sample_shift, sample_project, sample_merge, feature_gain, feature_shift, feature_project, feature_merge, dense_gain, dense_shift, dense_expand, expand_bias, dense_shrink, shrink_bias):
    weights = tuple((member.astype(jnp.float32) for member in (sample_gain, sample_shift, sample_project, sample_merge, feature_gain, feature_shift, feature_project, feature_merge, dense_gain, dense_shift, dense_expand, expand_bias, dense_shrink, shrink_bias)))
    positions = jnp.arange(SAMPLES, dtype=jnp.int32)

    def one_task(carried, item):
        source, upstream, count = item
        live_mask = (positions < count).astype(jnp.float32)

        def forward(values, params):
            return task_forward(values, live_mask, params)
        result, pull = jax.vjp(forward, source.astype(jnp.float32), weights)
        grad_source, grad_params = pull(upstream.astype(jnp.float32))
        carried = tuple((summed + added for summed, added in zip(carried, grad_params)))
        return (carried, (result.astype(jnp.bfloat16), grad_source))
    zeros_start = tuple((jnp.zeros_like(member) for member in weights))
    totals, (layer_out, input_grad) = lax.scan(one_task, zeros_start, (tokens, cotangent, counts))
    return (layer_out, input_grad) + totals
```

```python
import functools

import jax
import jax.numpy as jnp
from jax import lax
from jax.experimental import pallas as pl
from jax.experimental.pallas import tpu as pltpu
from jax.sharding import PartitionSpec as P

HEADS = 8
NORM_EPS = 1e-05
MASKED = -1e30
PAIR = 128
GROUP = 16
F32 = jnp.float32
BF16 = jnp.bfloat16


def nt(left, right):
    return lax.dot_general(left, right, (((1,), (1,)), ((), ())), preferred_element_type=F32)


def tn(left, right):
    return lax.dot_general(left, right, (((0,), (0,)), ((), ())), preferred_element_type=F32)


def nn(left, right):
    return lax.dot_general(left, right, (((1,), (0,)), ((), ())), preferred_element_type=F32)


def normalise(values):
    center = values - jnp.mean(values, axis=-1, keepdims=True)
    spread = jnp.mean(center * center, axis=-1, keepdims=True)
    scale = lax.rsqrt(spread + NORM_EPS)
    return center * scale, scale


def normalise_back(incoming, normed, scale, gain):
    weighted = incoming * gain
    first = jnp.mean(weighted, axis=-1, keepdims=True)
    second = jnp.mean(weighted * normed, axis=-1, keepdims=True)
    return scale * (weighted - first - normed * second)


def head_masks(scale):
    lane = lax.broadcasted_iota(jnp.int32, (1, PAIR), 1)
    low = jnp.where(lane < PAIR // 2, scale, 0.0).astype(BF16)
    high = jnp.where(lane < PAIR // 2, 0.0, scale).astype(BF16)
    return low, high


def two_heads(rows, scale):
    low, high = head_masks(scale)
    return jnp.concatenate([rows * low, rows * high], axis=0)


def join_heads(turned, length):
    half = PAIR // 2
    joined = jnp.concatenate([turned[:half, :length], turned[half:, length:]], axis=0)
    return joined.T


def attend(query, key, value_turned, bias, head_scale):
    scores = nt(key, two_heads(query, head_scale)) + bias
    top = jnp.max(scores, axis=0, keepdims=True)
    expo = jnp.exp(scores - top)
    total = jnp.sum(expo, axis=0, keepdims=True)
    chances = (expo * (1.0 / total)).astype(BF16)
    mixed = join_heads(nn(value_turned, chances), query.shape[0])
    return mixed, top + jnp.log(total)


def attend_back(query, key, value, key_turned, grad_out, log_total, bias, head_scale):
    queries = two_heads(query, head_scale)
    scores = nt(key, queries) + bias
    chances = jnp.exp(scores - log_total)
    grads = two_heads(grad_out, 1.0)
    grad_chances = nt(value, grads)
    inner = jnp.sum(chances * grad_chances, axis=0, keepdims=True)
    grad_scores = (chances * (grad_chances - inner)).astype(BF16)
    grad_value = nn(chances.astype(BF16), grads)
    grad_key = nn(grad_scores, queries)
    grad_query = join_heads(nn(key_turned, grad_scores), query.shape[0]) * head_scale
    return grad_query, grad_key, grad_value


def sample_forward_kernel(
    counts_ref, tokens_ref, gain_ref, shift_ref, project_ref, merge_ref,
    triple_ref, mixed_ref, logs_ref, hidden_ref,
):
    count = counts_ref[pl.program_id(0)]
    samples, width = tokens_ref.shape[1:]
    chunk = min(256, samples)
    gain = gain_ref[...].astype(F32)
    shift = shift_ref[...].astype(F32)
    for start in range(0, samples, chunk):
        rows = tokens_ref[0, pl.ds(start, chunk), :].astype(F32)
        normed = (normalise(rows)[0] * gain + shift).astype(BF16)
        triple_ref[0, pl.ds(start, chunk), :] = nn(normed, project_ref[...]).astype(BF16)
    keys = lax.broadcasted_iota(jnp.int32, (samples, 1), 0)
    bias = jnp.where(keys < count, 0.0, MASKED)
    head_scale = (width // HEADS) ** (-0.5)
    pairs = width // PAIR

    def one_pair(pair, carry):
        lanes = pl.multiple_of(pair * PAIR, PAIR)
        key = triple_ref[0, :, pl.ds(lanes + width, PAIR)]
        value_turned = triple_ref[0, :, pl.ds(lanes + 2 * width, PAIR)].T
        for at in range(samples // PAIR):
            query = triple_ref[0, pl.ds(at * PAIR, PAIR), pl.ds(lanes, PAIR)]
            mixed, log_total = attend(query, key, value_turned, bias, head_scale)
            mixed_ref[0, pl.ds(at * PAIR, PAIR), pl.ds(lanes, PAIR)] = mixed.astype(BF16)
            logs_ref[0, pl.ds(pair * (samples // PAIR) + at, 1), :] = log_total
        return carry

    lax.fori_loop(0, pairs, one_pair, 0)
    for start in range(0, samples, chunk):
        rows = tokens_ref[0, pl.ds(start, chunk), :].astype(F32)
        at = lax.broadcasted_iota(jnp.int32, (chunk, 1), 0) + start
        live = jnp.where(at < count, 1.0, 0.0)
        merged = nn(mixed_ref[0, pl.ds(start, chunk), :], merge_ref[...])
        hidden_ref[0, pl.ds(start, chunk), :] = (rows + live * merged).astype(BF16)


def sample_backward_kernel(
    counts_ref, tokens_ref, gain_ref, shift_ref, project_ref, merge_ref,
    triple_ref, mixed_ref, logs_ref, flow_ref,
    input_grad_ref, project_grad_ref, merge_grad_ref, gain_grad_ref, shift_grad_ref,
    grad_mixed, grad_triple, key_sum, value_sum,
):
    task = pl.program_id(0)
    count = counts_ref[task]
    samples, width = tokens_ref.shape[1:]
    chunk = min(256, samples)
    gain = gain_ref[...].astype(F32)
    shift = shift_ref[...].astype(F32)

    @pl.when(task == 0)
    def _():
        project_grad_ref[...] = jnp.zeros_like(project_grad_ref)
        merge_grad_ref[...] = jnp.zeros_like(merge_grad_ref)
        gain_grad_ref[...] = jnp.zeros_like(gain_grad_ref)
        shift_grad_ref[...] = jnp.zeros_like(shift_grad_ref)

    for start in range(0, samples, chunk):
        at = lax.broadcasted_iota(jnp.int32, (chunk, 1), 0) + start
        live = jnp.where(at < count, 1.0, 0.0)
        branch = (flow_ref[0, pl.ds(start, chunk), :].astype(F32) * live).astype(BF16)
        merge_grad_ref[...] += tn(mixed_ref[0, pl.ds(start, chunk), :], branch)
        grad_mixed[pl.ds(start, chunk), :] = nt(branch, merge_ref[...]).astype(BF16)
    keys = lax.broadcasted_iota(jnp.int32, (samples, 1), 0)
    bias = jnp.where(keys < count, 0.0, MASKED)
    head_scale = (width // HEADS) ** (-0.5)
    pairs = width // PAIR

    def one_pair(pair, carry):
        lanes = pl.multiple_of(pair * PAIR, PAIR)
        key = triple_ref[0, :, pl.ds(lanes + width, PAIR)]
        value = triple_ref[0, :, pl.ds(lanes + 2 * width, PAIR)]
        key_turned = key.T
        for at in range(samples // PAIR):
            query = triple_ref[0, pl.ds(at * PAIR, PAIR), pl.ds(lanes, PAIR)]
            grad_out = grad_mixed[pl.ds(at * PAIR, PAIR), pl.ds(lanes, PAIR)]
            log_total = logs_ref[0, pl.ds(pair * (samples // PAIR) + at, 1), :]
            grad_query, grad_key, grad_value = attend_back(
                query, key, value, key_turned, grad_out, log_total, bias, head_scale
            )
            grad_triple[pl.ds(at * PAIR, PAIR), pl.ds(lanes, PAIR)] = grad_query.astype(BF16)
            if at == 0:
                key_sum[...] = grad_key
                value_sum[...] = grad_value
            else:
                key_sum[...] += grad_key
                value_sum[...] += grad_value
        grad_triple[:, pl.ds(lanes + width, PAIR)] = key_sum[...].astype(BF16)
        grad_triple[:, pl.ds(lanes + 2 * width, PAIR)] = value_sum[...].astype(BF16)
        return carry

    lax.fori_loop(0, pairs, one_pair, 0)
    for start in range(0, samples, chunk):
        rows = tokens_ref[0, pl.ds(start, chunk), :].astype(F32)
        normed, scale = normalise(rows)
        part = grad_triple[pl.ds(start, chunk), :]
        project_grad_ref[...] += tn((normed * gain + shift).astype(BF16), part)
        incoming = nt(part, project_ref[...])
        gain_grad_ref[...] += jnp.sum(incoming * normed, axis=0, keepdims=True)
        shift_grad_ref[...] += jnp.sum(incoming, axis=0, keepdims=True)
        back = normalise_back(incoming, normed, scale, gain)
        input_grad_ref[0, pl.ds(start, chunk), :] = (
            flow_ref[0, pl.ds(start, chunk), :].astype(F32) + back
        )


def block_kernel(
    rows_per_task, blocks,
    counts_ref, hidden_ref, upstream_ref,
    gain_two_ref, shift_two_ref, project_ref, merge_ref,
    gain_three_ref, shift_three_ref, expand_ref, bias_in_ref, shrink_ref, bias_out_ref,
    out_ref, flow_ref,
    gain_two_grad, shift_two_grad, project_grad, merge_grad,
    gain_three_grad, shift_three_grad, expand_grad, bias_in_grad, shrink_grad, bias_out_grad,
    triple, mixed, logs, grad_mixed, grad_triple, key_sum, value_sum,
):
    step = pl.program_id(0)
    place = lax.axis_index("feat")
    feats, _, width = hidden_ref.shape
    size = feats * GROUP
    rows = blocks * size
    hidden_units = expand_ref.shape[1]
    sums = (
        gain_two_grad, shift_two_grad, project_grad, merge_grad, gain_three_grad,
        shift_three_grad, expand_grad, bias_in_grad, shrink_grad, bias_out_grad,
    )

    @pl.when(step == 0)
    def _():
        for ref in sums:
            ref[...] = jnp.zeros_like(ref)

    def load(ref):
        pieces = [
            ref[:, pl.ds(block * GROUP, GROUP), :].reshape(size, width) for block in range(blocks)
        ]
        return pieces[0] if blocks == 1 else jnp.concatenate(pieces, axis=0)

    def store(ref, values):
        for block in range(blocks):
            piece = values[block * size : (block + 1) * size]
            ref[:, pl.ds(block * GROUP, GROUP), :] = piece.reshape(feats, GROUP, width)

    row = lax.broadcasted_iota(jnp.int32, (rows, 1), 0)
    row = (step * blocks + row // size) * GROUP + row % GROUP
    sample = place * rows_per_task + row % rows_per_task
    count = jnp.zeros_like(row)
    for task in range(counts_ref.shape[0]):
        count = jnp.where(row // rows_per_task == task, counts_ref[task], count)
    live = jnp.where(sample < count, 1.0, 0.0)

    gain_two = gain_two_ref[...].astype(F32)
    shift_two = shift_two_ref[...].astype(F32)
    gain_three = gain_three_ref[...].astype(F32)
    shift_three = shift_three_ref[...].astype(F32)
    hidden_one = load(hidden_ref).astype(F32)
    unit_two, scale_two = normalise(hidden_one)
    normed_two = (unit_two * gain_two + shift_two).astype(BF16)
    triple[...] = nn(normed_two, project_ref[...]).astype(BF16)

    reach = min(PAIR, size)
    key_at = lax.broadcasted_iota(jnp.int32, (size, 2 * reach), 0) % GROUP
    query_at = lax.broadcasted_iota(jnp.int32, (size, 2 * reach), 1) % GROUP
    bias = jnp.where(key_at == query_at, 0.0, MASKED)
    head_scale = (width // HEADS) ** (-0.5)
    parts = size // reach
    pairs = width // PAIR
    for block in range(blocks):
        start = block * size
        for pair in range(pairs):
            lanes = pair * PAIR
            key = triple[pl.ds(start, size), pl.ds(width + lanes, PAIR)]
            value_turned = triple[pl.ds(start, size), pl.ds(2 * width + lanes, PAIR)].T
            for part in range(parts):
                at = start + part * reach
                query = triple[pl.ds(at, reach), pl.ds(lanes, PAIR)]
                result, log_total = attend(query, key, value_turned, bias, head_scale)
                mixed[pl.ds(at, reach), pl.ds(lanes, PAIR)] = result.astype(BF16)
                logs[pl.ds((block * pairs + pair) * parts + part, 1), :] = log_total

    hidden_two = hidden_one + live * nn(mixed[...], merge_ref[...])
    unit_three, scale_three = normalise(hidden_two)
    normed_three = (unit_three * gain_three + shift_three).astype(BF16)
    upstream = load(upstream_ref).astype(F32)
    grad_dense = (upstream * live).astype(BF16)
    bias_out_grad[...] += jnp.sum(grad_dense.astype(F32), axis=0, keepdims=True)
    lanes = min(512, hidden_units)
    dense = None
    incoming = None
    for start in range(0, hidden_units, lanes):
        cut = pl.ds(start, lanes)
        expanded = nn(normed_three, expand_ref[:, cut]) + bias_in_ref[:, cut].astype(F32)
        square = expanded * expanded
        steep = 0.7978845608028654
        bend = jnp.tanh(expanded * (steep + (steep * 0.044715) * square))
        half_up = 0.5 + 0.5 * bend
        activated = (expanded * half_up).astype(BF16)
        slope = half_up + (0.5 * expanded) * (1.0 - bend * bend) * (
            steep + (3.0 * steep * 0.044715) * square
        )
        grad_expanded = (slope * nt(grad_dense, shrink_ref[cut, :])).astype(BF16)
        bias_in_grad[:, cut] += jnp.sum(grad_expanded.astype(F32), axis=0, keepdims=True)
        shrink_grad[cut, :] += tn(activated, grad_dense)
        expand_grad[:, cut] += tn(normed_three, grad_expanded)
        up = nn(activated, shrink_ref[cut, :])
        down = nt(grad_expanded, expand_ref[:, cut])
        dense = up if dense is None else dense + up
        incoming = down if incoming is None else incoming + down
    result = hidden_two + live * (dense + bias_out_ref[...].astype(F32))
    store(out_ref, result.astype(BF16))

    gain_three_grad[...] += jnp.sum(incoming * unit_three, axis=0, keepdims=True)
    shift_three_grad[...] += jnp.sum(incoming, axis=0, keepdims=True)
    flow_two = upstream + normalise_back(incoming, unit_three, scale_three, gain_three)
    branch = (flow_two * live).astype(BF16)
    merge_grad[...] += tn(mixed[...], branch)
    grad_mixed[...] = nt(branch, merge_ref[...]).astype(BF16)
    for block in range(blocks):
        start = block * size
        for pair in range(pairs):
            lanes = pair * PAIR
            key = triple[pl.ds(start, size), pl.ds(width + lanes, PAIR)]
            value = triple[pl.ds(start, size), pl.ds(2 * width + lanes, PAIR)]
            key_turned = key.T
            for part in range(parts):
                at = start + part * reach
                query = triple[pl.ds(at, reach), pl.ds(lanes, PAIR)]
                grad_out = grad_mixed[pl.ds(at, reach), pl.ds(lanes, PAIR)]
                log_total = logs[pl.ds((block * pairs + pair) * parts + part, 1), :]
                grad_query, grad_key, grad_value = attend_back(
                    query, key, value, key_turned, grad_out, log_total, bias, head_scale
                )
                grad_triple[pl.ds(at, reach), pl.ds(lanes, PAIR)] = grad_query.astype(BF16)
                if part > 0:
                    grad_key += key_sum[...]
                    grad_value += value_sum[...]
                if part == parts - 1:
                    where = pl.ds(start, size)
                    grad_triple[where, pl.ds(width + lanes, PAIR)] = grad_key.astype(BF16)
                    grad_triple[where, pl.ds(2 * width + lanes, PAIR)] = grad_value.astype(BF16)
                else:
                    key_sum[...] = grad_key
                    value_sum[...] = grad_value
    project_grad[...] += tn(normed_two, grad_triple[...])
    incoming = nt(grad_triple[...], project_ref[...])
    gain_two_grad[...] += jnp.sum(incoming * unit_two, axis=0, keepdims=True)
    shift_two_grad[...] += jnp.sum(incoming, axis=0, keepdims=True)
    flow_one = flow_two + normalise_back(incoming, unit_two, scale_two, gain_two)
    store(flow_ref, flow_one.astype(BF16))


VMEM = pl.BlockSpec(memory_space=pltpu.VMEM)
SMEM = pl.BlockSpec(memory_space=pltpu.SMEM)
LIMIT = 56 * 1024 * 1024


def shape(dims, kind):
    return jax.ShapeDtypeStruct(dims, kind)


def by_task(*dims):
    return pl.BlockSpec((1,) + dims, lambda task: (task,) + (0,) * len(dims))


def body(tokens, cotangent, counts, *shards):
    groups = lax.axis_size("feat")
    tasks, samples, local, width = tokens.shape
    rows_per_task = samples // groups
    gathered = [lax.all_gather(part, "feat", axis=0, tiled=True) for part in shards]
    gathered = [part[None, :] if part.ndim == 1 else part for part in gathered]
    (
        gain_one, shift_one, project_one, merge_one, gain_two, shift_two, project_two, merge_two,
        gain_three, shift_three, expand, bias_in, shrink, bias_out,
    ) = gathered
    hidden_units = expand.shape[1]
    source = tokens.reshape(tasks, samples, width)

    def to_blocks(rows):
        rows = rows.reshape(tasks, groups, rows_per_task, width)
        rows = jnp.transpose(rows, (1, 0, 2, 3))
        rows = lax.all_to_all(rows, "feat", split_axis=0, concat_axis=0, tiled=True)
        return rows.reshape(groups, tasks * rows_per_task, width)

    def from_blocks(rows):
        rows = rows.reshape(groups, tasks, rows_per_task, width)
        rows = lax.all_to_all(rows, "feat", split_axis=0, concat_axis=0, tiled=True)
        rows = jnp.transpose(rows, (1, 0, 2, 3))
        return rows.reshape(tasks, samples, width)

    upstream = to_blocks(cotangent.reshape(tasks, samples, width))
    log_rows = samples * width // PAIR // PAIR
    triple, mixed, logs, hidden = pl.pallas_call(
        sample_forward_kernel,
        grid=(tasks,),
        in_specs=[SMEM, by_task(samples, width), VMEM, VMEM, VMEM, VMEM],
        out_specs=[
            by_task(samples, 3 * width), by_task(samples, width),
            by_task(log_rows, 2 * PAIR), by_task(samples, width),
        ],
        out_shape=[
            shape((tasks, samples, 3 * width), BF16),
            shape((tasks, samples, width), BF16),
            shape((tasks, log_rows, 2 * PAIR), F32),
            shape((tasks, samples, width), BF16),
        ],
        compiler_params=pltpu.CompilerParams(vmem_limit_bytes=LIMIT),
        name="sample_forward",
    )(counts, source, gain_one, shift_one, project_one, merge_one)

    hidden = to_blocks(hidden)
    all_rows = tasks * rows_per_task
    size = groups * GROUP
    blocks = max(1, min(all_rows // GROUP, 256 // size))
    steps = all_rows // (GROUP * blocks)
    rows = blocks * size
    slab = pl.BlockSpec((groups, GROUP * blocks, width), lambda step: (0, step, 0))
    reach = min(PAIR, size)
    pieces = blocks * (width // PAIR) * (size // reach)
    grads = [
        shape((1, width), F32), shape((1, width), F32),
        shape((width, 3 * width), F32), shape((width, width), F32),
        shape((1, width), F32), shape((1, width), F32),
        shape((width, hidden_units), F32), shape((1, hidden_units), F32),
        shape((hidden_units, width), F32), shape((1, width), F32),
    ]
    results = pl.pallas_call(
        functools.partial(block_kernel, rows_per_task, blocks),
        grid=(steps,),
        in_specs=[SMEM, slab, slab] + [VMEM] * 10,
        out_specs=[slab, slab] + [VMEM] * 10,
        out_shape=[shape((groups, all_rows, width), BF16)] * 2 + grads,
        scratch_shapes=[
            pltpu.VMEM((rows, 3 * width), BF16),
            pltpu.VMEM((rows, width), BF16),
            pltpu.VMEM((pieces, 2 * reach), F32),
            pltpu.VMEM((rows, width), BF16),
            pltpu.VMEM((rows, 3 * width), BF16),
            pltpu.VMEM((size, PAIR), F32),
            pltpu.VMEM((size, PAIR), F32),
        ],
        compiler_params=pltpu.CompilerParams(vmem_limit_bytes=LIMIT),
        name="block_layer",
    )(
        counts, hidden, upstream, gain_two, shift_two, project_two, merge_two,
        gain_three, shift_three, expand, bias_in, shrink, bias_out,
    )
    layer_out = from_blocks(results[0])
    flow = from_blocks(results[1])

    first = pl.pallas_call(
        sample_backward_kernel,
        grid=(tasks,),
        in_specs=[
            SMEM, by_task(samples, width), VMEM, VMEM, VMEM, VMEM,
            by_task(samples, 3 * width), by_task(samples, width),
            by_task(log_rows, 2 * PAIR), by_task(samples, width),
        ],
        out_specs=[by_task(samples, width), VMEM, VMEM, VMEM, VMEM],
        out_shape=[
            shape((tasks, samples, width), F32),
            shape((width, 3 * width), F32), shape((width, width), F32),
            shape((1, width), F32), shape((1, width), F32),
        ],
        scratch_shapes=[
            pltpu.VMEM((samples, width), BF16),
            pltpu.VMEM((samples, 3 * width), BF16),
            pltpu.VMEM((samples, PAIR), F32),
            pltpu.VMEM((samples, PAIR), F32),
        ],
        compiler_params=pltpu.CompilerParams(vmem_limit_bytes=LIMIT),
        name="sample_backward",
    )(
        counts, source, gain_one, shift_one, project_one, merge_one, triple, mixed, logs, flow,
    )
    (
        gain_two_grad, shift_two_grad, project_two_grad, merge_two_grad, gain_three_grad,
        shift_three_grad, expand_grad, bias_in_grad, shrink_grad, bias_out_grad,
    ) = results[2:]
    totals = (
        first[3], first[4], first[1], first[2], gain_two_grad, shift_two_grad, project_two_grad,
        merge_two_grad, gain_three_grad, shift_three_grad, expand_grad, bias_in_grad,
        shrink_grad, bias_out_grad,
    )
    totals = [part[0] if part.shape[0] == 1 else part for part in totals]
    totals = tuple(part.astype(BF16) for part in totals)
    totals = lax.psum_scatter(totals, "feat", scatter_dimension=0, tiled=True)
    totals = lax.psum(totals, "task")
    return (
        layer_out.reshape(tokens.shape),
        first[0].reshape(tokens.shape),
    ) + tuple(part.astype(F32) for part in totals)


def solution(mesh):
    wide = P("task", None, "feat", None)
    row, grid = P("feat"), P("feat", None)
    weights = (
        row, row, grid, grid, row, row, grid, grid, row, row, grid, row, grid, row,
    )
    return jax.shard_map(
        body,
        mesh=mesh,
        in_specs=(wide, wide, P("task")) + weights,
        out_specs=(wide, wide) + weights,
        check_vma=False,
    )
```

```python
import functools
import types

import jax
import jax.numpy as jnp
from jax import lax
from jax.experimental import pallas as pl
from jax.experimental.pallas import tpu as pltpu
from jax.sharding import PartitionSpec as P

HEADS = 8
NORM_EPS = 1e-05
MASKED = -1e30
PAIR = 128
GROUP = 16
F32 = jnp.float32
BF16 = jnp.bfloat16


def nt(left, right):
    return lax.dot_general(left, right, (((1,), (1,)), ((), ())), preferred_element_type=F32)


def tn(left, right):
    return lax.dot_general(left, right, (((0,), (0,)), ((), ())), preferred_element_type=F32)


def nn(left, right):
    return lax.dot_general(left, right, (((1,), (0,)), ((), ())), preferred_element_type=F32)


def normalise(values):
    center = values - jnp.mean(values, axis=-1, keepdims=True)
    spread = jnp.mean(center * center, axis=-1, keepdims=True)
    scale = lax.rsqrt(spread + NORM_EPS)
    return center * scale, scale


def normalise_back(incoming, normed, scale, gain):
    weighted = incoming * gain
    first = jnp.mean(weighted, axis=-1, keepdims=True)
    second = jnp.mean(weighted * normed, axis=-1, keepdims=True)
    return scale * (weighted - first - normed * second)


def head_masks(scale):
    lane = lax.broadcasted_iota(jnp.int32, (1, PAIR), 1)
    low = jnp.where(lane < PAIR // 2, scale, 0.0).astype(BF16)
    high = jnp.where(lane < PAIR // 2, 0.0, scale).astype(BF16)
    return low, high


def two_heads(rows, scale):
    low, high = head_masks(scale)
    return jnp.concatenate([rows * low, rows * high], axis=0)


def join_heads(turned, length):
    half = PAIR // 2
    joined = jnp.concatenate([turned[:half, :length], turned[half:, length:]], axis=0)
    return joined.T


def attend(query, key, value_turned, bias, head_scale):
    scores = nt(key, two_heads(query, head_scale)) + bias
    top = jnp.max(scores, axis=0, keepdims=True)
    expo = jnp.exp(scores - top)
    total = jnp.sum(expo, axis=0, keepdims=True)
    chances = (expo * (1.0 / total)).astype(BF16)
    mixed = join_heads(nn(value_turned, chances), query.shape[0])
    return mixed, top + jnp.log(total)


def attend_back(query, key, value, key_turned, grad_out, log_total, bias, head_scale):
    queries = two_heads(query, head_scale)
    scores = nt(key, queries) + bias
    chances = jnp.exp(scores - log_total)
    grads = two_heads(grad_out, 1.0)
    grad_chances = nt(value, grads)
    inner = jnp.sum(chances * grad_chances, axis=0, keepdims=True)
    grad_scores = (chances * (grad_chances - inner)).astype(BF16)
    grad_value = nn(chances.astype(BF16), grads)
    grad_key = nn(grad_scores, queries)
    grad_query = join_heads(nn(key_turned, grad_scores), query.shape[0]) * head_scale
    return grad_query, grad_key, grad_value


def sample_forward_kernel(
    counts_ref, tokens_ref, gain_ref, shift_ref, project_ref, merge_ref,
    triple_ref, mixed_ref, logs_ref, hidden_ref,
):
    count = counts_ref[pl.program_id(0)]
    samples, width = tokens_ref.shape[1:]
    chunk = min(256, samples)
    gain = gain_ref[...].astype(F32)
    shift = shift_ref[...].astype(F32)
    for start in range(0, samples, chunk):
        rows = tokens_ref[0, pl.ds(start, chunk), :].astype(F32)
        normed = (normalise(rows)[0] * gain + shift).astype(BF16)
        triple_ref[0, pl.ds(start, chunk), :] = nn(normed, project_ref[...]).astype(BF16)
    keys = lax.broadcasted_iota(jnp.int32, (samples, 1), 0)
    bias = jnp.where(keys < count, 0.0, MASKED)
    head_scale = (width // HEADS) ** (-0.5)
    pairs = width // PAIR

    def one_pair(pair, carry):
        lanes = pl.multiple_of(pair * PAIR, PAIR)
        key = triple_ref[0, :, pl.ds(lanes + width, PAIR)]
        value_turned = triple_ref[0, :, pl.ds(lanes + 2 * width, PAIR)].T
        for at in range(samples // PAIR):
            query = triple_ref[0, pl.ds(at * PAIR, PAIR), pl.ds(lanes, PAIR)]
            mixed, log_total = attend(query, key, value_turned, bias, head_scale)
            mixed_ref[0, pl.ds(at * PAIR, PAIR), pl.ds(lanes, PAIR)] = mixed.astype(BF16)
            logs_ref[0, pl.ds(pair * (samples // PAIR) + at, 1), :] = log_total
        return carry

    lax.fori_loop(0, pairs, one_pair, 0)
    for start in range(0, samples, chunk):
        rows = tokens_ref[0, pl.ds(start, chunk), :].astype(F32)
        at = lax.broadcasted_iota(jnp.int32, (chunk, 1), 0) + start
        live = jnp.where(at < count, 1.0, 0.0)
        merged = nn(mixed_ref[0, pl.ds(start, chunk), :], merge_ref[...])
        hidden_ref[0, pl.ds(start, chunk), :] = (rows + live * merged).astype(BF16)


def sample_backward_kernel(
    counts_ref, tokens_ref, gain_ref, shift_ref, project_ref, merge_ref,
    triple_ref, mixed_ref, logs_ref, flow_ref,
    input_grad_ref, project_grad_ref, merge_grad_ref, gain_grad_ref, shift_grad_ref,
    grad_mixed, grad_triple, key_sum, value_sum,
):
    task = pl.program_id(0)
    count = counts_ref[task]
    samples, width = tokens_ref.shape[1:]
    chunk = min(256, samples)
    gain = gain_ref[...].astype(F32)
    shift = shift_ref[...].astype(F32)

    @pl.when(task == 0)
    def _():
        project_grad_ref[...] = jnp.zeros_like(project_grad_ref)
        merge_grad_ref[...] = jnp.zeros_like(merge_grad_ref)
        gain_grad_ref[...] = jnp.zeros_like(gain_grad_ref)
        shift_grad_ref[...] = jnp.zeros_like(shift_grad_ref)

    for start in range(0, samples, chunk):
        at = lax.broadcasted_iota(jnp.int32, (chunk, 1), 0) + start
        live = jnp.where(at < count, 1.0, 0.0)
        branch = (flow_ref[0, pl.ds(start, chunk), :].astype(F32) * live).astype(BF16)
        merge_grad_ref[...] += tn(mixed_ref[0, pl.ds(start, chunk), :], branch)
        grad_mixed[pl.ds(start, chunk), :] = nt(branch, merge_ref[...]).astype(BF16)
    keys = lax.broadcasted_iota(jnp.int32, (samples, 1), 0)
    bias = jnp.where(keys < count, 0.0, MASKED)
    head_scale = (width // HEADS) ** (-0.5)
    pairs = width // PAIR

    def one_pair(pair, carry):
        lanes = pl.multiple_of(pair * PAIR, PAIR)
        key = triple_ref[0, :, pl.ds(lanes + width, PAIR)]
        value = triple_ref[0, :, pl.ds(lanes + 2 * width, PAIR)]
        key_turned = key.T
        for at in range(samples // PAIR):
            query = triple_ref[0, pl.ds(at * PAIR, PAIR), pl.ds(lanes, PAIR)]
            grad_out = grad_mixed[pl.ds(at * PAIR, PAIR), pl.ds(lanes, PAIR)]
            log_total = logs_ref[0, pl.ds(pair * (samples // PAIR) + at, 1), :]
            grad_query, grad_key, grad_value = attend_back(
                query, key, value, key_turned, grad_out, log_total, bias, head_scale
            )
            grad_triple[pl.ds(at * PAIR, PAIR), pl.ds(lanes, PAIR)] = grad_query.astype(BF16)
            if at == 0:
                key_sum[...] = grad_key
                value_sum[...] = grad_value
            else:
                key_sum[...] += grad_key
                value_sum[...] += grad_value
        grad_triple[:, pl.ds(lanes + width, PAIR)] = key_sum[...].astype(BF16)
        grad_triple[:, pl.ds(lanes + 2 * width, PAIR)] = value_sum[...].astype(BF16)
        return carry

    lax.fori_loop(0, pairs, one_pair, 0)
    for start in range(0, samples, chunk):
        rows = tokens_ref[0, pl.ds(start, chunk), :].astype(F32)
        normed, scale = normalise(rows)
        part = grad_triple[pl.ds(start, chunk), :]
        project_grad_ref[...] += tn((normed * gain + shift).astype(BF16), part)
        incoming = nt(part, project_ref[...])
        gain_grad_ref[...] += jnp.sum(incoming * normed, axis=0, keepdims=True)
        shift_grad_ref[...] += jnp.sum(incoming, axis=0, keepdims=True)
        back = normalise_back(incoming, normed, scale, gain)
        input_grad_ref[0, pl.ds(start, chunk), :] = (
            flow_ref[0, pl.ds(start, chunk), :].astype(F32) + back
        )


def block_kernel(
    rows_per_task, blocks,
    counts_ref, hidden_ref, upstream_ref,
    gain_two_ref, shift_two_ref, project_ref, merge_ref,
    gain_three_ref, shift_three_ref, expand_ref, bias_in_ref, shrink_ref, bias_out_ref,
    out_ref, flow_ref,
    gain_two_grad, shift_two_grad, project_grad, merge_grad,
    gain_three_grad, shift_three_grad, expand_grad, bias_in_grad, shrink_grad, bias_out_grad,
    triple, mixed, logs, grad_mixed, grad_triple, key_sum, value_sum,
):
    step = pl.program_id(0)
    place = lax.axis_index("feat")
    feats, _, width = hidden_ref.shape
    size = feats * GROUP
    rows = blocks * size
    hidden_units = expand_ref.shape[1]
    sums = (
        gain_two_grad, shift_two_grad, project_grad, merge_grad, gain_three_grad,
        shift_three_grad, expand_grad, bias_in_grad, shrink_grad, bias_out_grad,
    )

    @pl.when(step == 0)
    def _():
        for ref in sums:
            ref[...] = jnp.zeros_like(ref)

    def load(ref):
        pieces = [
            ref[:, pl.ds(block * GROUP, GROUP), :].reshape(size, width) for block in range(blocks)
        ]
        return pieces[0] if blocks == 1 else jnp.concatenate(pieces, axis=0)

    def store(ref, values):
        for block in range(blocks):
            piece = values[block * size : (block + 1) * size]
            ref[:, pl.ds(block * GROUP, GROUP), :] = piece.reshape(feats, GROUP, width)

    row = lax.broadcasted_iota(jnp.int32, (rows, 1), 0)
    row = (step * blocks + row // size) * GROUP + row % GROUP
    sample = place * rows_per_task + row % rows_per_task
    count = jnp.zeros_like(row)
    for task in range(counts_ref.shape[0]):
        count = jnp.where(row // rows_per_task == task, counts_ref[task], count)
    live = jnp.where(sample < count, 1.0, 0.0)

    gain_two = gain_two_ref[...].astype(F32)
    shift_two = shift_two_ref[...].astype(F32)
    gain_three = gain_three_ref[...].astype(F32)
    shift_three = shift_three_ref[...].astype(F32)
    hidden_one = load(hidden_ref).astype(F32)
    unit_two, scale_two = normalise(hidden_one)
    normed_two = (unit_two * gain_two + shift_two).astype(BF16)
    triple[...] = nn(normed_two, project_ref[...]).astype(BF16)

    reach = min(PAIR, size)
    key_at = lax.broadcasted_iota(jnp.int32, (size, 2 * reach), 0) % GROUP
    query_at = lax.broadcasted_iota(jnp.int32, (size, 2 * reach), 1) % GROUP
    bias = jnp.where(key_at == query_at, 0.0, MASKED)
    head_scale = (width // HEADS) ** (-0.5)
    parts = size // reach
    pairs = width // PAIR
    for block in range(blocks):
        start = block * size
        for pair in range(pairs):
            lanes = pair * PAIR
            key = triple[pl.ds(start, size), pl.ds(width + lanes, PAIR)]
            value_turned = triple[pl.ds(start, size), pl.ds(2 * width + lanes, PAIR)].T
            for part in range(parts):
                at = start + part * reach
                query = triple[pl.ds(at, reach), pl.ds(lanes, PAIR)]
                result, log_total = attend(query, key, value_turned, bias, head_scale)
                mixed[pl.ds(at, reach), pl.ds(lanes, PAIR)] = result.astype(BF16)
                logs[pl.ds((block * pairs + pair) * parts + part, 1), :] = log_total

    hidden_two = hidden_one + live * nn(mixed[...], merge_ref[...])
    unit_three, scale_three = normalise(hidden_two)
    normed_three = (unit_three * gain_three + shift_three).astype(BF16)
    upstream = load(upstream_ref).astype(F32)
    grad_dense = (upstream * live).astype(BF16)
    bias_out_grad[...] += jnp.sum(grad_dense.astype(F32), axis=0, keepdims=True)
    lanes = min(512, hidden_units)
    dense = None
    incoming = None
    for start in range(0, hidden_units, lanes):
        cut = pl.ds(start, lanes)
        expanded = nn(normed_three, expand_ref[:, cut]) + bias_in_ref[:, cut].astype(F32)
        square = expanded * expanded
        steep = 0.7978845608028654
        bend = jnp.tanh(expanded * (steep + (steep * 0.044715) * square))
        half_up = 0.5 + 0.5 * bend
        activated = (expanded * half_up).astype(BF16)
        slope = half_up + (0.5 * expanded) * (1.0 - bend * bend) * (
            steep + (3.0 * steep * 0.044715) * square
        )
        grad_expanded = (slope * nt(grad_dense, shrink_ref[cut, :])).astype(BF16)
        bias_in_grad[:, cut] += jnp.sum(grad_expanded.astype(F32), axis=0, keepdims=True)
        shrink_grad[cut, :] += tn(activated, grad_dense)
        expand_grad[:, cut] += tn(normed_three, grad_expanded)
        up = nn(activated, shrink_ref[cut, :])
        down = nt(grad_expanded, expand_ref[:, cut])
        dense = up if dense is None else dense + up
        incoming = down if incoming is None else incoming + down
    result = hidden_two + live * (dense + bias_out_ref[...].astype(F32))
    store(out_ref, result.astype(BF16))

    gain_three_grad[...] += jnp.sum(incoming * unit_three, axis=0, keepdims=True)
    shift_three_grad[...] += jnp.sum(incoming, axis=0, keepdims=True)
    flow_two = upstream + normalise_back(incoming, unit_three, scale_three, gain_three)
    branch = (flow_two * live).astype(BF16)
    merge_grad[...] += tn(mixed[...], branch)
    grad_mixed[...] = nt(branch, merge_ref[...]).astype(BF16)
    for block in range(blocks):
        start = block * size
        for pair in range(pairs):
            lanes = pair * PAIR
            key = triple[pl.ds(start, size), pl.ds(width + lanes, PAIR)]
            value = triple[pl.ds(start, size), pl.ds(2 * width + lanes, PAIR)]
            key_turned = key.T
            for part in range(parts):
                at = start + part * reach
                query = triple[pl.ds(at, reach), pl.ds(lanes, PAIR)]
                grad_out = grad_mixed[pl.ds(at, reach), pl.ds(lanes, PAIR)]
                log_total = logs[pl.ds((block * pairs + pair) * parts + part, 1), :]
                grad_query, grad_key, grad_value = attend_back(
                    query, key, value, key_turned, grad_out, log_total, bias, head_scale
                )
                grad_triple[pl.ds(at, reach), pl.ds(lanes, PAIR)] = grad_query.astype(BF16)
                if part > 0:
                    grad_key += key_sum[...]
                    grad_value += value_sum[...]
                if part == parts - 1:
                    where = pl.ds(start, size)
                    grad_triple[where, pl.ds(width + lanes, PAIR)] = grad_key.astype(BF16)
                    grad_triple[where, pl.ds(2 * width + lanes, PAIR)] = grad_value.astype(BF16)
                else:
                    key_sum[...] = grad_key
                    value_sum[...] = grad_value
    project_grad[...] += tn(normed_two, grad_triple[...])
    incoming = nt(grad_triple[...], project_ref[...])
    gain_two_grad[...] += jnp.sum(incoming * unit_two, axis=0, keepdims=True)
    shift_two_grad[...] += jnp.sum(incoming, axis=0, keepdims=True)
    flow_one = flow_two + normalise_back(incoming, unit_two, scale_two, gain_two)
    store(flow_ref, flow_one.astype(BF16))


VMEM = pl.BlockSpec(memory_space=pltpu.VMEM)
SMEM = pl.BlockSpec(memory_space=pltpu.SMEM)
LIMIT = 56 * 1024 * 1024


def shape(dims, kind):
    return jax.ShapeDtypeStruct(dims, kind)


def by_task(*dims):
    return pl.BlockSpec((1,) + dims, lambda task: (task,) + (0,) * len(dims))


def body(tokens, cotangent, counts, *shards):
    groups = lax.axis_size("feat")
    tasks, samples, local, width = tokens.shape
    rows_per_task = samples // groups
    gathered = [lax.all_gather(part, "feat", axis=0, tiled=True) for part in shards]
    gathered = [part[None, :] if part.ndim == 1 else part for part in gathered]
    (
        gain_one, shift_one, project_one, merge_one, gain_two, shift_two, project_two, merge_two,
        gain_three, shift_three, expand, bias_in, shrink, bias_out,
    ) = gathered
    hidden_units = expand.shape[1]
    source = tokens.reshape(tasks, samples, width)

    def to_blocks(rows):
        rows = rows.reshape(tasks, groups, rows_per_task, width)
        rows = jnp.transpose(rows, (1, 0, 2, 3))
        rows = lax.all_to_all(rows, "feat", split_axis=0, concat_axis=0, tiled=True)
        return rows.reshape(groups, tasks * rows_per_task, width)

    def from_blocks(rows):
        rows = rows.reshape(groups, tasks, rows_per_task, width)
        rows = lax.all_to_all(rows, "feat", split_axis=0, concat_axis=0, tiled=True)
        rows = jnp.transpose(rows, (1, 0, 2, 3))
        return rows.reshape(tasks, samples, width)

    upstream = to_blocks(cotangent.reshape(tasks, samples, width))
    log_rows = samples * width // PAIR // PAIR
    triple, mixed, logs, hidden = pl.pallas_call(
        sample_forward_kernel,
        grid=(tasks,),
        in_specs=[SMEM, by_task(samples, width), VMEM, VMEM, VMEM, VMEM],
        out_specs=[
            by_task(samples, 3 * width), by_task(samples, width),
            by_task(log_rows, 2 * PAIR), by_task(samples, width),
        ],
        out_shape=[
            shape((tasks, samples, 3 * width), BF16),
            shape((tasks, samples, width), BF16),
            shape((tasks, log_rows, 2 * PAIR), F32),
            shape((tasks, samples, width), BF16),
        ],
        compiler_params=pltpu.CompilerParams(vmem_limit_bytes=LIMIT),
        name="sample_forward",
    )(counts, source, gain_one, shift_one, project_one, merge_one)

    hidden = to_blocks(hidden)
    all_rows = tasks * rows_per_task
    size = groups * GROUP
    blocks = max(1, min(all_rows // GROUP, 256 // size))
    steps = all_rows // (GROUP * blocks)
    rows = blocks * size
    slab = pl.BlockSpec((groups, GROUP * blocks, width), lambda step: (0, step, 0))
    reach = min(PAIR, size)
    pieces = blocks * (width // PAIR) * (size // reach)
    grads = [
        shape((1, width), F32), shape((1, width), F32),
        shape((width, 3 * width), F32), shape((width, width), F32),
        shape((1, width), F32), shape((1, width), F32),
        shape((width, hidden_units), F32), shape((1, hidden_units), F32),
        shape((hidden_units, width), F32), shape((1, width), F32),
    ]
    results = pl.pallas_call(
        functools.partial(block_kernel, rows_per_task, blocks),
        grid=(steps,),
        in_specs=[SMEM, slab, slab] + [VMEM] * 10,
        out_specs=[slab, slab] + [VMEM] * 10,
        out_shape=[shape((groups, all_rows, width), BF16)] * 2 + grads,
        scratch_shapes=[
            pltpu.VMEM((rows, 3 * width), BF16),
            pltpu.VMEM((rows, width), BF16),
            pltpu.VMEM((pieces, 2 * reach), F32),
            pltpu.VMEM((rows, width), BF16),
            pltpu.VMEM((rows, 3 * width), BF16),
            pltpu.VMEM((size, PAIR), F32),
            pltpu.VMEM((size, PAIR), F32),
        ],
        compiler_params=pltpu.CompilerParams(vmem_limit_bytes=LIMIT),
        name="block_layer",
    )(
        counts, hidden, upstream, gain_two, shift_two, project_two, merge_two,
        gain_three, shift_three, expand, bias_in, shrink, bias_out,
    )
    layer_out = from_blocks(results[0])
    flow = from_blocks(results[1])

    first = pl.pallas_call(
        sample_backward_kernel,
        grid=(tasks,),
        in_specs=[
            SMEM, by_task(samples, width), VMEM, VMEM, VMEM, VMEM,
            by_task(samples, 3 * width), by_task(samples, width),
            by_task(log_rows, 2 * PAIR), by_task(samples, width),
        ],
        out_specs=[by_task(samples, width), VMEM, VMEM, VMEM, VMEM],
        out_shape=[
            shape((tasks, samples, width), F32),
            shape((width, 3 * width), F32), shape((width, width), F32),
            shape((1, width), F32), shape((1, width), F32),
        ],
        scratch_shapes=[
            pltpu.VMEM((samples, width), BF16),
            pltpu.VMEM((samples, 3 * width), BF16),
            pltpu.VMEM((samples, PAIR), F32),
            pltpu.VMEM((samples, PAIR), F32),
        ],
        compiler_params=pltpu.CompilerParams(vmem_limit_bytes=LIMIT),
        name="sample_backward",
    )(
        counts, source, gain_one, shift_one, project_one, merge_one, triple, mixed, logs, flow,
    )
    (
        gain_two_grad, shift_two_grad, project_two_grad, merge_two_grad, gain_three_grad,
        shift_three_grad, expand_grad, bias_in_grad, shrink_grad, bias_out_grad,
    ) = results[2:]
    totals = (
        first[3], first[4], first[1], first[2], gain_two_grad, shift_two_grad, project_two_grad,
        merge_two_grad, gain_three_grad, shift_three_grad, expand_grad, bias_in_grad,
        shrink_grad, bias_out_grad,
    )
    totals = [part[0] if part.shape[0] == 1 else part for part in totals]
    totals = tuple(part.astype(BF16) for part in totals)
    totals = lax.psum_scatter(totals, "feat", scatter_dimension=0, tiled=True)
    totals = lax.psum(totals, "task")
    return (
        layer_out.reshape(tokens.shape),
        first[0].reshape(tokens.shape),
    ) + tuple(part.astype(F32) for part in totals)


FUSED_LIMIT = 62 * 1024 * 1024

MESH = pl.DeviceIdType.MESH
DEPTH, WIDE_Y, CORES, HALVES = 4, 2, 2, 2
SPLIT = CORES * HALVES
VECTORS = 16
FINISH_LIMIT = 56 * 1024 * 1024
BUFFERS = ("halves", "quarters", "lines", "outer", "crossed", "paired", "final", "twin")


def remote(source, target, sent, arrived, device):
    return pltpu.make_async_remote_copy(
        src_ref=source, dst_ref=target, send_sem=sent, recv_sem=arrived,
        device_id=device, device_id_type=MESH,
    )


class Place:
    def __init__(self):
        self.feat = lax.axis_index("feat")
        self.task = lax.axis_index("task")
        self.z = lax.div(self.feat, WIDE_Y)
        self.y = lax.rem(self.feat, WIDE_Y)
        self.x = lax.div(self.task, CORES)
        self.c = lax.rem(self.task, CORES)
        self.mine = HALVES * self.c + self.x
        self.theirs = HALVES * self.c + 1 - self.x
        self.below = HALVES * self.c
        self.other = HALVES * (1 - self.c)
        self.along_y = (self.task, WIDE_Y * self.z + 1 - self.y)
        self.along_x = (CORES * (1 - self.x) + self.c, self.feat)
        self.sibling = (CORES * self.x + 1 - self.c, self.feat)
        self.across = DEPTH - 1 - self.z
        self.near_low = 2 * lax.div(self.z, 2)
        self.far_low = 2 - self.near_low
        self.pair = 2 * self.near_low + 1 - self.z
        self.inner = jnp.logical_or(self.z == 1, self.z == 2)

    def along_z(self, shift):
        return lax.rem(self.z + shift, DEPTH)

    def at_z(self, z):
        return (self.task, WIDE_Y * z + self.y)

    def peer(self, shift, groups):
        return lax.rem(self.feat + shift, groups)


class Moves:
    def __init__(self, place, index, wide, sent, arrived, stages):
        self.place, self.wide = place, wide
        self.rows = pl.ds(place.below, HALVES) if wide else pl.ds(place.mine, 1)
        self.sent = [sent.at[index, stage] for stage in range(stages)]
        self.arrived = [arrived.at[index, stage] for stage in range(stages)]

    def move(self, stage, source, target, device):
        return remote(source, target, self.sent[stage], self.arrived[stage], device)


class Gather(Moves):
    def __init__(self, place, index, shard, weight, sent, arrived, local, wide=False, direct=False):
        super().__init__(place, index, wide, sent, arrived, 6)
        self.shard, self.weight, self.local, self.direct = shard, weight, local.at[index], direct

    def _own(self):
        p = self.place
        return pltpu.make_async_copy(
            self.shard.at[self.rows], self.weight.at[p.z, p.y, self.rows], self.local
        )

    def _pair(self, z_count):
        p = self.place
        part = self.weight.at[pl.ds(0, z_count), p.y, self.rows]
        return self.move(0, part, part, p.at_z(p.pair))

    def _far(self, stage, low, device):
        part = self.weight.at[pl.ds(low, 2), self.place.y, self.rows]
        return self.move(stage, part, part, device)

    def _along_y(self):
        p = self.place
        part = self.weight.at[:, p.y, self.rows]
        return self.move(3, part, part, p.along_y)

    def _along_x(self):
        p = self.place
        part = self.weight.at[:, :, self.rows]
        return self.move(4, part, part, p.along_x)

    def _across(self):
        p = self.place
        part = self.weight.at[:, :, pl.ds(p.below, HALVES)]
        return self.move(5, part, part, p.sibling)

    def start(self):
        p = self.place
        self._own().start()
        targets = [p.along_z(shift) for shift in range(1, DEPTH)] if self.direct else [p.pair]
        for z in targets:
            self.move(
                0, self.shard.at[self.rows], self.weight.at[p.z, p.y, self.rows], p.at_z(z)
            ).start()

    def middle(self):
        if self.direct:
            return
        p = self.place

        @pl.when(p.inner)
        def _():
            self._own().wait()
            self._pair(1).wait_recv()
            self._far(1, p.near_low, p.at_z(p.across)).start()

    def outward(self):
        if self.direct:
            return
        p = self.place

        @pl.when(p.inner)
        def _():
            self._far(1, p.far_low, p.at_z(p.across)).wait_recv()
            self._far(2, p.far_low, p.at_z(p.pair)).start()

    def along_y(self):
        p = self.place
        if self.direct:
            self._own().wait()
            self._pair(DEPTH - 1).wait_recv()
        else:
            @pl.when(jnp.logical_not(p.inner))
            def _():
                self._own().wait()
                self._pair(1).wait_recv()
                self._far(2, p.far_low, p.at_z(p.pair)).wait_recv()

        self._along_y().start()

    def along_x(self):
        if not self.wide:
            self._along_y().wait_recv()
            self._along_x().start()

    def core(self):
        if self.wide:
            self._along_y().wait_recv()
        else:
            self._along_x().wait_recv()
        self._across().start()

    def done(self):
        self._across().wait_recv()

    def finish(self):
        p = self.place
        if self.direct:
            self._pair(DEPTH - 1).wait_send()
        else:
            self._pair(1).wait_send()

            @pl.when(p.inner)
            def _():
                self._far(1, p.near_low, p.at_z(p.across)).wait_send()
                self._far(2, p.far_low, p.at_z(p.pair)).wait_send()

        self._along_y().wait_send()
        if not self.wide:
            self._along_x().wait_send()
        self._across().wait_send()


class Reduce(Moves):
    def __init__(
        self, place, index, total, staged, memory, sent, arrived, wide=False, direct=False
    ):
        super().__init__(place, index, wide, sent, arrived, 8)
        self.total, self.staged, self.direct = total, staged, direct
        (
            self.halves, self.quarters, self.lines, self.outer, self.crossed, self.paired,
            self.final, self.twin,
        ) = memory

    def _core(self):
        p = self.place
        return self.move(
            0, self.staged.at[:, :, pl.ds(p.other, HALVES)], self.halves, p.sibling
        )

    def _x(self):
        p = self.place
        return self.move(1, self.staged.at[:, :, pl.ds(p.theirs, 1)], self.quarters, p.along_x)

    def _y(self):
        p = self.place
        return self.move(2, self.staged.at[:, 1 - p.y, self.rows], self.lines, p.along_y)

    def _inward(self):
        p = self.place
        if self.direct:
            return self.move(3, self.outer, self.outer, p.at_z(p.pair))
        return self.move(
            3, self.staged.at[pl.ds(p.far_low, 2), p.y, self.rows], self.outer, p.at_z(p.pair)
        )

    def _over(self):
        p = self.place
        return self.move(
            4, self.staged.at[pl.ds(p.far_low, 2), p.y, self.rows], self.crossed, p.at_z(p.across)
        )

    def _pair(self):
        p = self.place
        return self.move(5, self.staged.at[p.pair, p.y, self.rows], self.paired, p.at_z(p.pair))

    def _twin(self):
        p = self.place
        part = self.final.at[self.rows]
        return self.move(6, part, self.twin if self.wide else part, p.along_x)

    def _across(self):
        p = self.place
        part = self.final.at[pl.ds(p.below, HALVES)]
        return self.move(7, part, part, p.sibling)

    def core(self):
        p = self.place

        def one(z, carry):
            cut = pl.ds(p.other, HALVES)
            self.staged[z, :, cut] = self.total[z, :, cut].astype(BF16)
            return carry

        lax.fori_loop(0, DEPTH, one, 0)
        self._core().start()

    def x(self):
        p = self.place
        if self.wide:
            return
        self._core().wait_recv()

        def one(z, carry):
            summed = self.total[z, :, p.theirs] + self.halves[z, :, 1 - p.x].astype(F32)
            self.staged[z, :, p.theirs] = summed.astype(BF16)
            return carry

        lax.fori_loop(0, DEPTH, one, 0)
        self._x().start()

    def y(self):
        p = self.place
        if self.wide:
            self._core().wait_recv()
        else:
            self._x().wait_recv()

        def one(z, carry):
            if self.wide:
                summed = self.total[z, :, self.rows] + self.halves[z].astype(F32)
            else:
                summed = self.total[z, :, self.rows] + self.halves[z, :, pl.ds(p.x, 1)].astype(F32)
                summed = summed + self.quarters[z].astype(F32)
            self.staged[z, :, self.rows] = summed.astype(BF16)
            return carry

        lax.fori_loop(0, DEPTH, one, 0)
        self._y().start()

    def inward(self):
        p = self.place
        self._y().wait_recv()

        def one(z, carry):
            summed = self.staged[z, p.y, self.rows].astype(F32) + self.lines[z].astype(F32)
            self.staged[z, p.y, self.rows] = summed.astype(BF16)
            return carry

        lax.fori_loop(0, DEPTH, one, 0)
        if self.direct:
            for shift in range(1, DEPTH):
                z = p.along_z(shift)
                self.move(
                    3, self.staged.at[z, p.y, self.rows], self.outer.at[shift - 1], p.at_z(z)
                ).start()
            return

        @pl.when(jnp.logical_not(p.inner))
        def _():
            self._inward().start()

    def over(self):
        p = self.place

        @pl.when(p.inner)
        def _():
            self._inward().wait_recv()
            for at in range(2):
                z = p.far_low + at
                summed = self.staged[z, p.y, self.rows].astype(F32) + self.outer[at].astype(F32)
                self.staged[z, p.y, self.rows] = summed.astype(BF16)
            self._over().start()

    def pair(self):
        p = self.place

        @pl.when(p.inner)
        def _():
            self._over().wait_recv()
            for at in range(2):
                z = p.near_low + at
                summed = self.staged[z, p.y, self.rows].astype(F32) + self.crossed[at].astype(F32)
                self.staged[z, p.y, self.rows] = summed.astype(BF16)

        self._pair().start()

    def twins(self):
        p = self.place
        summed = self.staged[p.z, p.y, self.rows].astype(F32)
        if self.direct:
            self._inward().wait_recv()
            for shift in range(DEPTH - 1):
                summed = summed + self.outer[shift].astype(F32)
        else:
            self._pair().wait_recv()
            summed = summed + self.paired[...].astype(F32)
        self.final[self.rows] = summed.astype(BF16)
        self._twin().start()

    def share(self):
        self._twin().wait_recv()
        if self.wide:
            self._twin().wait_send()
            summed = self.final[self.rows].astype(F32) + self.twin[...].astype(F32)
            self.final[self.rows] = summed.astype(BF16)
        self._across().start()

    def done(self):
        self._across().wait_recv()

    def finish(self):
        p = self.place
        self._core().wait_send()
        if not self.wide:
            self._x().wait_send()
            self._twin().wait_send()
        self._y().wait_send()
        self._across().wait_send()
        if self.direct:
            self._inward().wait_send()
            return

        @pl.when(p.inner)
        def _():
            self._over().wait_send()

        @pl.when(jnp.logical_not(p.inner))
        def _():
            self._inward().wait_send()

        self._pair().wait_send()


SCHEDULE = {
    "start": (
        ("query", "start"),
        ("key", "start"),
        ("value", "start"),
        ("merge_one", "start"),
        ("merge_two", "start"),
        ("project_two", "start"),
        ("expand_low", "start"),
        ("expand_high", "start"),
        ("shrink_low", "start"),
        ("shrink_high", "start"),
    ),
    "norm1": (
        ("query", "along_y"),
    ),
    "until_query": (
        ("key", "along_y"),
        ("value", "along_y"),
        ("merge_two", "middle"),
        ("query", "along_x"),
        ("project_two", "middle"),
        ("merge_one", "along_y"),
        ("key", "along_x"),
        ("expand_low", "middle"),
        ("expand_high", "middle"),
        ("merge_two", "outward"),
        ("shrink_low", "middle"),
        ("value", "core"),
        ("query", "core"),
        ("project_two", "outward"),
        ("shrink_high", "middle"),
        ("merge_two", "along_y"),
        ("merge_one", "along_x"),
        ("expand_low", "outward"),
    ),
    "until_key": (
        ("key", "core"),
        ("expand_high", "outward"),
        ("project_two", "along_y"),
    ),
    "projk": (
        ("merge_two", "along_x"),
    ),
    "pair00": (
        ("merge_one", "core"),
        ("expand_low", "along_y"),
        ("shrink_low", "outward"),
        ("expand_high", "along_y"),
    ),
    "pair01": (
        ("shrink_high", "outward"),
    ),
    "pair02": (
        ("merge_two", "core"),
        ("project_two", "along_x"),
    ),
    "pair03": (
        ("shrink_low", "along_y"),
    ),
    "merge0": (
        ("expand_low", "along_x"),
    ),
    "proj1": (
        ("shrink_high", "along_y"),
    ),
    "pair10": (
        ("expand_high", "along_x"),
    ),
    "pair13": (
        ("project_two", "core"),
    ),
    "dense": (
        ("expand_low", "core"),
        ("expand_high", "core"),
        ("shrink_low", "core"),
    ),
    "until_shrink": (
        ("shrink_high", "core"),
    ),
    "dense_grads": (
        ("d_expand_low", "core"),
        ("d_shrink_low", "core"),
        ("d_shrink_high", "core"),
        ("d_expand_high", "core"),
    ),
    "feature_grads": (
        ("d_expand_low", "x"),
        ("d_shrink_low", "y"),
        ("d_shrink_high", "y"),
    ),
    "layer_end": (
        ("d_project_two", "core"),
        ("d_merge_two", "core"),
    ),
    "layer_after": (
        ("d_expand_high", "x"),
    ),
    "back00": (
        ("d_expand_low", "y"),
        ("d_shrink_low", "inward"),
        ("d_project_two", "x"),
        ("d_merge_two", "x"),
    ),
    "back02": (
        ("d_shrink_high", "inward"),
        ("d_expand_high", "y"),
    ),
    "back03": (
        ("d_shrink_low", "over"),
    ),
    "merge_grads": (
        ("d_merge_one", "core"),
    ),
    "back10": (
        ("d_expand_low", "inward"),
        ("d_project_two", "y"),
        ("d_shrink_high", "over"),
        ("d_merge_one", "y"),
    ),
    "back11": (
        ("d_shrink_low", "pair"),
        ("d_expand_high", "inward"),
        ("d_merge_two", "y"),
    ),
    "low_grads": (
        ("d_project_low", "core"),
    ),
    "low": (
        ("d_expand_low", "over"),
    ),
    "back12": (
        ("d_shrink_low", "twins"),
        ("d_project_two", "inward"),
        ("d_shrink_high", "pair"),
        ("d_project_low", "y"),
    ),
    "back13": (
        ("d_expand_low", "pair"),
        ("d_expand_high", "over"),
        ("d_merge_two", "inward"),
        ("d_merge_one", "inward"),
    ),
    "high_grads": (
        ("d_project_high", "core"),
    ),
    "high": (
        ("d_shrink_low", "share"),
        ("d_project_two", "over"),
    ),
    "first0": (
        ("d_shrink_high", "twins"),
    ),
    "first1": (
        ("d_project_high", "y"),
        ("d_expand_low", "twins"),
        ("d_expand_high", "pair"),
        ("d_merge_two", "over"),
        ("d_project_low", "inward"),
    ),
    "first2": (
        ("d_merge_one", "twins"),
    ),
    "first3": (
        ("d_expand_low", "share"),
        ("d_shrink_high", "share"),
        ("d_expand_high", "twins"),
    ),
    "end": (
        ("d_project_two", "pair"),
        ("d_merge_two", "pair"),
        ("d_merge_one", "share"),
        ("d_project_high", "inward"),
        ("d_expand_high", "share"),
        ("d_project_two", "twins"),
        ("d_merge_two", "twins"),
        ("d_project_low", "twins"),
        ("d_project_two", "share"),
        ("d_merge_two", "share"),
        ("d_project_low", "share"),
        ("d_project_high", "twins"),
        ("d_project_high", "share"),
    ),
}


def flat(ref):
    return ref[...].reshape(-1, ref.shape[-1])


def fused_kernel(names, *refs):
    r = types.SimpleNamespace(**dict(zip(names, refs)))
    p = Place()
    tasks, samples, width = r.tokens.shape
    groups = r.hidden_blocks.shape[0]
    members = r.task_slots.shape[0]
    block_rows = samples // groups
    hidden_units = r.w_expand.shape[-1]
    chunk = 256
    head_scale = (width // HEADS) ** (-0.5)
    pairs = width // PAIR
    parts = samples // PAIR

    entry = pltpu.get_barrier_semaphore()
    for shift in range(1, groups):
        pl.semaphore_signal(
            entry, inc=1, device_id=(p.task, p.peer(shift, groups)), device_id_type=MESH
        )
    for shift in range(1, members):
        pl.semaphore_signal(
            entry, inc=1, device_id=(lax.rem(p.task + shift, members), p.feat),
            device_id_type=MESH,
        )
    pl.semaphore_wait(entry, groups + members - 2)

    third = width
    gathers = []

    def gather(name, rows=None, columns=None, wide=False, direct=False):
        shard, weight = getattr(r, "s_" + name), getattr(r, "w_" + name)
        if rows is not None:
            shard, weight = shard.at[:, pl.ds(*rows), :], weight.at[:, :, :, pl.ds(*rows), :]
        if columns is not None:
            shard = shard.at[:, :, pl.ds(*columns)]
            weight = weight.at[:, :, :, :, pl.ds(*columns)]
        item = Gather(
            p, len(gathers), shard, weight, r.gather_sent, r.gather_arrived, r.gather_local,
            wide, direct,
        )
        gathers.append(item)
        return item

    deep = r.w_shrink.shape[3] // 2
    half_units = hidden_units // 2
    items = {
        "query": gather("project_one", columns=(0, third), direct=True),
        "key": gather("project_one", columns=(third, third), direct=True),
        "value": gather("project_one", columns=(2 * third, third), wide=True, direct=True),
        "merge_one": gather("merge_one", direct=True),
        "project_two": gather("project_two"),
        "merge_two": gather("merge_two"),
        "expand_low": gather("expand", columns=(0, half_units)),
        "expand_high": gather("expand", columns=(half_units, half_units)),
        "shrink_low": gather("shrink", rows=(0, deep), wide=True),
        "shrink_high": gather("shrink", rows=(deep, deep), wide=True),
    }
    dense_items = ("expand_low", "shrink_low", "shrink_high", "expand_high")

    def run(point):
        for name, stage in SCHEDULE.get(point, ()):
            getattr(items[name], stage)()

    def vectors_in():
        most = r.vector_slots.at[pl.ds(0, groups - 1)]
        return remote(most, most, r.vector_sent.at[0], r.vector_arrived.at[0], p.along_y)

    own_vectors = pltpu.make_async_copy(
        r.vectors, r.vector_slots.at[p.feat], r.vector_local.at[0]
    )
    own_vectors.start()
    for shift in range(1, groups):
        remote(
            r.vectors, r.vector_slots.at[p.feat], r.vector_sent.at[0], r.vector_arrived.at[0],
            (p.task, p.peer(shift, groups)),
        ).start()
    run("start")

    def spread(source, target, task, sent, arrived, local):
        def own():
            return pltpu.make_async_copy(
                source.at[task, pl.ds(p.feat * block_rows, block_rows)],
                target.at[p.feat, task], local.at[task],
            )

        def all_of():
            most = target.at[pl.ds(0, groups - 1), task]
            return remote(most, most, sent.at[task], arrived.at[task], p.along_y)

        def start():
            own().start()
            for shift in range(1, groups):
                peer = p.peer(shift, groups)
                remote(
                    source.at[task, pl.ds(peer * block_rows, block_rows)],
                    target.at[p.feat, task], sent.at[task], arrived.at[task], (p.task, peer),
                ).start()

        def wait():
            own().wait()
            all_of().wait_recv()

        def finish():
            all_of().wait_send()

        return types.SimpleNamespace(start=start, wait=wait, finish=finish)

    upstream = [
        spread(
            r.upstream, r.upstream_blocks, task, r.upstream_sent, r.upstream_arrived,
            r.upstream_local,
        )
        for task in range(tasks)
    ]
    hidden = [
        spread(
            r.grad_mixed, r.hidden_blocks, task, r.hidden_sent, r.hidden_arrived, r.hidden_local
        )
        for task in range(tasks)
    ]

    for ref in (r.t_project_two, r.t_merge_two, r.t_expand, r.t_shrink, r.vector_sums):
        ref[...] = jnp.zeros_like(ref)
    run("zero")
    own_vectors.wait()
    vectors_in().wait_recv()
    lane = lax.broadcasted_iota(jnp.int32, (1, PAIR), 1)
    per_slot = r.vector_slots.shape[1:]
    turned = [pltpu.roll(r.vector_slots[index], PAIR // 2, 1) for index in range(groups)]
    whole = [r.vector_slots[index] for index in range(groups)]
    bias_tiles = hidden_units // groups // PAIR
    for row in range(7):
        tile = bias_tiles + row // 2
        for at in range(groups // 2):
            first = (turned if row % 2 else whole)[2 * at][tile : tile + 1]
            second = (whole if row % 2 else turned)[2 * at + 1][tile : tile + 1]
            r.params[pl.ds(row, 1), pl.ds(at * PAIR, PAIR)] = jnp.where(
                lane < PAIR // 2, first, second
            )
    for at in range(groups * bias_tiles):
        row, tile = divmod(at, width // PAIR)
        r.params[pl.ds(7 + row, 1), pl.ds(tile * PAIR, PAIR)] = whole[at // bias_tiles][
            at % bias_tiles : at % bias_tiles + 1
        ]
    run("params")

    def param(row):
        return r.params[pl.ds(row, 1), :]

    def add_vector(row, value):
        r.vector_sums[pl.ds(row, 1), :] += jnp.sum(value, axis=0, keepdims=True)

    def norm_one(task):
        for start in range(0, samples, chunk):
            rows = r.tokens[task, pl.ds(start, chunk), :].astype(F32)
            normed = normalise(rows)[0] * param(0) + param(1)
            r.normed_one[task, pl.ds(start, chunk), :] = normed.astype(BF16)

    for task in range(tasks):
        norm_one(task)
        run("norm%d" % task)

    def key_bias(task):
        keys = lax.broadcasted_iota(jnp.int32, (samples, 1), 0)
        return jnp.where(keys < r.counts[task], 0.0, MASKED)

    def live_rows(task, start):
        at = lax.broadcasted_iota(jnp.int32, (chunk, 1), 0) + start
        return jnp.where(at < r.counts[task], 1.0, 0.0)

    def attend_pairs(task, low, high):
        bias = key_bias(task)

        def one_pair(pair, carry):
            lanes = pl.multiple_of(pair * PAIR, PAIR)
            key = r.triple[task, :, pl.ds(lanes + width, PAIR)]
            value_turned = r.triple[task, :, pl.ds(lanes + 2 * width, PAIR)].T
            for at in range(parts):
                query = r.triple[task, pl.ds(at * PAIR, PAIR), pl.ds(lanes, PAIR)]
                mixed, log_total = attend(query, key, value_turned, bias, head_scale)
                r.mixed_one[task, pl.ds(at * PAIR, PAIR), pl.ds(lanes, PAIR)] = mixed.astype(BF16)
                r.logs_one[pl.ds((task * pairs + pair) * parts + at, 1), :] = log_total
            return carry

        lax.fori_loop(low, high, one_pair, 0)

    def project(task, part):
        weight = r.w_project_one[:, :, :, :, pl.ds(part * width, width)].reshape(width, width)
        for start in range(0, samples, chunk):
            normed = r.normed_one[task, pl.ds(start, chunk), :]
            r.triple[task, pl.ds(start, chunk), pl.ds(part * width, width)] = nn(
                normed, weight
            ).astype(BF16)

    for name, part in (("query", 0), ("key", 1), ("value", 2)):
        run("until_" + name)
        items[name].done()
        project(0, part)
        run(("projq", "projk", "projv")[part])
    for task in range(tasks):
        if task > 0:
            for part in range(3):
                project(task, part)
            run("proj%d" % task)
        for pair in range(pairs):
            attend_pairs(task, pair, pair + 1)
            run("pair%d%d" % (task, pair))
            if task == 0 and pair == 1:
                upstream[0].start()
        if task == 0:
            items["merge_one"].done()
        for start in range(0, samples, chunk):
            rows = r.tokens[task, pl.ds(start, chunk), :].astype(F32)
            merged = nn(r.mixed_one[task, pl.ds(start, chunk), :], flat(r.w_merge_one))
            summed = rows + live_rows(task, start) * merged
            r.grad_mixed[task, pl.ds(start, chunk), :] = summed.astype(BF16)
        hidden[task].start()
        if task > 0:
            upstream[task].start()
        run("merge%d" % task)

    size = groups * GROUP
    blocks = chunk // size
    piece = blocks * GROUP
    per_task = block_rows // piece

    def own_piece(source, target, task, start, semaphore):
        return pltpu.make_async_copy(
            source.at[p.feat, task, pl.ds(start, piece)],
            target.at[task, pl.ds(p.feat * block_rows + start, piece)], semaphore,
        )

    def send_back(source, target, task, start, sent, arrived, local):
        own_piece(source, target, task, start, local).start()
        for shift in range(1, groups):
            peer = p.peer(shift, groups)
            remote(
                source.at[peer, task, pl.ds(start, piece)],
                target.at[task, pl.ds(p.feat * block_rows + start, piece)],
                sent, arrived, (p.task, peer),
            ).start()

    reductions = []

    def reduction(total, staged, wide=False, direct=False):
        index = len(reductions)
        item = Reduce(
            p, index, total, staged,
            [getattr(r, "m%d_%s" % (index, kind), None) for kind in BUFFERS],
            r.reduce_sent, r.reduce_arrived, wide, direct,
        )
        reductions.append(item)
        return item

    def part_of(ref, rows=None, columns=None):
        if rows is not None:
            return ref.at[:, :, :, pl.ds(*rows), :]
        return ref.at[:, :, :, :, pl.ds(*columns)]

    def half_of(name, at, wide):
        total, staged = getattr(r, "t_" + name), getattr(r, "w_" + name)
        if name == "shrink":
            cut = (at * deep, deep)
            return reduction(part_of(total, cut), part_of(staged, cut), wide)
        cut = (at * half_units, half_units)
        return reduction(part_of(total, None, cut), part_of(staged, None, cut), wide)

    items["d_shrink_low"] = half_of("shrink", 0, True)
    items["d_shrink_high"] = half_of("shrink", 1, True)
    items["d_expand_low"] = half_of("expand", 0, False)
    items["d_expand_high"] = half_of("expand", 1, False)
    items["d_project_two"] = reduction(r.t_project_two, r.w_project_two)
    items["d_merge_two"] = reduction(r.t_merge_two, r.w_merge_two)
    items["d_merge_one"] = reduction(r.t_merge_one, r.w_merge_one, True, True)
    items["d_project_low"] = reduction(r.t_project_low, r.b_project_low, True, True)
    items["d_project_high"] = reduction(r.t_project_high, r.b_project_high, True, True)

    def layer_chunk(step, carry):
        task = lax.div(step, per_task)
        begin = pl.multiple_of(lax.rem(step, per_task) * piece, piece)

        first = step == 0
        final = step == tasks * per_task - 1

        @pl.when(first)
        def _():
            hidden[0].wait()
            items["project_two"].done()

        for later in range(1, tasks):
            @pl.when(step == later * per_task)
            def _():
                upstream[later].wait()
                hidden[later].wait()

        def load(ref):
            pieces = [
                ref[:, task, pl.ds(begin + block * GROUP, GROUP), :].reshape(size, width)
                for block in range(blocks)
            ]
            return pieces[0] if blocks == 1 else jnp.concatenate(pieces, axis=0)

        def store(ref, values):
            for block in range(blocks):
                part = values[block * size : (block + 1) * size].reshape(groups, GROUP, width)
                ref[:, task, pl.ds(begin + block * GROUP, GROUP), :] = part

        row = lax.broadcasted_iota(jnp.int32, (chunk, 1), 0)
        row = (row // size) * GROUP + row % GROUP + begin + p.feat * block_rows
        live = jnp.where(row < r.counts[task], 1.0, 0.0)

        hidden_one = load(r.hidden_blocks).astype(F32)
        unit_two, scale_two = normalise(hidden_one)
        normed_two = (unit_two * param(2) + param(3)).astype(BF16)
        r.block_triple[...] = nn(normed_two, flat(r.w_project_two)).astype(BF16)
        reach = min(PAIR, size)
        key_at = lax.broadcasted_iota(jnp.int32, (size, 2 * reach), 0) % GROUP
        query_at = lax.broadcasted_iota(jnp.int32, (size, 2 * reach), 1) % GROUP
        bias = jnp.where(key_at == query_at, 0.0, MASKED)
        for block in range(blocks):
            where = pl.ds(block * size, size)
            for pair in range(pairs):
                lanes = pair * PAIR
                key = r.block_triple[where, pl.ds(width + lanes, PAIR)]
                value_turned = r.block_triple[where, pl.ds(2 * width + lanes, PAIR)].T
                query = r.block_triple[where, pl.ds(lanes, PAIR)]
                result, log_total = attend(query, key, value_turned, bias, head_scale)
                r.block_mixed[where, pl.ds(lanes, PAIR)] = result.astype(BF16)
                r.block_logs[pl.ds(block * pairs + pair, 1), :] = log_total

        @pl.when(first)
        def _():
            items["merge_two"].done()

        hidden_two = hidden_one + live * nn(r.block_mixed[...], flat(r.w_merge_two))
        unit_three, scale_three = normalise(hidden_two)
        normed_three = (unit_three * param(4) + param(5)).astype(BF16)
        @pl.when(first)
        def _():
            run("dense")
            upstream[0].wait()

        flow = load(r.upstream_blocks).astype(F32)
        grad_dense = (flow * live).astype(BF16)
        add_vector(6, grad_dense.astype(F32))

        @pl.when(first)
        def _():
            items["expand_low"].done()
            items["shrink_low"].done()
            run("until_shrink")
            items["shrink_high"].done()

        dense = None
        incoming = None
        lanes = hidden_units // DEPTH
        for turn in range(DEPTH):
            cut = pl.ds(turn * lanes, lanes)
            if turn == DEPTH // 2:
                @pl.when(first)
                def _():
                    items["expand_high"].done()

            up_weight = r.w_expand[:, :, :, :, cut].reshape(width, lanes)
            down_weight = r.w_shrink[turn].reshape(lanes, width)
            expanded = nn(normed_three, up_weight) + param(7 + turn)
            square = expanded * expanded
            steep = 0.7978845608028654
            bend = jnp.tanh(expanded * (steep + (steep * 0.044715) * square))
            half_up = 0.5 + 0.5 * bend
            activated = (expanded * half_up).astype(BF16)
            slope = half_up + (0.5 * expanded) * (1.0 - bend * bend) * (
                steep + (3.0 * steep * 0.044715) * square
            )
            grad_expanded = (slope * nt(grad_dense, down_weight)).astype(BF16)
            add_vector(7 + turn, grad_expanded.astype(F32))
            r.t_shrink[turn] += tn(activated, grad_dense).reshape(r.t_shrink.shape[1:])
            r.t_expand[:, :, :, :, cut] += tn(normed_three, grad_expanded).reshape(
                r.t_expand.shape[:4] + (lanes,)
            )
            up = nn(activated, down_weight)
            down = nt(grad_expanded, up_weight)
            dense = up if dense is None else dense + up
            incoming = down if incoming is None else incoming + down
        @pl.when(final)
        def _():
            for name in dense_items:
                items[name].finish()
            run("dense_grads")

        result = hidden_two + live * (dense + param(6))
        store(r.upstream_blocks, result.astype(BF16))

        add_vector(4, incoming * unit_three)
        add_vector(5, incoming)
        flow = flow + normalise_back(incoming, unit_three, scale_three, param(4))
        branch = (flow * live).astype(BF16)
        r.t_merge_two[...] += tn(r.block_mixed[...], branch).reshape(r.t_merge_two.shape)
        r.block_mixed[...] = nt(branch, flat(r.w_merge_two)).astype(BF16)

        @pl.when(final)
        def _():
            run("feature_grads")

        for block in range(blocks):
            where = pl.ds(block * size, size)
            for pair in range(pairs):
                lanes = pair * PAIR
                key = r.block_triple[where, pl.ds(width + lanes, PAIR)]
                value = r.block_triple[where, pl.ds(2 * width + lanes, PAIR)]
                query = r.block_triple[where, pl.ds(lanes, PAIR)]
                grad_query, grad_key, grad_value = attend_back(
                    query, key, value, key.T, r.block_mixed[where, pl.ds(lanes, PAIR)],
                    r.block_logs[pl.ds(block * pairs + pair, 1), :], bias, head_scale,
                )
                r.block_triple[where, pl.ds(lanes, PAIR)] = grad_query.astype(BF16)
                r.block_triple[where, pl.ds(width + lanes, PAIR)] = grad_key.astype(BF16)
                r.block_triple[where, pl.ds(2 * width + lanes, PAIR)] = grad_value.astype(BF16)
        grad_triple = r.block_triple[...]
        r.t_project_two[...] += tn(normed_two, grad_triple).reshape(r.t_project_two.shape)
        incoming = nt(grad_triple, flat(r.w_project_two))
        add_vector(2, incoming * unit_two)
        add_vector(3, incoming)
        flow = flow + normalise_back(incoming, unit_two, scale_two, param(2))
        store(r.hidden_blocks, flow.astype(BF16))
        send_back(
            r.hidden_blocks, r.flow, task, begin,
            r.flow_sent.at[0], r.flow_arrived.at[task], r.flow_local.at[task],
        )
        send_back(
            r.upstream_blocks, r.layer_out, task, begin,
            r.out_sent.at[0], r.out_arrived.at[0], r.out_local.at[0],
        )
        return carry

    lax.fori_loop(0, tasks * per_task, layer_chunk, 0)

    for name in ("query", "key", "value", "merge_one", "project_two", "merge_two"):
        items[name].finish()
    for task in range(tasks):
        hidden[task].finish()
    run("layer_end")
    run("layer_after")

    def flow_in(task):
        most = r.flow.at[task, pl.ds(0, samples - block_rows)]
        return remote(most, most, r.flow_sent.at[0], r.flow_arrived.at[task], p.along_y)

    def wait_flow(task):
        flow_in(task).wait_recv()
        own = r.flow.at[task, pl.ds(0, block_rows)]
        pltpu.make_async_copy(own, own, r.flow_local.at[task]).wait()

    def merge_back(task):
        for start in range(0, samples, chunk):
            live = live_rows(task, start)
            branch = (r.flow[task, pl.ds(start, chunk), :].astype(F32) * live).astype(BF16)
            part = tn(r.mixed_one[task, pl.ds(start, chunk), :], branch)
            part = part.reshape(r.t_merge_one.shape)
            if task == 0 and start == 0:
                r.t_merge_one[...] = part
            else:
                r.t_merge_one[...] += part
            r.grad_mixed[task, pl.ds(start, chunk), :] = nt(branch, flat(r.w_merge_one)).astype(BF16)

    def attend_pairs_back(task, low, high):
        bias = key_bias(task)

        def one_pair(pair, carry):
            lanes = pl.multiple_of(pair * PAIR, PAIR)
            key = r.triple[task, :, pl.ds(lanes + width, PAIR)]
            value = r.triple[task, :, pl.ds(lanes + 2 * width, PAIR)]
            key_turned = key.T
            for at in range(parts):
                query = r.triple[task, pl.ds(at * PAIR, PAIR), pl.ds(lanes, PAIR)]
                grad_out = r.grad_mixed[task, pl.ds(at * PAIR, PAIR), pl.ds(lanes, PAIR)]
                log_total = r.logs_one[pl.ds((task * pairs + pair) * parts + at, 1), :]
                grad_query, grad_key, grad_value = attend_back(
                    query, key, value, key_turned, grad_out, log_total, bias, head_scale
                )
                r.triple[task, pl.ds(at * PAIR, PAIR), pl.ds(lanes, PAIR)] = grad_query.astype(BF16)
                if at == 0:
                    r.key_sum[...] = grad_key
                    r.value_sum[...] = grad_value
                else:
                    r.key_sum[...] += grad_key
                    r.value_sum[...] += grad_value
            r.triple[task, :, pl.ds(lanes + width, PAIR)] = r.key_sum[...].astype(BF16)
            r.triple[task, :, pl.ds(lanes + 2 * width, PAIR)] = r.value_sum[...].astype(BF16)
            return carry

        lax.fori_loop(low, high, one_pair, 0)

    def project_weight(which):
        ref = (r.t_project_low, r.t_project_high)[which]
        lanes = width // 2
        for third in range(3):
            cut = pl.ds(third * width + which * lanes, lanes)
            part = None
            for task in range(tasks):
                one = tn(r.normed_one[task], r.triple[task, :, cut])
                part = one if part is None else part + one
            ref[:, :, :, :, pl.ds(third * lanes, lanes)] = part.reshape(ref.shape[:4] + (lanes,))

    def project_back(task, start):
        rows = r.tokens[task, pl.ds(start, chunk), :].astype(F32)
        normed, scale = normalise(rows)
        incoming = nt(r.triple[task, pl.ds(start, chunk), :], flat(r.w_project_one))
        add_vector(0, incoming * normed)
        add_vector(1, incoming)
        back = normalise_back(incoming, normed, scale, param(0))
        back = r.flow[task, pl.ds(start, chunk), :].astype(F32) + back
        tiles = width // PAIR
        for tile in range(tiles):
            r.input_grad[task, pl.ds(start * tiles + tile, chunk, stride=tiles), :] = back[
                :, tile * PAIR : (tile + 1) * PAIR
            ]

    half = pairs // 2
    for task in range(tasks):
        wait_flow(task)
        merge_back(task)
        if task == tasks - 1:
            run("merge_grads")
        run("merged%d" % task)
        for pair in range(pairs):
            attend_pairs_back(task, pair, pair + 1)
            run("back%d%d" % (task, pair))
            if task == tasks - 1 and pair == half - 1:
                project_weight(0)
                run("low_grads")
                run("low")
    project_weight(1)
    run("high_grads")
    run("high")
    for task in range(tasks):
        for start in range(0, samples, chunk):
            project_back(task, start)
            run("first%d" % (task * (samples // chunk) + start // chunk))

    r.vector_slots_out[p.feat] = r.vector_sums[...]
    for shift in range(1, groups):
        remote(
            r.vector_sums, r.vector_slots_out.at[p.feat],
            r.vector_sent.at[1], r.vector_arrived.at[1], (p.task, p.peer(shift, groups)),
        ).start()
    ending = SCHEDULE["end"]
    middle = ending.index(("d_project_high", "inward")) + 1
    for name, stage in ending[:middle]:
        getattr(items[name], stage)()

    def vectors_out(stage, slots, count):
        most = slots.at[pl.ds(0, count - 1)]
        return remote(most, most, r.vector_sent.at[stage], r.vector_arrived.at[stage], p.along_y)

    vectors_out(1, r.vector_slots_out, groups).wait_recv()
    total = r.vector_slots_out[0]
    for index in range(1, groups):
        total = total + r.vector_slots_out[index]
    r.vector_total[...] = total
    r.task_slots[p.task] = total
    for device in (p.sibling, p.along_x, (CORES * (1 - p.x) + 1 - p.c, p.feat)):
        remote(
            r.vector_total, r.task_slots.at[p.task],
            r.vector_sent.at[2], r.vector_arrived.at[2], device,
        ).start()
    for name, stage in ending[middle:]:
        getattr(items[name], stage)()
    for at, end in enumerate(("low", "high")):
        item = items["d_shrink_" + end]
        item.done()
        r.o_shrink[:, pl.ds(at * deep, deep), :] = item.final[...]
        item = items["d_expand_" + end]
        item.done()
        r.o_expand[:, :, pl.ds(at * half_units, half_units)] = item.final[...]
    for name in ("project_two", "merge_two", "merge_one"):
        item = items["d_" + name]
        item.done()
        getattr(r, "o_" + name)[...] = item.final[...]
    vectors_out(2, r.task_slots, members).wait_recv()
    total = r.task_slots[0]
    for index in range(1, members):
        total = total + r.task_slots[index]
    r.o_vectors[...] = total
    lanes = width // 2
    for which, end in enumerate(("low", "high")):
        item = items["d_project_" + end]
        item.done()
        for part in range(3):
            r.o_project_one[:, :, pl.ds(part * width + which * lanes, lanes)] = item.final[
                :, :, pl.ds(part * lanes, lanes)
            ]

    vectors_in().wait_send()
    vectors_out(1, r.vector_slots_out, groups).wait_send()
    vectors_out(2, r.task_slots, members).wait_send()
    for task in range(tasks):
        upstream[task].finish()
    everywhere = r.flow.at[:, pl.ds(0, samples - block_rows)]
    remote(everywhere, everywhere, r.flow_sent.at[0], r.flow_arrived.at[0], p.along_y).wait_send()
    everywhere = r.layer_out.at[:, pl.ds(0, samples - block_rows)]
    both = remote(everywhere, everywhere, r.out_sent.at[0], r.out_arrived.at[0], p.along_y)
    both.wait_send()
    both.wait_recv()
    own = r.layer_out.at[:, pl.ds(0, block_rows)]
    pltpu.make_async_copy(own, own, r.out_local.at[0]).wait()
    for item in reductions:
        item.finish()


def finish_kernel(*refs):
    count = 9
    sources, targets = refs[:count], refs[count : count + 16]
    held = refs[count + 16 : 2 * count + 16]
    made = refs[2 * count + 16 : 2 * count + 22]
    read, written = refs[2 * count + 22 :]
    reads = [
        pltpu.make_async_copy(source, memory, read.at[at])
        for at, (source, memory) in enumerate(zip(sources, held))
    ]
    for copy in reads:
        copy.start()
    writes = []
    for at in range(2, 8):
        reads[at].wait()
        made[at - 2][...] = held[at][...].astype(F32)
        writes.append(pltpu.make_async_copy(made[at - 2], targets[at], written.at[at]))
        writes[-1].start()
    for at in range(2):
        reads[at].wait()
        writes.append(pltpu.make_async_copy(held[at], targets[at], written.at[at]))
        writes[-1].start()
    reads[8].wait()
    vectors_ref, small_to, bias_to = held[8], targets[8:15], targets[15]
    place = lax.axis_index("feat")
    width = vectors_ref.shape[1]
    size = small_to[0].shape[1]
    turned = pltpu.roll(vectors_ref[...], lax.rem(width - place * size, width), 1)
    for row, target in enumerate(small_to):
        target[...] = turned[row : row + 1, :size]
    size = bias_to.shape[1]
    per_row = width // size
    row = vectors_ref[pl.ds(len(small_to) + lax.div(place, per_row), 1), :]
    bias = row[:, :size]
    for at in range(1, per_row):
        bias = jnp.where(lax.rem(place, per_row) == at, row[:, at * size : (at + 1) * size], bias)
    bias_to[...] = bias
    for copy in writes:
        copy.wait()


def fused_body(tokens, cotangent, counts, *shards):
    (
        gain_one, shift_one, project_one, merge_one, gain_two, shift_two, project_two, merge_two,
        gain_three, shift_three, expand, bias_in, shrink, bias_out,
    ) = shards
    groups = lax.axis_size("feat")
    members = lax.axis_size("task")
    place = lax.axis_index("feat")
    tasks, samples, _, width = tokens.shape
    block_rows = samples // groups
    hidden_units = expand.shape[1]
    pairs = width // PAIR

    small = (
        gain_one, shift_one, gain_two, shift_two, gain_three, shift_three, bias_out,
    )
    length = sum(part.shape[0] for part in (bias_in,) + small)
    slots = -(-length // (8 * PAIR)) * 8
    vectors, low = None, 0
    for part in (bias_in,) + small:
        high = slots * PAIR - low - part.shape[0]
        moved = jnp.pad(part.astype(F32), (low, high))
        vectors = moved if vectors is None else vectors + moved
        low += part.shape[0]
    vectors = vectors.reshape(slots, PAIR)

    big = {
        "project_one": project_one, "merge_one": merge_one, "project_two": project_two,
        "merge_two": merge_two, "expand": expand, "shrink": shrink,
    }
    names, operands, specs = [], [], []

    def operand(name, value, spec):
        names.append(name)
        operands.append(value)
        specs.append(spec)

    any_spec = pl.BlockSpec(memory_space=pl.ANY)
    operand("counts", counts, SMEM)
    operand("tokens", tokens.reshape(tasks, samples, width), VMEM)
    operand("upstream", cotangent.reshape(tasks, samples, width), any_spec)
    operand("vectors", vectors, any_spec)
    shapes = {}
    for name, shard in big.items():
        rows, columns = shard.shape[0] // SPLIT, shard.shape[1]
        shapes[name] = (rows, columns)
        operand("s_" + name, shard.reshape(SPLIT, rows, columns), any_spec)

    outs, out_specs = [], []

    def output(name, dims, kind, spec):
        names.append(name)
        outs.append(shape(dims, kind))
        out_specs.append(spec)

    output("layer_out", (tasks, samples, width), BF16, any_spec)
    output("input_grad", (tasks, samples * width // PAIR, PAIR), F32, VMEM)
    for name in big:
        output("o_" + name, (SPLIT,) + shapes[name], BF16, VMEM)
    output("o_vectors", (VECTORS, width), F32, VMEM)

    scratch = []

    def memory(name, dims, kind):
        names.append(name)
        scratch.append(pltpu.VMEM(dims, kind))

    def semaphores(name, dims):
        names.append(name)
        scratch.append(pltpu.SemaphoreType.DMA(dims))

    for name in big:
        memory("w_" + name, (DEPTH, WIDE_Y, SPLIT) + shapes[name], BF16)
    for name in big:
        if name != "project_one":
            memory("t_" + name, (DEPTH, WIDE_Y, SPLIT) + shapes[name], F32)
    rows, columns = shapes["project_one"]
    for name in ("project_low", "project_high"):
        memory("t_" + name, (DEPTH, WIDE_Y, SPLIT, rows, columns // 2), F32)
        memory("b_" + name, (DEPTH, WIDE_Y, SPLIT, rows, columns // 2), BF16)
    rows, columns = shapes["shrink"]
    shrink_part = (rows // 2, columns)
    rows, columns = shapes["expand"]
    expand_part = (rows, columns // 2)
    rows, columns = shapes["project_one"]
    half_project = (rows, columns // 2)
    items = (
        (shrink_part, True, False), (shrink_part, True, False),
        (expand_part, False, False), (expand_part, False, False),
        (shapes["project_two"], False, False), (shapes["merge_two"], False, False),
        (shapes["merge_one"], True, True), (half_project, True, True), (half_project, True, True),
    )
    for index, (dims, wide, direct) in enumerate(items):
        count = HALVES if wide else 1
        sizes = {
            "halves": (DEPTH, WIDE_Y, HALVES), "quarters": (DEPTH, WIDE_Y, 1),
            "lines": (DEPTH, count), "outer": (DEPTH - 1 if direct else 2, count),
            "crossed": (2, count), "paired": (count,), "final": (SPLIT,), "twin": (count,),
        }
        unused = {"quarters" if wide else "twin"}
        if direct:
            unused |= {"crossed", "paired"}
        for kind in BUFFERS:
            if kind not in unused:
                memory("m%d_%s" % (index, kind), sizes[kind] + dims, BF16)
    memory("vector_slots", (groups, slots, PAIR), F32)
    memory("params", (VECTORS, width), F32)
    memory("vector_sums", (VECTORS, width), F32)
    memory("vector_slots_out", (groups, VECTORS, width), F32)
    memory("vector_total", (VECTORS, width), F32)
    memory("task_slots", (members, VECTORS, width), F32)
    memory("normed_one", (tasks, samples, width), BF16)
    memory("triple", (tasks, samples, 3 * width), BF16)
    memory("mixed_one", (tasks, samples, width), BF16)
    memory("logs_one", (tasks * pairs * (samples // PAIR), 2 * PAIR), F32)
    memory("grad_mixed", (tasks, samples, width), BF16)
    memory("flow", (tasks, samples, width), BF16)
    memory("hidden_blocks", (groups, tasks, block_rows, width), BF16)
    memory("upstream_blocks", (groups, tasks, block_rows, width), BF16)
    memory("block_triple", (256, 3 * width), BF16)
    memory("block_mixed", (256, width), BF16)
    memory("block_logs", (8, 2 * PAIR), F32)
    memory("key_sum", (samples, PAIR), F32)
    memory("value_sum", (samples, PAIR), F32)
    semaphores("gather_sent", (10, 6))
    semaphores("gather_arrived", (10, 6))
    semaphores("gather_local", (10,))
    semaphores("reduce_sent", (len(items), 8))
    semaphores("reduce_arrived", (len(items), 8))
    for name in ("vector_sent", "vector_arrived"):
        semaphores(name, (3,))
    semaphores("vector_local", (1,))
    for name in ("upstream", "hidden"):
        for kind in ("_sent", "_arrived", "_local"):
            semaphores(name + kind, (tasks,))
    semaphores("flow_sent", (1,))
    semaphores("flow_arrived", (tasks,))
    semaphores("flow_local", (tasks,))
    for kind in ("_sent", "_arrived", "_local"):
        semaphores("out" + kind, (1,))

    results = pl.pallas_call(
        functools.partial(fused_kernel, tuple(names)),
        in_specs=specs,
        out_specs=out_specs,
        out_shape=outs,
        scratch_shapes=scratch,
        compiler_params=pltpu.CompilerParams(
            vmem_limit_bytes=FUSED_LIMIT, collective_id=0, has_side_effects=True
        ),
        name="layer",
    )(*operands)
    outs = [
        shape((tasks, samples, width), BF16),
        shape((tasks, samples * width // PAIR, PAIR), F32),
    ]
    outs += [shape((SPLIT,) + shapes[name], F32) for name in big]
    outs += [shape((1, part.shape[0]), F32) for part in small]
    outs += [shape((1, bias_in.shape[0]), F32)]
    finished = pl.pallas_call(
        finish_kernel,
        in_specs=[any_spec] * len(results),
        out_specs=[any_spec] * (2 + len(big)) + [VMEM] * (len(small) + 1),
        out_shape=outs,
        scratch_shapes=[pltpu.VMEM(result.shape, result.dtype) for result in results]
        + [pltpu.VMEM(out.shape, F32) for out in outs[2 : 2 + len(big)]]
        + [pltpu.SemaphoreType.DMA((len(results),))] * 2,
        compiler_params=pltpu.CompilerParams(vmem_limit_bytes=FINISH_LIMIT),
        name="finish",
    )(*results)
    grads = {
        name: result.reshape(big[name].shape) for name, result in zip(big, finished[2:])
    }
    ends = [part.reshape(-1) for part in finished[2 + len(big):]]
    return (
        finished[0].reshape(tokens.shape), finished[1].reshape(tokens.shape),
        ends[0], ends[1], grads["project_one"], grads["merge_one"],
        ends[2], ends[3], grads["project_two"], grads["merge_two"],
        ends[4], ends[5], grads["expand"], ends[7], grads["shrink"], ends[6],
    )


def solution(mesh):
    wide = P("task", None, "feat", None)
    row, grid = P("feat"), P("feat", None)
    weights = (
        row, row, grid, grid, row, row, grid, grid, row, row, grid, row, grid, row,
    )
    fits = mesh.shape["feat"] == DEPTH * WIDE_Y and mesh.shape["task"] == CORES * HALVES
    return jax.shard_map(
        fused_body if fits else body,
        mesh=mesh,
        in_specs=(wide, wide, P("task")) + weights,
        out_specs=(wide, wide) + weights,
        check_vma=False,
    )
```

```python
import functools
import types

import jax
import jax.numpy as jnp
from jax import lax
from jax.experimental import pallas as pl
from jax.experimental.pallas import tpu as pltpu
from jax.sharding import PartitionSpec as P

HEADS = 8
NORM_EPS = 1e-05
MASKED = -1e30
PAIR = 128
GROUP = 16
F32 = jnp.float32
BF16 = jnp.bfloat16


def nt(left, right):
    return lax.dot_general(left, right, (((1,), (1,)), ((), ())), preferred_element_type=F32)


def tn(left, right):
    return lax.dot_general(left, right, (((0,), (0,)), ((), ())), preferred_element_type=F32)


def nn(left, right):
    return lax.dot_general(left, right, (((1,), (0,)), ((), ())), preferred_element_type=F32)


def normalise(values):
    center = values - jnp.mean(values, axis=-1, keepdims=True)
    spread = jnp.mean(center * center, axis=-1, keepdims=True)
    scale = lax.rsqrt(spread + NORM_EPS)
    return center * scale, scale


def normalise_back(incoming, normed, scale, gain):
    weighted = incoming * gain
    first = jnp.mean(weighted, axis=-1, keepdims=True)
    second = jnp.mean(weighted * normed, axis=-1, keepdims=True)
    return scale * (weighted - first - normed * second)


def head_masks(scale):
    lane = lax.broadcasted_iota(jnp.int32, (1, PAIR), 1)
    low = jnp.where(lane < PAIR // 2, scale, 0.0).astype(BF16)
    high = jnp.where(lane < PAIR // 2, 0.0, scale).astype(BF16)
    return low, high


def two_heads(rows, scale):
    low, high = head_masks(scale)
    return jnp.concatenate([rows * low, rows * high], axis=0)


def join_heads(turned, length):
    half = PAIR // 2
    joined = jnp.concatenate([turned[:half, :length], turned[half:, length:]], axis=0)
    return joined.T


def attend(query, key, value_turned, bias, head_scale):
    scores = nt(key, two_heads(query, head_scale)) + bias
    top = jnp.max(scores, axis=0, keepdims=True)
    expo = jnp.exp(scores - top)
    total = jnp.sum(expo, axis=0, keepdims=True)
    mixed = nn(value_turned, expo.astype(BF16)) * (1.0 / total)
    return join_heads(mixed, query.shape[0]), top + jnp.log(total)


def attend_back(
    query, key, value, key_turned, result, grad_out, log_total, bias, head_scale
):
    half = PAIR // 2
    product = (result.astype(F32) * grad_out.astype(F32)).T
    inner = jnp.concatenate(
        [
            jnp.sum(product[:half], axis=0, keepdims=True),
            jnp.sum(product[half:], axis=0, keepdims=True),
        ],
        axis=1,
    )
    queries = two_heads(query, head_scale)
    grads = two_heads(grad_out, 1.0)
    chances = jnp.exp(nt(key, queries) + bias - log_total)
    grad_scores = (chances * (nt(value, grads) - inner)).astype(BF16)
    grad_value = nn(chances.astype(BF16), grads)
    grad_key = nn(grad_scores, queries)
    grad_query = join_heads(nn(key_turned, grad_scores), query.shape[0]) * head_scale
    return grad_query, grad_key, grad_value


def sample_forward_kernel(
    counts_ref, tokens_ref, gain_ref, shift_ref, project_ref, merge_ref,
    triple_ref, mixed_ref, logs_ref, hidden_ref,
):
    count = counts_ref[pl.program_id(0)]
    samples, width = tokens_ref.shape[1:]
    chunk = min(256, samples)
    gain = gain_ref[...].astype(F32)
    shift = shift_ref[...].astype(F32)
    for start in range(0, samples, chunk):
        rows = tokens_ref[0, pl.ds(start, chunk), :].astype(F32)
        normed = (normalise(rows)[0] * gain + shift).astype(BF16)
        triple_ref[0, pl.ds(start, chunk), :] = nn(normed, project_ref[...]).astype(BF16)
    keys = lax.broadcasted_iota(jnp.int32, (samples, 1), 0)
    bias = jnp.where(keys < count, 0.0, MASKED)
    head_scale = (width // HEADS) ** (-0.5)
    pairs = width // PAIR

    def one_pair(pair, carry):
        lanes = pl.multiple_of(pair * PAIR, PAIR)
        key = triple_ref[0, :, pl.ds(lanes + width, PAIR)]
        value_turned = triple_ref[0, :, pl.ds(lanes + 2 * width, PAIR)].T
        for at in range(samples // PAIR):
            query = triple_ref[0, pl.ds(at * PAIR, PAIR), pl.ds(lanes, PAIR)]
            mixed, log_total = attend(query, key, value_turned, bias, head_scale)
            mixed_ref[0, pl.ds(at * PAIR, PAIR), pl.ds(lanes, PAIR)] = mixed.astype(BF16)
            logs_ref[0, pl.ds(pair * (samples // PAIR) + at, 1), :] = log_total
        return carry

    lax.fori_loop(0, pairs, one_pair, 0)
    for start in range(0, samples, chunk):
        rows = tokens_ref[0, pl.ds(start, chunk), :].astype(F32)
        at = lax.broadcasted_iota(jnp.int32, (chunk, 1), 0) + start
        live = jnp.where(at < count, 1.0, 0.0)
        merged = nn(mixed_ref[0, pl.ds(start, chunk), :], merge_ref[...])
        hidden_ref[0, pl.ds(start, chunk), :] = (rows + live * merged).astype(BF16)


def sample_backward_kernel(
    counts_ref, tokens_ref, gain_ref, shift_ref, project_ref, merge_ref,
    triple_ref, mixed_ref, logs_ref, flow_ref,
    input_grad_ref, project_grad_ref, merge_grad_ref, gain_grad_ref, shift_grad_ref,
    grad_mixed, grad_triple, key_sum, value_sum,
):
    task = pl.program_id(0)
    count = counts_ref[task]
    samples, width = tokens_ref.shape[1:]
    chunk = min(256, samples)
    gain = gain_ref[...].astype(F32)
    shift = shift_ref[...].astype(F32)

    @pl.when(task == 0)
    def _():
        project_grad_ref[...] = jnp.zeros_like(project_grad_ref)
        merge_grad_ref[...] = jnp.zeros_like(merge_grad_ref)
        gain_grad_ref[...] = jnp.zeros_like(gain_grad_ref)
        shift_grad_ref[...] = jnp.zeros_like(shift_grad_ref)

    for start in range(0, samples, chunk):
        at = lax.broadcasted_iota(jnp.int32, (chunk, 1), 0) + start
        live = jnp.where(at < count, 1.0, 0.0)
        branch = (flow_ref[0, pl.ds(start, chunk), :].astype(F32) * live).astype(BF16)
        merge_grad_ref[...] += tn(mixed_ref[0, pl.ds(start, chunk), :], branch)
        grad_mixed[pl.ds(start, chunk), :] = nt(branch, merge_ref[...]).astype(BF16)
    keys = lax.broadcasted_iota(jnp.int32, (samples, 1), 0)
    bias = jnp.where(keys < count, 0.0, MASKED)
    head_scale = (width // HEADS) ** (-0.5)
    pairs = width // PAIR

    def one_pair(pair, carry):
        lanes = pl.multiple_of(pair * PAIR, PAIR)
        key = triple_ref[0, :, pl.ds(lanes + width, PAIR)]
        value = triple_ref[0, :, pl.ds(lanes + 2 * width, PAIR)]
        key_turned = key.T
        for at in range(samples // PAIR):
            query = triple_ref[0, pl.ds(at * PAIR, PAIR), pl.ds(lanes, PAIR)]
            grad_out = grad_mixed[pl.ds(at * PAIR, PAIR), pl.ds(lanes, PAIR)]
            log_total = logs_ref[0, pl.ds(pair * (samples // PAIR) + at, 1), :]
            grad_query, grad_key, grad_value = attend_back(
                query, key, value, key_turned,
                mixed_ref[0, pl.ds(at * PAIR, PAIR), pl.ds(lanes, PAIR)],
                grad_out, log_total, bias, head_scale,
            )
            grad_triple[pl.ds(at * PAIR, PAIR), pl.ds(lanes, PAIR)] = grad_query.astype(BF16)
            if at == 0:
                key_sum[...] = grad_key
                value_sum[...] = grad_value
            else:
                key_sum[...] += grad_key
                value_sum[...] += grad_value
        grad_triple[:, pl.ds(lanes + width, PAIR)] = key_sum[...].astype(BF16)
        grad_triple[:, pl.ds(lanes + 2 * width, PAIR)] = value_sum[...].astype(BF16)
        return carry

    lax.fori_loop(0, pairs, one_pair, 0)
    for start in range(0, samples, chunk):
        rows = tokens_ref[0, pl.ds(start, chunk), :].astype(F32)
        normed, scale = normalise(rows)
        part = grad_triple[pl.ds(start, chunk), :]
        project_grad_ref[...] += tn((normed * gain + shift).astype(BF16), part)
        incoming = nt(part, project_ref[...])
        gain_grad_ref[...] += jnp.sum(incoming * normed, axis=0, keepdims=True)
        shift_grad_ref[...] += jnp.sum(incoming, axis=0, keepdims=True)
        back = normalise_back(incoming, normed, scale, gain)
        input_grad_ref[0, pl.ds(start, chunk), :] = (
            flow_ref[0, pl.ds(start, chunk), :].astype(F32) + back
        )


def block_kernel(
    rows_per_task, blocks,
    counts_ref, hidden_ref, upstream_ref,
    gain_two_ref, shift_two_ref, project_ref, merge_ref,
    gain_three_ref, shift_three_ref, expand_ref, bias_in_ref, shrink_ref, bias_out_ref,
    out_ref, flow_ref,
    gain_two_grad, shift_two_grad, project_grad, merge_grad,
    gain_three_grad, shift_three_grad, expand_grad, bias_in_grad, shrink_grad, bias_out_grad,
    triple, mixed, logs, grad_mixed, grad_triple, key_sum, value_sum,
):
    step = pl.program_id(0)
    place = lax.axis_index("feat")
    feats, _, width = hidden_ref.shape
    size = feats * GROUP
    rows = blocks * size
    hidden_units = expand_ref.shape[1]
    sums = (
        gain_two_grad, shift_two_grad, project_grad, merge_grad, gain_three_grad,
        shift_three_grad, expand_grad, bias_in_grad, shrink_grad, bias_out_grad,
    )

    @pl.when(step == 0)
    def _():
        for ref in sums:
            ref[...] = jnp.zeros_like(ref)

    def load(ref):
        pieces = [
            ref[:, pl.ds(block * GROUP, GROUP), :].reshape(size, width) for block in range(blocks)
        ]
        return pieces[0] if blocks == 1 else jnp.concatenate(pieces, axis=0)

    def store(ref, values):
        for block in range(blocks):
            piece = values[block * size : (block + 1) * size]
            ref[:, pl.ds(block * GROUP, GROUP), :] = piece.reshape(feats, GROUP, width)

    row = lax.broadcasted_iota(jnp.int32, (rows, 1), 0)
    row = (step * blocks + row // size) * GROUP + row % GROUP
    sample = place * rows_per_task + row % rows_per_task
    count = jnp.zeros_like(row)
    for task in range(counts_ref.shape[0]):
        count = jnp.where(row // rows_per_task == task, counts_ref[task], count)
    live = jnp.where(sample < count, 1.0, 0.0)

    gain_two = gain_two_ref[...].astype(F32)
    shift_two = shift_two_ref[...].astype(F32)
    gain_three = gain_three_ref[...].astype(F32)
    shift_three = shift_three_ref[...].astype(F32)
    hidden_one = load(hidden_ref).astype(F32)
    unit_two, scale_two = normalise(hidden_one)
    normed_two = (unit_two * gain_two + shift_two).astype(BF16)
    triple[...] = nn(normed_two, project_ref[...]).astype(BF16)

    reach = min(PAIR, size)
    key_at = lax.broadcasted_iota(jnp.int32, (size, 2 * reach), 0) % GROUP
    query_at = lax.broadcasted_iota(jnp.int32, (size, 2 * reach), 1) % GROUP
    bias = jnp.where(key_at == query_at, 0.0, MASKED)
    head_scale = (width // HEADS) ** (-0.5)
    parts = size // reach
    pairs = width // PAIR
    for block in range(blocks):
        start = block * size
        for pair in range(pairs):
            lanes = pair * PAIR
            key = triple[pl.ds(start, size), pl.ds(width + lanes, PAIR)]
            value_turned = triple[pl.ds(start, size), pl.ds(2 * width + lanes, PAIR)].T
            for part in range(parts):
                at = start + part * reach
                query = triple[pl.ds(at, reach), pl.ds(lanes, PAIR)]
                result, log_total = attend(query, key, value_turned, bias, head_scale)
                mixed[pl.ds(at, reach), pl.ds(lanes, PAIR)] = result.astype(BF16)
                logs[pl.ds((block * pairs + pair) * parts + part, 1), :] = log_total

    hidden_two = hidden_one + live * nn(mixed[...], merge_ref[...])
    unit_three, scale_three = normalise(hidden_two)
    normed_three = (unit_three * gain_three + shift_three).astype(BF16)
    upstream = load(upstream_ref).astype(F32)
    grad_dense = (upstream * live).astype(BF16)
    bias_out_grad[...] += jnp.sum(grad_dense.astype(F32), axis=0, keepdims=True)
    lanes = min(512, hidden_units)
    dense = None
    incoming = None
    for start in range(0, hidden_units, lanes):
        cut = pl.ds(start, lanes)
        expanded = nn(normed_three, expand_ref[:, cut]) + bias_in_ref[:, cut].astype(F32)
        square = expanded * expanded
        steep = 0.7978845608028654
        bend = jnp.tanh(expanded * (steep + (steep * 0.044715) * square))
        half_up = 0.5 + 0.5 * bend
        activated = (expanded * half_up).astype(BF16)
        slope = half_up + (0.5 * expanded) * (1.0 - bend * bend) * (
            steep + (3.0 * steep * 0.044715) * square
        )
        grad_expanded = (slope * nt(grad_dense, shrink_ref[cut, :])).astype(BF16)
        bias_in_grad[:, cut] += jnp.sum(grad_expanded.astype(F32), axis=0, keepdims=True)
        shrink_grad[cut, :] += tn(activated, grad_dense)
        expand_grad[:, cut] += tn(normed_three, grad_expanded)
        up = nn(activated, shrink_ref[cut, :])
        down = nt(grad_expanded, expand_ref[:, cut])
        dense = up if dense is None else dense + up
        incoming = down if incoming is None else incoming + down
    result = hidden_two + live * (dense + bias_out_ref[...].astype(F32))
    store(out_ref, result.astype(BF16))

    gain_three_grad[...] += jnp.sum(incoming * unit_three, axis=0, keepdims=True)
    shift_three_grad[...] += jnp.sum(incoming, axis=0, keepdims=True)
    flow_two = upstream + normalise_back(incoming, unit_three, scale_three, gain_three)
    branch = (flow_two * live).astype(BF16)
    merge_grad[...] += tn(mixed[...], branch)
    grad_mixed[...] = nt(branch, merge_ref[...]).astype(BF16)
    for block in range(blocks):
        start = block * size
        for pair in range(pairs):
            lanes = pair * PAIR
            key = triple[pl.ds(start, size), pl.ds(width + lanes, PAIR)]
            value = triple[pl.ds(start, size), pl.ds(2 * width + lanes, PAIR)]
            key_turned = key.T
            for part in range(parts):
                at = start + part * reach
                query = triple[pl.ds(at, reach), pl.ds(lanes, PAIR)]
                grad_out = grad_mixed[pl.ds(at, reach), pl.ds(lanes, PAIR)]
                log_total = logs[pl.ds((block * pairs + pair) * parts + part, 1), :]
                grad_query, grad_key, grad_value = attend_back(
                    query, key, value, key_turned, mixed[pl.ds(at, reach), pl.ds(lanes, PAIR)],
                    grad_out, log_total, bias, head_scale,
                )
                grad_triple[pl.ds(at, reach), pl.ds(lanes, PAIR)] = grad_query.astype(BF16)
                if part > 0:
                    grad_key += key_sum[...]
                    grad_value += value_sum[...]
                if part == parts - 1:
                    where = pl.ds(start, size)
                    grad_triple[where, pl.ds(width + lanes, PAIR)] = grad_key.astype(BF16)
                    grad_triple[where, pl.ds(2 * width + lanes, PAIR)] = grad_value.astype(BF16)
                else:
                    key_sum[...] = grad_key
                    value_sum[...] = grad_value
    project_grad[...] += tn(normed_two, grad_triple[...])
    incoming = nt(grad_triple[...], project_ref[...])
    gain_two_grad[...] += jnp.sum(incoming * unit_two, axis=0, keepdims=True)
    shift_two_grad[...] += jnp.sum(incoming, axis=0, keepdims=True)
    flow_one = flow_two + normalise_back(incoming, unit_two, scale_two, gain_two)
    store(flow_ref, flow_one.astype(BF16))


VMEM = pl.BlockSpec(memory_space=pltpu.VMEM)
SMEM = pl.BlockSpec(memory_space=pltpu.SMEM)
LIMIT = 56 * 1024 * 1024


def shape(dims, kind):
    return jax.ShapeDtypeStruct(dims, kind)


def by_task(*dims):
    return pl.BlockSpec((1,) + dims, lambda task: (task,) + (0,) * len(dims))


def body(tokens, cotangent, counts, *shards):
    groups = lax.axis_size("feat")
    tasks, samples, local, width = tokens.shape
    rows_per_task = samples // groups
    gathered = [lax.all_gather(part, "feat", axis=0, tiled=True) for part in shards]
    gathered = [part[None, :] if part.ndim == 1 else part for part in gathered]
    (
        gain_one, shift_one, project_one, merge_one, gain_two, shift_two, project_two, merge_two,
        gain_three, shift_three, expand, bias_in, shrink, bias_out,
    ) = gathered
    hidden_units = expand.shape[1]
    source = tokens.reshape(tasks, samples, width)

    def to_blocks(rows):
        rows = rows.reshape(tasks, groups, rows_per_task, width)
        rows = jnp.transpose(rows, (1, 0, 2, 3))
        rows = lax.all_to_all(rows, "feat", split_axis=0, concat_axis=0, tiled=True)
        return rows.reshape(groups, tasks * rows_per_task, width)

    def from_blocks(rows):
        rows = rows.reshape(groups, tasks, rows_per_task, width)
        rows = lax.all_to_all(rows, "feat", split_axis=0, concat_axis=0, tiled=True)
        rows = jnp.transpose(rows, (1, 0, 2, 3))
        return rows.reshape(tasks, samples, width)

    upstream = to_blocks(cotangent.reshape(tasks, samples, width))
    log_rows = samples * width // PAIR // PAIR
    triple, mixed, logs, hidden = pl.pallas_call(
        sample_forward_kernel,
        grid=(tasks,),
        in_specs=[SMEM, by_task(samples, width), VMEM, VMEM, VMEM, VMEM],
        out_specs=[
            by_task(samples, 3 * width), by_task(samples, width),
            by_task(log_rows, 2 * PAIR), by_task(samples, width),
        ],
        out_shape=[
            shape((tasks, samples, 3 * width), BF16),
            shape((tasks, samples, width), BF16),
            shape((tasks, log_rows, 2 * PAIR), F32),
            shape((tasks, samples, width), BF16),
        ],
        compiler_params=pltpu.CompilerParams(vmem_limit_bytes=LIMIT),
        name="sample_forward",
    )(counts, source, gain_one, shift_one, project_one, merge_one)

    hidden = to_blocks(hidden)
    all_rows = tasks * rows_per_task
    size = groups * GROUP
    blocks = max(1, min(all_rows // GROUP, 256 // size))
    steps = all_rows // (GROUP * blocks)
    rows = blocks * size
    slab = pl.BlockSpec((groups, GROUP * blocks, width), lambda step: (0, step, 0))
    reach = min(PAIR, size)
    pieces = blocks * (width // PAIR) * (size // reach)
    grads = [
        shape((1, width), F32), shape((1, width), F32),
        shape((width, 3 * width), F32), shape((width, width), F32),
        shape((1, width), F32), shape((1, width), F32),
        shape((width, hidden_units), F32), shape((1, hidden_units), F32),
        shape((hidden_units, width), F32), shape((1, width), F32),
    ]
    results = pl.pallas_call(
        functools.partial(block_kernel, rows_per_task, blocks),
        grid=(steps,),
        in_specs=[SMEM, slab, slab] + [VMEM] * 10,
        out_specs=[slab, slab] + [VMEM] * 10,
        out_shape=[shape((groups, all_rows, width), BF16)] * 2 + grads,
        scratch_shapes=[
            pltpu.VMEM((rows, 3 * width), BF16),
            pltpu.VMEM((rows, width), BF16),
            pltpu.VMEM((pieces, 2 * reach), F32),
            pltpu.VMEM((rows, width), BF16),
            pltpu.VMEM((rows, 3 * width), BF16),
            pltpu.VMEM((size, PAIR), F32),
            pltpu.VMEM((size, PAIR), F32),
        ],
        compiler_params=pltpu.CompilerParams(vmem_limit_bytes=LIMIT),
        name="block_layer",
    )(
        counts, hidden, upstream, gain_two, shift_two, project_two, merge_two,
        gain_three, shift_three, expand, bias_in, shrink, bias_out,
    )
    layer_out = from_blocks(results[0])
    flow = from_blocks(results[1])

    first = pl.pallas_call(
        sample_backward_kernel,
        grid=(tasks,),
        in_specs=[
            SMEM, by_task(samples, width), VMEM, VMEM, VMEM, VMEM,
            by_task(samples, 3 * width), by_task(samples, width),
            by_task(log_rows, 2 * PAIR), by_task(samples, width),
        ],
        out_specs=[by_task(samples, width), VMEM, VMEM, VMEM, VMEM],
        out_shape=[
            shape((tasks, samples, width), F32),
            shape((width, 3 * width), F32), shape((width, width), F32),
            shape((1, width), F32), shape((1, width), F32),
        ],
        scratch_shapes=[
            pltpu.VMEM((samples, width), BF16),
            pltpu.VMEM((samples, 3 * width), BF16),
            pltpu.VMEM((samples, PAIR), F32),
            pltpu.VMEM((samples, PAIR), F32),
        ],
        compiler_params=pltpu.CompilerParams(vmem_limit_bytes=LIMIT),
        name="sample_backward",
    )(
        counts, source, gain_one, shift_one, project_one, merge_one, triple, mixed, logs, flow,
    )
    (
        gain_two_grad, shift_two_grad, project_two_grad, merge_two_grad, gain_three_grad,
        shift_three_grad, expand_grad, bias_in_grad, shrink_grad, bias_out_grad,
    ) = results[2:]
    totals = (
        first[3], first[4], first[1], first[2], gain_two_grad, shift_two_grad, project_two_grad,
        merge_two_grad, gain_three_grad, shift_three_grad, expand_grad, bias_in_grad,
        shrink_grad, bias_out_grad,
    )
    totals = [part[0] if part.shape[0] == 1 else part for part in totals]
    totals = tuple(part.astype(BF16) for part in totals)
    totals = lax.psum_scatter(totals, "feat", scatter_dimension=0, tiled=True)
    totals = lax.psum(totals, "task")
    return (
        layer_out.reshape(tokens.shape),
        first[0].reshape(tokens.shape),
    ) + tuple(part.astype(F32) for part in totals)


FUSED_LIMIT = 62 * 1024 * 1024

MESH = pl.DeviceIdType.MESH
DEPTH, WIDE_Y, CORES, HALVES = 4, 2, 2, 2
SPLIT = CORES * HALVES
VECTORS = 16
FINISH_LIMIT = 56 * 1024 * 1024
BUFFERS = ("halves", "quarters", "lines", "outer", "crossed", "paired", "final", "twin")


def remote(source, target, sent, arrived, device):
    return pltpu.make_async_remote_copy(
        src_ref=source, dst_ref=target, send_sem=sent, recv_sem=arrived,
        device_id=device, device_id_type=MESH,
    )


class Place:
    def __init__(self):
        self.feat = lax.axis_index("feat")
        self.task = lax.axis_index("task")
        self.z = lax.div(self.feat, WIDE_Y)
        self.y = lax.rem(self.feat, WIDE_Y)
        self.x = lax.div(self.task, CORES)
        self.c = lax.rem(self.task, CORES)
        self.mine = HALVES * self.c + self.x
        self.theirs = HALVES * self.c + 1 - self.x
        self.below = HALVES * self.c
        self.other = HALVES * (1 - self.c)
        self.along_y = (self.task, WIDE_Y * self.z + 1 - self.y)
        self.along_x = (CORES * (1 - self.x) + self.c, self.feat)
        self.sibling = (CORES * self.x + 1 - self.c, self.feat)
        self.across = DEPTH - 1 - self.z
        self.near_low = 2 * lax.div(self.z, 2)
        self.far_low = 2 - self.near_low
        self.pair = 2 * self.near_low + 1 - self.z
        self.inner = jnp.logical_or(self.z == 1, self.z == 2)

    def along_z(self, shift):
        return lax.rem(self.z + shift, DEPTH)

    def at_z(self, z):
        return (self.task, WIDE_Y * z + self.y)

    def peer(self, shift, groups):
        return lax.rem(self.feat + shift, groups)


class Moves:
    def __init__(self, place, index, wide, sent, arrived, stages):
        self.place, self.wide = place, wide
        self.rows = pl.ds(place.below, HALVES) if wide else pl.ds(place.mine, 1)
        self.sent = [sent.at[index, stage] for stage in range(stages)]
        self.arrived = [arrived.at[index, stage] for stage in range(stages)]

    def move(self, stage, source, target, device):
        return remote(source, target, self.sent[stage], self.arrived[stage], device)


class Gather(Moves):
    def __init__(self, place, index, shard, weight, sent, arrived, local, wide=False, direct=False):
        super().__init__(place, index, wide, sent, arrived, 6)
        self.shard, self.weight, self.local, self.direct = shard, weight, local.at[index], direct

    def _own(self):
        p = self.place
        return pltpu.make_async_copy(
            self.shard.at[self.rows], self.weight.at[p.z, p.y, self.rows], self.local
        )

    def _pair(self, z_count):
        p = self.place
        part = self.weight.at[pl.ds(0, z_count), p.y, self.rows]
        return self.move(0, part, part, p.at_z(p.pair))

    def _far(self, stage, low, device):
        part = self.weight.at[pl.ds(low, 2), self.place.y, self.rows]
        return self.move(stage, part, part, device)

    def _along_y(self):
        p = self.place
        part = self.weight.at[:, p.y, self.rows]
        return self.move(3, part, part, p.along_y)

    def _along_x(self):
        p = self.place
        part = self.weight.at[:, :, self.rows]
        return self.move(4, part, part, p.along_x)

    def _across(self):
        p = self.place
        part = self.weight.at[:, :, pl.ds(p.below, HALVES)]
        return self.move(5, part, part, p.sibling)

    def start(self):
        p = self.place
        self._own().start()
        targets = [p.along_z(shift) for shift in range(1, DEPTH)] if self.direct else [p.pair]
        for z in targets:
            self.move(
                0, self.shard.at[self.rows], self.weight.at[p.z, p.y, self.rows], p.at_z(z)
            ).start()

    def middle(self):
        if self.direct:
            return
        p = self.place

        @pl.when(p.inner)
        def _():
            self._own().wait()
            self._pair(1).wait_recv()
            self._far(1, p.near_low, p.at_z(p.across)).start()

    def outward(self):
        if self.direct:
            return
        p = self.place

        @pl.when(p.inner)
        def _():
            self._far(1, p.far_low, p.at_z(p.across)).wait_recv()
            self._far(2, p.far_low, p.at_z(p.pair)).start()

    def along_y(self):
        p = self.place
        if self.direct:
            self._own().wait()
            self._pair(DEPTH - 1).wait_recv()
        else:
            @pl.when(jnp.logical_not(p.inner))
            def _():
                self._own().wait()
                self._pair(1).wait_recv()
                self._far(2, p.far_low, p.at_z(p.pair)).wait_recv()

        self._along_y().start()

    def along_x(self):
        if not self.wide:
            self._along_y().wait_recv()
            self._along_x().start()

    def core(self):
        if self.wide:
            self._along_y().wait_recv()
        else:
            self._along_x().wait_recv()
        self._across().start()

    def done(self):
        self._across().wait_recv()

    def finish(self):
        p = self.place
        if self.direct:
            self._pair(DEPTH - 1).wait_send()
        else:
            self._pair(1).wait_send()

            @pl.when(p.inner)
            def _():
                self._far(1, p.near_low, p.at_z(p.across)).wait_send()
                self._far(2, p.far_low, p.at_z(p.pair)).wait_send()

        self._along_y().wait_send()
        if not self.wide:
            self._along_x().wait_send()
        self._across().wait_send()


class Reduce(Moves):
    def __init__(
        self, place, index, total, staged, memory, sent, arrived, wide=False, direct=False
    ):
        super().__init__(place, index, wide, sent, arrived, 8)
        self.total, self.staged, self.direct = total, staged, direct
        (
            self.halves, self.quarters, self.lines, self.outer, self.crossed, self.paired,
            self.final, self.twin,
        ) = memory

    def _core(self):
        p = self.place
        return self.move(
            0, self.staged.at[:, :, pl.ds(p.other, HALVES)], self.halves, p.sibling
        )

    def _x(self):
        p = self.place
        return self.move(1, self.staged.at[:, :, pl.ds(p.theirs, 1)], self.quarters, p.along_x)

    def _y(self):
        p = self.place
        return self.move(2, self.staged.at[:, 1 - p.y, self.rows], self.lines, p.along_y)

    def _inward(self):
        p = self.place
        if self.direct:
            return self.move(3, self.outer, self.outer, p.at_z(p.pair))
        return self.move(
            3, self.staged.at[pl.ds(p.far_low, 2), p.y, self.rows], self.outer, p.at_z(p.pair)
        )

    def _over(self):
        p = self.place
        return self.move(
            4, self.staged.at[pl.ds(p.far_low, 2), p.y, self.rows], self.crossed, p.at_z(p.across)
        )

    def _pair(self):
        p = self.place
        return self.move(5, self.staged.at[p.pair, p.y, self.rows], self.paired, p.at_z(p.pair))

    def _twin(self):
        p = self.place
        part = self.final.at[self.rows]
        return self.move(6, part, self.twin if self.wide else part, p.along_x)

    def _across(self):
        p = self.place
        part = self.final.at[pl.ds(p.below, HALVES)]
        return self.move(7, part, part, p.sibling)

    def core(self):
        p = self.place

        def one(z, carry):
            cut = pl.ds(p.other, HALVES)
            self.staged[z, :, cut] = self.total[z, :, cut].astype(BF16)
            return carry

        lax.fori_loop(0, DEPTH, one, 0)
        self._core().start()

    def x(self):
        p = self.place
        if self.wide:
            return
        self._core().wait_recv()

        def one(z, carry):
            summed = self.total[z, :, p.theirs] + self.halves[z, :, 1 - p.x].astype(F32)
            self.staged[z, :, p.theirs] = summed.astype(BF16)
            return carry

        lax.fori_loop(0, DEPTH, one, 0)
        self._x().start()

    def y(self):
        p = self.place
        if self.wide:
            self._core().wait_recv()
        else:
            self._x().wait_recv()

        def one(z, carry):
            if self.wide:
                summed = self.total[z, :, self.rows] + self.halves[z].astype(F32)
            else:
                summed = self.total[z, :, self.rows] + self.halves[z, :, pl.ds(p.x, 1)].astype(F32)
                summed = summed + self.quarters[z].astype(F32)
            self.staged[z, :, self.rows] = summed.astype(BF16)
            return carry

        lax.fori_loop(0, DEPTH, one, 0)
        self._y().start()

    def inward(self):
        p = self.place
        self._y().wait_recv()

        def one(z, carry):
            summed = self.staged[z, p.y, self.rows].astype(F32) + self.lines[z].astype(F32)
            self.staged[z, p.y, self.rows] = summed.astype(BF16)
            return carry

        lax.fori_loop(0, DEPTH, one, 0)
        if self.direct:
            for shift in range(1, DEPTH):
                z = p.along_z(shift)
                self.move(
                    3, self.staged.at[z, p.y, self.rows], self.outer.at[shift - 1], p.at_z(z)
                ).start()
            return

        @pl.when(jnp.logical_not(p.inner))
        def _():
            self._inward().start()

    def over(self):
        p = self.place

        @pl.when(p.inner)
        def _():
            self._inward().wait_recv()
            for at in range(2):
                z = p.far_low + at
                summed = self.staged[z, p.y, self.rows].astype(F32) + self.outer[at].astype(F32)
                self.staged[z, p.y, self.rows] = summed.astype(BF16)
            self._over().start()

    def pair(self):
        p = self.place

        @pl.when(p.inner)
        def _():
            self._over().wait_recv()
            for at in range(2):
                z = p.near_low + at
                summed = self.staged[z, p.y, self.rows].astype(F32) + self.crossed[at].astype(F32)
                self.staged[z, p.y, self.rows] = summed.astype(BF16)

        self._pair().start()

    def twins(self):
        p = self.place
        summed = self.staged[p.z, p.y, self.rows].astype(F32)
        if self.direct:
            self._inward().wait_recv()
            for shift in range(DEPTH - 1):
                summed = summed + self.outer[shift].astype(F32)
        else:
            self._pair().wait_recv()
            summed = summed + self.paired[...].astype(F32)
        self.final[self.rows] = summed.astype(BF16)
        self._twin().start()

    def share(self):
        self._twin().wait_recv()
        if self.wide:
            self._twin().wait_send()
            summed = self.final[self.rows].astype(F32) + self.twin[...].astype(F32)
            self.final[self.rows] = summed.astype(BF16)
        self._across().start()

    def done(self):
        self._across().wait_recv()

    def finish(self):
        p = self.place
        self._core().wait_send()
        if not self.wide:
            self._x().wait_send()
            self._twin().wait_send()
        self._y().wait_send()
        self._across().wait_send()
        if self.direct:
            self._inward().wait_send()
            return

        @pl.when(p.inner)
        def _():
            self._over().wait_send()

        @pl.when(jnp.logical_not(p.inner))
        def _():
            self._inward().wait_send()

        self._pair().wait_send()


(
    START, ZERO, PARAMS, NORM0, NORM1, UNTIL_QUERY, UNTIL_KEY, UNTIL_VALUE, PROJQ, PROJK,
    PROJV, PROJ1, PAIR00, PAIR01, PAIR02, PAIR03, MERGE0, PAIR10, PAIR11, PAIR12, PAIR13,
    MERGE1, DENSE, UNTIL_SHRINK, DENSE_GRADS, FEATURE_GRADS, LAYER_END, MERGED0, BACK00,
    BACK01, BACK02, BACK03, MERGE_GRADS, MERGED1, BACK10, BACK11, BACK12, BACK13, LOW_GRADS,
    HIGH_GRADS, FIRST0, FIRST1, FIRST2, FIRST3, END,
) = range(45)
NORM_POINTS = (NORM0, NORM1)
PROJECT_POINTS = (PROJQ, PROJK, PROJV)
UNTIL_POINTS = (UNTIL_QUERY, UNTIL_KEY, UNTIL_VALUE)
MERGE_POINTS = (MERGE0, MERGE1)
MERGED_POINTS = (MERGED0, MERGED1)
PAIR_POINTS = ((PAIR00, PAIR01, PAIR02, PAIR03), (PAIR10, PAIR11, PAIR12, PAIR13))
BACK_POINTS = ((BACK00, BACK01, BACK02, BACK03), (BACK10, BACK11, BACK12, BACK13))
FIRST_POINTS = (FIRST0, FIRST1, FIRST2, FIRST3)
QUERY, KEY, VALUE, MERGE_ONE, MERGE_TWO, PROJECT_TWO = range(6)
EXPAND_LOW, EXPAND_HIGH, SHRINK_LOW, SHRINK_HIGH = range(6, 10)
D_SHRINK_LOW, D_SHRINK_HIGH, D_EXPAND_LOW, D_EXPAND_HIGH = range(10, 14)
D_PROJECT_TWO, D_MERGE_TWO, D_MERGE_ONE, D_PROJECT_LOW, D_PROJECT_HIGH = range(14, 19)
SCHEDULE = {
    START: (
        (QUERY, Gather.start),
        (KEY, Gather.start),
        (VALUE, Gather.start),
        (MERGE_ONE, Gather.start),
        (MERGE_TWO, Gather.start),
        (PROJECT_TWO, Gather.start),
        (EXPAND_LOW, Gather.start),
        (EXPAND_HIGH, Gather.start),
        (SHRINK_LOW, Gather.start),
        (SHRINK_HIGH, Gather.start),
    ),
    NORM1: (
        (QUERY, Gather.along_y),
    ),
    UNTIL_QUERY: (
        (KEY, Gather.along_y),
        (VALUE, Gather.along_y),
        (MERGE_TWO, Gather.middle),
        (QUERY, Gather.along_x),
        (PROJECT_TWO, Gather.middle),
        (MERGE_ONE, Gather.along_y),
        (KEY, Gather.along_x),
        (EXPAND_LOW, Gather.middle),
        (EXPAND_HIGH, Gather.middle),
        (MERGE_TWO, Gather.outward),
        (SHRINK_LOW, Gather.middle),
        (VALUE, Gather.core),
        (QUERY, Gather.core),
        (PROJECT_TWO, Gather.outward),
        (SHRINK_HIGH, Gather.middle),
        (MERGE_TWO, Gather.along_y),
        (MERGE_ONE, Gather.along_x),
        (EXPAND_LOW, Gather.outward),
    ),
    UNTIL_KEY: (
        (KEY, Gather.core),
        (EXPAND_HIGH, Gather.outward),
        (PROJECT_TWO, Gather.along_y),
    ),
    PROJK: (
        (MERGE_TWO, Gather.along_x),
    ),
    PAIR00: (
        (MERGE_ONE, Gather.core),
        (EXPAND_LOW, Gather.along_y),
        (SHRINK_LOW, Gather.outward),
        (EXPAND_HIGH, Gather.along_y),
    ),
    PAIR01: (
        (SHRINK_HIGH, Gather.outward),
    ),
    PAIR02: (
        (MERGE_TWO, Gather.core),
        (PROJECT_TWO, Gather.along_x),
    ),
    PAIR03: (
        (SHRINK_LOW, Gather.along_y),
    ),
    MERGE0: (
        (EXPAND_LOW, Gather.along_x),
    ),
    PROJ1: (
        (SHRINK_HIGH, Gather.along_y),
    ),
    PAIR10: (
        (EXPAND_HIGH, Gather.along_x),
    ),
    PAIR13: (
        (PROJECT_TWO, Gather.core),
    ),
    DENSE: (
        (EXPAND_LOW, Gather.core),
        (EXPAND_HIGH, Gather.core),
        (SHRINK_LOW, Gather.core),
    ),
    UNTIL_SHRINK: (
        (SHRINK_HIGH, Gather.core),
    ),
    DENSE_GRADS: (
        (D_EXPAND_LOW, Reduce.core),
        (D_SHRINK_LOW, Reduce.core),
        (D_SHRINK_HIGH, Reduce.core),
        (D_EXPAND_HIGH, Reduce.core),
    ),
    FEATURE_GRADS: (
        (D_EXPAND_LOW, Reduce.x),
        (D_SHRINK_LOW, Reduce.y),
        (D_SHRINK_HIGH, Reduce.y),
    ),
    LAYER_END: (
        (D_PROJECT_TWO, Reduce.core),
        (D_MERGE_TWO, Reduce.core),
        (D_EXPAND_HIGH, Reduce.x),
    ),
    BACK00: (
        (D_EXPAND_LOW, Reduce.y),
        (D_SHRINK_LOW, Reduce.inward),
        (D_PROJECT_TWO, Reduce.x),
        (D_MERGE_TWO, Reduce.x),
    ),
    BACK02: (
        (D_SHRINK_HIGH, Reduce.inward),
        (D_EXPAND_HIGH, Reduce.y),
    ),
    BACK03: (
        (D_SHRINK_LOW, Reduce.over),
    ),
    MERGE_GRADS: (
        (D_MERGE_ONE, Reduce.core),
    ),
    BACK10: (
        (D_EXPAND_LOW, Reduce.inward),
        (D_PROJECT_TWO, Reduce.y),
        (D_SHRINK_HIGH, Reduce.over),
        (D_MERGE_ONE, Reduce.y),
    ),
    BACK11: (
        (D_SHRINK_LOW, Reduce.pair),
        (D_EXPAND_HIGH, Reduce.inward),
        (D_MERGE_TWO, Reduce.y),
    ),
    LOW_GRADS: (
        (D_PROJECT_LOW, Reduce.core),
        (D_EXPAND_LOW, Reduce.over),
    ),
    BACK12: (
        (D_SHRINK_LOW, Reduce.twins),
        (D_PROJECT_TWO, Reduce.inward),
        (D_SHRINK_HIGH, Reduce.pair),
        (D_PROJECT_LOW, Reduce.y),
    ),
    BACK13: (
        (D_EXPAND_LOW, Reduce.pair),
        (D_EXPAND_HIGH, Reduce.over),
        (D_MERGE_TWO, Reduce.inward),
        (D_MERGE_ONE, Reduce.inward),
    ),
    HIGH_GRADS: (
        (D_PROJECT_HIGH, Reduce.core),
        (D_SHRINK_LOW, Reduce.share),
        (D_PROJECT_TWO, Reduce.over),
    ),
    FIRST0: (
        (D_SHRINK_HIGH, Reduce.twins),
    ),
    FIRST1: (
        (D_PROJECT_HIGH, Reduce.y),
        (D_EXPAND_LOW, Reduce.twins),
        (D_EXPAND_HIGH, Reduce.pair),
        (D_MERGE_TWO, Reduce.over),
        (D_PROJECT_LOW, Reduce.inward),
    ),
    FIRST2: (
        (D_MERGE_ONE, Reduce.twins),
    ),
    FIRST3: (
        (D_EXPAND_LOW, Reduce.share),
        (D_SHRINK_HIGH, Reduce.share),
        (D_EXPAND_HIGH, Reduce.twins),
    ),
    END: (
        (D_PROJECT_TWO, Reduce.pair),
        (D_MERGE_TWO, Reduce.pair),
        (D_MERGE_ONE, Reduce.share),
        (D_PROJECT_HIGH, Reduce.inward),
        (D_EXPAND_HIGH, Reduce.share),
        (D_PROJECT_TWO, Reduce.twins),
        (D_MERGE_TWO, Reduce.twins),
        (D_PROJECT_LOW, Reduce.twins),
        (D_PROJECT_TWO, Reduce.share),
        (D_MERGE_TWO, Reduce.share),
        (D_PROJECT_LOW, Reduce.share),
        (D_PROJECT_HIGH, Reduce.twins),
        (D_PROJECT_HIGH, Reduce.share),
    ),
}


def flat(ref):
    return ref[...].reshape(-1, ref.shape[-1])


def fused_kernel(names, *refs):
    r = types.SimpleNamespace(**dict(zip(names, refs)))
    p = Place()
    tasks, samples, width = r.tokens.shape
    groups = r.hidden_in.shape[0]
    members = r.task_slots.shape[0]
    block_rows = samples // groups
    hidden_units = r.w_expand.shape[-1]
    chunk = 256
    head_scale = (width // HEADS) ** (-0.5)
    pairs = width // PAIR
    parts = samples // PAIR

    entry = pltpu.get_barrier_semaphore()
    for shift in range(1, groups):
        pl.semaphore_signal(
            entry, inc=1, device_id=(p.task, p.peer(shift, groups)), device_id_type=MESH
        )
    for shift in range(1, members):
        pl.semaphore_signal(
            entry, inc=1, device_id=(lax.rem(p.task + shift, members), p.feat),
            device_id_type=MESH,
        )
    pl.semaphore_wait(entry, groups + members - 2)

    third = width
    gathers = []

    def gather(name, rows=None, columns=None, wide=False, direct=False):
        shard, weight = getattr(r, "s_" + name), getattr(r, "w_" + name)
        if rows is not None:
            shard, weight = shard.at[:, pl.ds(*rows), :], weight.at[:, :, :, pl.ds(*rows), :]
        if columns is not None:
            shard = shard.at[:, :, pl.ds(*columns)]
            weight = weight.at[:, :, :, :, pl.ds(*columns)]
        item = Gather(
            p, len(gathers), shard, weight, r.gather_sent, r.gather_arrived, r.gather_local,
            wide, direct,
        )
        gathers.append(item)
        return item

    deep = r.w_shrink.shape[3] // 2
    half_units = hidden_units // 2
    items = {
        QUERY: gather("project_one", columns=(0, third), direct=True),
        KEY: gather("project_one", columns=(third, third), direct=True),
        VALUE: gather("project_one", columns=(2 * third, third), wide=True, direct=True),
        MERGE_ONE: gather("merge_one", direct=True),
        PROJECT_TWO: gather("project_two"),
        MERGE_TWO: gather("merge_two"),
        EXPAND_LOW: gather("expand", columns=(0, half_units)),
        EXPAND_HIGH: gather("expand", columns=(half_units, half_units)),
        SHRINK_LOW: gather("shrink", rows=(0, deep), wide=True),
        SHRINK_HIGH: gather("shrink", rows=(deep, deep), wide=True),
    }
    dense_items = (EXPAND_LOW, SHRINK_LOW, SHRINK_HIGH, EXPAND_HIGH)

    def run(point):
        for name, stage in SCHEDULE.get(point, ()):
            stage(items[name])

    def vectors_in():
        most = r.vector_slots.at[pl.ds(0, groups - 1)]
        return remote(most, most, r.vector_sent.at[0], r.vector_arrived.at[0], p.along_y)

    own_vectors = pltpu.make_async_copy(
        r.vectors, r.vector_slots.at[p.feat], r.vector_local.at[0]
    )
    own_vectors.start()
    for shift in range(1, groups):
        remote(
            r.vectors, r.vector_slots.at[p.feat], r.vector_sent.at[0], r.vector_arrived.at[0],
            (p.task, p.peer(shift, groups)),
        ).start()
    run(START)

    def spread(source, target, task, sent, arrived, local):
        def own():
            return pltpu.make_async_copy(
                source.at[task, pl.ds(p.feat * block_rows, block_rows)],
                target.at[p.feat, task], local.at[task],
            )

        def all_of():
            most = target.at[pl.ds(0, groups - 1), task]
            return remote(most, most, sent.at[task], arrived.at[task], p.along_y)

        def start():
            own().start()
            for shift in range(1, groups):
                peer = p.peer(shift, groups)
                remote(
                    source.at[task, pl.ds(peer * block_rows, block_rows)],
                    target.at[p.feat, task], sent.at[task], arrived.at[task], (p.task, peer),
                ).start()

        def wait():
            own().wait()
            all_of().wait_recv()

        def finish():
            all_of().wait_send()

        return types.SimpleNamespace(start=start, wait=wait, finish=finish)

    upstream = [
        spread(
            r.upstream, r.upstream_in, task, r.upstream_sent, r.upstream_arrived,
            r.upstream_local,
        )
        for task in range(tasks)
    ]
    hidden = [
        spread(
            r.grad_mixed, r.hidden_in, task, r.hidden_sent, r.hidden_arrived, r.hidden_local
        )
        for task in range(tasks)
    ]

    for ref in (r.t_project_two, r.t_merge_two, r.t_expand, r.t_shrink, r.vector_sums):
        ref[...] = jnp.zeros_like(ref)
    run(ZERO)
    own_vectors.wait()
    vectors_in().wait_recv()
    lane = lax.broadcasted_iota(jnp.int32, (1, PAIR), 1)
    per_slot = r.vector_slots.shape[1:]
    turned = [pltpu.roll(r.vector_slots[index], PAIR // 2, 1) for index in range(groups)]
    whole = [r.vector_slots[index] for index in range(groups)]
    bias_tiles = hidden_units // groups // PAIR
    for row in range(7):
        tile = bias_tiles + row // 2
        for at in range(groups // 2):
            first = (turned if row % 2 else whole)[2 * at][tile : tile + 1]
            second = (whole if row % 2 else turned)[2 * at + 1][tile : tile + 1]
            r.params[pl.ds(row, 1), pl.ds(at * PAIR, PAIR)] = jnp.where(
                lane < PAIR // 2, first, second
            )
    for at in range(groups * bias_tiles):
        row, tile = divmod(at, width // PAIR)
        r.params[pl.ds(7 + row, 1), pl.ds(tile * PAIR, PAIR)] = whole[at // bias_tiles][
            at % bias_tiles : at % bias_tiles + 1
        ]
    run(PARAMS)

    def param(row):
        return r.params[pl.ds(row, 1), :]

    def add_vector(row, value):
        r.vector_sums[pl.ds(row, 1), :] += jnp.sum(value, axis=0, keepdims=True)

    def norm_one(task):
        for start in range(0, samples, chunk):
            rows = r.tokens[task, pl.ds(start, chunk), :].astype(F32)
            normed = normalise(rows)[0] * param(0) + param(1)
            r.normed_one[task, pl.ds(start, chunk), :] = normed.astype(BF16)

    for task in range(tasks):
        norm_one(task)
        run(NORM_POINTS[task])

    def key_bias(task):
        keys = lax.broadcasted_iota(jnp.int32, (samples, 1), 0)
        return jnp.where(keys < r.counts[task], 0.0, MASKED)

    def live_rows(task, start):
        at = lax.broadcasted_iota(jnp.int32, (chunk, 1), 0) + start
        return jnp.where(at < r.counts[task], 1.0, 0.0)

    def at_pair(pair, points):
        for at, point in enumerate(points):
            if point in SCHEDULE:
                pl.when(pair == at)(functools.partial(run, point))

    def attend_pairs(task, points):
        bias = key_bias(task)

        def one_pair(pair, carry):
            lanes = pl.multiple_of(pair * PAIR, PAIR)
            key = r.triple[task, :, pl.ds(lanes + width, PAIR)]
            value_turned = r.triple[task, :, pl.ds(lanes + 2 * width, PAIR)].T
            for at in range(parts):
                query = r.triple[task, pl.ds(at * PAIR, PAIR), pl.ds(lanes, PAIR)]
                mixed, log_total = attend(query, key, value_turned, bias, head_scale)
                r.mixed_one[task, pl.ds(at * PAIR, PAIR), pl.ds(lanes, PAIR)] = mixed.astype(BF16)
                r.logs_one[pl.ds((task * pairs + pair) * parts + at, 1), :] = log_total
            at_pair(pair, points)
            if task == 0:
                pl.when(pair == 1)(upstream[0].start)
            return carry

        lax.fori_loop(0, pairs, one_pair, 0)

    def project(task, part):
        weight = r.w_project_one[:, :, :, :, pl.ds(part * width, width)].reshape(width, width)
        for start in range(0, samples, chunk):
            normed = r.normed_one[task, pl.ds(start, chunk), :]
            r.triple[task, pl.ds(start, chunk), pl.ds(part * width, width)] = nn(
                normed, weight
            ).astype(BF16)

    for name, part in ((QUERY, 0), (KEY, 1), (VALUE, 2)):
        run(UNTIL_POINTS[part])
        items[name].done()
        project(0, part)
        run(PROJECT_POINTS[part])
    for task in range(tasks):
        if task > 0:
            for part in range(3):
                project(task, part)
            run(PROJ1)
        attend_pairs(task, PAIR_POINTS[task])
        if task == 0:
            items[MERGE_ONE].done()
        for start in range(0, samples, chunk):
            rows = r.tokens[task, pl.ds(start, chunk), :].astype(F32)
            merged = nn(r.mixed_one[task, pl.ds(start, chunk), :], flat(r.w_merge_one))
            summed = rows + live_rows(task, start) * merged
            r.grad_mixed[task, pl.ds(start, chunk), :] = summed.astype(BF16)
        hidden[task].start()
        if task > 0:
            upstream[task].start()
        run(MERGE_POINTS[task])

    size = groups * GROUP
    blocks = chunk // size
    piece = blocks * GROUP
    per_task = block_rows // piece

    def own_piece(source, target, task, start, semaphore):
        return pltpu.make_async_copy(
            source.at[p.feat, task, pl.ds(start, piece)],
            target.at[task, pl.ds(p.feat * block_rows + start, piece)], semaphore,
        )

    def send_back(source, target, task, start, sent, arrived, local):
        own_piece(source, target, task, start, local).start()
        for shift in range(1, groups):
            peer = p.peer(shift, groups)
            remote(
                source.at[peer, task, pl.ds(start, piece)],
                target.at[task, pl.ds(p.feat * block_rows + start, piece)],
                sent, arrived, (p.task, peer),
            ).start()

    reductions = []

    def reduction(total, staged, wide=False, direct=False):
        index = len(reductions)
        item = Reduce(
            p, index, total, staged,
            [getattr(r, "m%d_%s" % (index, kind), None) for kind in BUFFERS],
            r.reduce_sent, r.reduce_arrived, wide, direct,
        )
        reductions.append(item)
        return item

    def part_of(ref, rows=None, columns=None):
        if rows is not None:
            return ref.at[:, :, :, pl.ds(*rows), :]
        return ref.at[:, :, :, :, pl.ds(*columns)]

    def half_of(name, at, wide):
        total, staged = getattr(r, "t_" + name), getattr(r, "w_" + name)
        if name == "shrink":
            cut = (at * deep, deep)
            return reduction(part_of(total, cut), part_of(staged, cut), wide)
        cut = (at * half_units, half_units)
        return reduction(part_of(total, None, cut), part_of(staged, None, cut), wide)

    items[D_SHRINK_LOW] = half_of("shrink", 0, True)
    items[D_SHRINK_HIGH] = half_of("shrink", 1, True)
    items[D_EXPAND_LOW] = half_of("expand", 0, False)
    items[D_EXPAND_HIGH] = half_of("expand", 1, False)
    items[D_PROJECT_TWO] = reduction(r.t_project_two, r.w_project_two)
    items[D_MERGE_TWO] = reduction(r.t_merge_two, r.w_merge_two)
    items[D_MERGE_ONE] = reduction(r.t_merge_one, r.w_merge_one, True, True)
    items[D_PROJECT_LOW] = reduction(r.t_low, r.b_low, True, True)
    items[D_PROJECT_HIGH] = reduction(r.t_high, r.b_high, True, True)

    def layer_chunk(step, carry):
        task = lax.div(step, per_task)
        begin = pl.multiple_of(lax.rem(step, per_task) * piece, piece)

        first = step == 0
        final = step == tasks * per_task - 1

        @pl.when(first)
        def _():
            hidden[0].wait()
            items[PROJECT_TWO].done()

        for later in range(1, tasks):
            @pl.when(step == later * per_task)
            def _():
                upstream[later].wait()
                hidden[later].wait()

        def load(ref):
            pieces = [
                ref[:, task, pl.ds(begin + block * GROUP, GROUP), :].reshape(size, width)
                for block in range(blocks)
            ]
            return pieces[0] if blocks == 1 else jnp.concatenate(pieces, axis=0)

        def store(ref, values):
            for block in range(blocks):
                part = values[block * size : (block + 1) * size].reshape(groups, GROUP, width)
                ref[:, task, pl.ds(begin + block * GROUP, GROUP), :] = part

        row = lax.broadcasted_iota(jnp.int32, (chunk, 1), 0)
        row = (row // size) * GROUP + row % GROUP + begin + p.feat * block_rows
        live = jnp.where(row < r.counts[task], 1.0, 0.0)

        hidden_one = load(r.hidden_in).astype(F32)
        unit_two, scale_two = normalise(hidden_one)
        normed_two = (unit_two * param(2) + param(3)).astype(BF16)
        r.part_triple[...] = nn(normed_two, flat(r.w_project_two)).astype(BF16)
        reach = min(PAIR, size)
        key_at = lax.broadcasted_iota(jnp.int32, (size, 2 * reach), 0) % GROUP
        query_at = lax.broadcasted_iota(jnp.int32, (size, 2 * reach), 1) % GROUP
        bias = jnp.where(key_at == query_at, 0.0, MASKED)
        for block in range(blocks):
            where = pl.ds(block * size, size)
            for pair in range(pairs):
                lanes = pair * PAIR
                key = r.part_triple[where, pl.ds(width + lanes, PAIR)]
                value_turned = r.part_triple[where, pl.ds(2 * width + lanes, PAIR)].T
                query = r.part_triple[where, pl.ds(lanes, PAIR)]
                result, log_total = attend(query, key, value_turned, bias, head_scale)
                r.block_mixed[where, pl.ds(lanes, PAIR)] = result.astype(BF16)
                r.block_logs[pl.ds(block * pairs + pair, 1), :] = log_total

        @pl.when(first)
        def _():
            items[MERGE_TWO].done()

        hidden_two = hidden_one + live * nn(r.block_mixed[...], flat(r.w_merge_two))
        unit_three, scale_three = normalise(hidden_two)
        normed_three = (unit_three * param(4) + param(5)).astype(BF16)
        @pl.when(first)
        def _():
            run(DENSE)
            upstream[0].wait()

        flow = load(r.upstream_in).astype(F32)
        grad_dense = (flow * live).astype(BF16)
        add_vector(6, grad_dense.astype(F32))

        @pl.when(first)
        def _():
            items[EXPAND_LOW].done()
            items[SHRINK_LOW].done()
            run(UNTIL_SHRINK)
            items[SHRINK_HIGH].done()

        dense = None
        incoming = None
        lanes = hidden_units // DEPTH
        for turn in range(DEPTH):
            cut = pl.ds(turn * lanes, lanes)
            if turn == DEPTH // 2:
                @pl.when(first)
                def _():
                    items[EXPAND_HIGH].done()

            up_weight = r.w_expand[:, :, :, :, cut].reshape(width, lanes)
            down_weight = r.w_shrink[turn].reshape(lanes, width)
            expanded = nn(normed_three, up_weight) + param(7 + turn)
            square = expanded * expanded
            steep = 0.7978845608028654
            bend = jnp.tanh(expanded * (steep + (steep * 0.044715) * square))
            half_up = 0.5 + 0.5 * bend
            activated = (expanded * half_up).astype(BF16)
            slope = half_up + (0.5 * expanded) * (1.0 - bend * bend) * (
                steep + (3.0 * steep * 0.044715) * square
            )
            grad_expanded = (slope * nt(grad_dense, down_weight)).astype(BF16)
            add_vector(7 + turn, grad_expanded.astype(F32))
            r.t_shrink[turn] += tn(activated, grad_dense).reshape(r.t_shrink.shape[1:])
            r.t_expand[:, :, :, :, cut] += tn(normed_three, grad_expanded).reshape(
                r.t_expand.shape[:4] + (lanes,)
            )
            up = nn(activated, down_weight)
            down = nt(grad_expanded, up_weight)
            dense = up if dense is None else dense + up
            incoming = down if incoming is None else incoming + down
        @pl.when(final)
        def _():
            for name in dense_items:
                items[name].finish()
            run(DENSE_GRADS)

        result = hidden_two + live * (dense + param(6))
        store(r.upstream_in, result.astype(BF16))

        add_vector(4, incoming * unit_three)
        add_vector(5, incoming)
        flow = flow + normalise_back(incoming, unit_three, scale_three, param(4))
        branch = (flow * live).astype(BF16)
        r.t_merge_two[...] += tn(r.block_mixed[...], branch).reshape(r.t_merge_two.shape)
        r.block_grad[...] = nt(branch, flat(r.w_merge_two)).astype(BF16)

        @pl.when(final)
        def _():
            run(FEATURE_GRADS)

        for block in range(blocks):
            where = pl.ds(block * size, size)
            for pair in range(pairs):
                lanes = pair * PAIR
                key = r.part_triple[where, pl.ds(width + lanes, PAIR)]
                value = r.part_triple[where, pl.ds(2 * width + lanes, PAIR)]
                query = r.part_triple[where, pl.ds(lanes, PAIR)]
                grad_query, grad_key, grad_value = attend_back(
                    query, key, value, key.T, r.block_mixed[where, pl.ds(lanes, PAIR)],
                    r.block_grad[where, pl.ds(lanes, PAIR)], r.block_logs[pl.ds(block * pairs + pair, 1), :], bias, head_scale,
                )
                r.part_triple[where, pl.ds(lanes, PAIR)] = grad_query.astype(BF16)
                r.part_triple[where, pl.ds(width + lanes, PAIR)] = grad_key.astype(BF16)
                r.part_triple[where, pl.ds(2 * width + lanes, PAIR)] = grad_value.astype(BF16)
        grad_triple = r.part_triple[...]
        r.t_project_two[...] += tn(normed_two, grad_triple).reshape(r.t_project_two.shape)
        incoming = nt(grad_triple, flat(r.w_project_two))
        add_vector(2, incoming * unit_two)
        add_vector(3, incoming)
        flow = flow + normalise_back(incoming, unit_two, scale_two, param(2))
        store(r.hidden_in, flow.astype(BF16))
        send_back(
            r.hidden_in, r.flow, task, begin,
            r.flow_sent.at[0], r.flow_arrived.at[task], r.flow_local.at[task],
        )
        send_back(
            r.upstream_in, r.layer_out, task, begin,
            r.out_sent.at[0], r.out_arrived.at[0], r.out_local.at[0],
        )
        return carry

    lax.fori_loop(0, tasks * per_task, layer_chunk, 0)

    for name in (QUERY, KEY, VALUE, MERGE_ONE, PROJECT_TWO, MERGE_TWO):
        items[name].finish()
    for task in range(tasks):
        hidden[task].finish()
    run(LAYER_END)

    def flow_in(task):
        most = r.flow.at[task, pl.ds(0, samples - block_rows)]
        return remote(most, most, r.flow_sent.at[0], r.flow_arrived.at[task], p.along_y)

    def wait_flow(task):
        flow_in(task).wait_recv()
        own = r.flow.at[task, pl.ds(0, block_rows)]
        pltpu.make_async_copy(own, own, r.flow_local.at[task]).wait()

    def merge_back(task):
        for start in range(0, samples, chunk):
            live = live_rows(task, start)
            branch = (r.flow[task, pl.ds(start, chunk), :].astype(F32) * live).astype(BF16)
            part = tn(r.mixed_one[task, pl.ds(start, chunk), :], branch)
            part = part.reshape(r.t_merge_one.shape)
            if task == 0 and start == 0:
                r.t_merge_one[...] = part
            else:
                r.t_merge_one[...] += part
            r.grad_mixed[task, pl.ds(start, chunk), :] = nt(branch, flat(r.w_merge_one)).astype(BF16)

    def attend_pairs_back(task, points):
        bias = key_bias(task)

        def one_pair(pair, carry):
            lanes = pl.multiple_of(pair * PAIR, PAIR)
            key = r.triple[task, :, pl.ds(lanes + width, PAIR)]
            value = r.triple[task, :, pl.ds(lanes + 2 * width, PAIR)]
            key_turned = key.T
            for at in range(parts):
                query = r.triple[task, pl.ds(at * PAIR, PAIR), pl.ds(lanes, PAIR)]
                grad_out = r.grad_mixed[task, pl.ds(at * PAIR, PAIR), pl.ds(lanes, PAIR)]
                log_total = r.logs_one[pl.ds((task * pairs + pair) * parts + at, 1), :]
                grad_query, grad_key, grad_value = attend_back(
                    query, key, value, key_turned,
                    r.mixed_one[task, pl.ds(at * PAIR, PAIR), pl.ds(lanes, PAIR)],
                    grad_out, log_total, bias, head_scale,
                )
                r.triple[task, pl.ds(at * PAIR, PAIR), pl.ds(lanes, PAIR)] = grad_query.astype(BF16)
                if at == 0:
                    r.key_sum[...] = grad_key
                    r.value_sum[...] = grad_value
                else:
                    r.key_sum[...] += grad_key
                    r.value_sum[...] += grad_value
            r.triple[task, :, pl.ds(lanes + width, PAIR)] = r.key_sum[...].astype(BF16)
            r.triple[task, :, pl.ds(lanes + 2 * width, PAIR)] = r.value_sum[...].astype(BF16)
            at_pair(pair, points)
            if task == tasks - 1:
                @pl.when(pair == half - 1)
                def _():
                    project_weight(0)
                    run(LOW_GRADS)

            return carry

        lax.fori_loop(0, pairs, one_pair, 0)

    def project_weight(which):
        ref = (r.t_low, r.t_high)[which]
        lanes = width // 2
        for third in range(3):
            cut = pl.ds(third * width + which * lanes, lanes)
            part = None
            for task in range(tasks):
                one = tn(r.normed_one[task], r.triple[task, :, cut])
                part = one if part is None else part + one
            ref[:, :, :, :, pl.ds(third * lanes, lanes)] = part.reshape(ref.shape[:4] + (lanes,))

    def project_back(task, start):
        rows = r.tokens[task, pl.ds(start, chunk), :].astype(F32)
        normed, scale = normalise(rows)
        incoming = nt(r.triple[task, pl.ds(start, chunk), :], flat(r.w_project_one))
        add_vector(0, incoming * normed)
        add_vector(1, incoming)
        back = normalise_back(incoming, normed, scale, param(0))
        back = r.flow[task, pl.ds(start, chunk), :].astype(F32) + back
        tiles = width // PAIR
        for tile in range(tiles):
            r.input_grad[task, pl.ds(start * tiles + tile, chunk, stride=tiles), :] = back[
                :, tile * PAIR : (tile + 1) * PAIR
            ]

    half = pairs // 2
    for task in range(tasks):
        wait_flow(task)
        merge_back(task)
        if task == tasks - 1:
            run(MERGE_GRADS)
        run(MERGED_POINTS[task])
        attend_pairs_back(task, BACK_POINTS[task])
    project_weight(1)
    run(HIGH_GRADS)
    for task in range(tasks):
        for start in range(0, samples, chunk):
            project_back(task, start)
            run(FIRST_POINTS[task * (samples // chunk) + start // chunk])

    r.vector_back[p.feat] = r.vector_sums[...]
    for shift in range(1, groups):
        remote(
            r.vector_sums, r.vector_back.at[p.feat],
            r.vector_sent.at[1], r.vector_arrived.at[1], (p.task, p.peer(shift, groups)),
        ).start()
    ending = SCHEDULE[END]
    middle = ending.index((D_PROJECT_HIGH, Reduce.inward)) + 1
    for name, stage in ending[:middle]:
        stage(items[name])

    def vectors_out(stage, slots, count):
        most = slots.at[pl.ds(0, count - 1)]
        return remote(most, most, r.vector_sent.at[stage], r.vector_arrived.at[stage], p.along_y)

    vectors_out(1, r.vector_back, groups).wait_recv()
    total = r.vector_back[0]
    for index in range(1, groups):
        total = total + r.vector_back[index]
    r.vector_total[...] = total
    r.task_slots[p.task] = total
    for device in (p.sibling, p.along_x, (CORES * (1 - p.x) + 1 - p.c, p.feat)):
        remote(
            r.vector_total, r.task_slots.at[p.task],
            r.vector_sent.at[2], r.vector_arrived.at[2], device,
        ).start()
    for name, stage in ending[middle:]:
        stage(items[name])
    for at in range(2):
        item = items[(D_SHRINK_LOW, D_SHRINK_HIGH)[at]]
        item.done()
        r.o_shrink[:, pl.ds(at * deep, deep), :] = item.final[...]
        item = items[(D_EXPAND_LOW, D_EXPAND_HIGH)[at]]
        item.done()
        r.o_expand[:, :, pl.ds(at * half_units, half_units)] = item.final[...]
    for name, out in (
        (D_PROJECT_TWO, r.o_project_two), (D_MERGE_TWO, r.o_merge_two), (D_MERGE_ONE, r.o_merge_one),
    ):
        items[name].done()
        out[...] = items[name].final[...]
    vectors_out(2, r.task_slots, members).wait_recv()
    total = r.task_slots[0]
    for index in range(1, members):
        total = total + r.task_slots[index]
    r.o_vectors[...] = total
    lanes = width // 2
    for which in range(2):
        item = items[(D_PROJECT_LOW, D_PROJECT_HIGH)[which]]
        item.done()
        for part in range(3):
            r.o_project_one[:, :, pl.ds(part * width + which * lanes, lanes)] = item.final[
                :, :, pl.ds(part * lanes, lanes)
            ]

    vectors_in().wait_send()
    vectors_out(1, r.vector_back, groups).wait_send()
    vectors_out(2, r.task_slots, members).wait_send()
    for task in range(tasks):
        upstream[task].finish()
    everywhere = r.flow.at[:, pl.ds(0, samples - block_rows)]
    remote(everywhere, everywhere, r.flow_sent.at[0], r.flow_arrived.at[0], p.along_y).wait_send()
    everywhere = r.layer_out.at[:, pl.ds(0, samples - block_rows)]
    both = remote(everywhere, everywhere, r.out_sent.at[0], r.out_arrived.at[0], p.along_y)
    both.wait_send()
    both.wait_recv()
    own = r.layer_out.at[:, pl.ds(0, block_rows)]
    pltpu.make_async_copy(own, own, r.out_local.at[0]).wait()
    for item in reductions:
        item.finish()


def finish_kernel(*refs):
    count = 9
    sources, targets = refs[:count], refs[count : count + 16]
    held = refs[count + 16 : 2 * count + 16]
    made = refs[2 * count + 16 : 2 * count + 22]
    read, written = refs[2 * count + 22 :]
    reads = [
        pltpu.make_async_copy(source, memory, read.at[at])
        for at, (source, memory) in enumerate(zip(sources, held))
    ]
    for copy in reads:
        copy.start()
    writes = []
    for at in range(2, 8):
        reads[at].wait()
        made[at - 2][...] = held[at][...].astype(F32)
        writes.append(pltpu.make_async_copy(made[at - 2], targets[at], written.at[at]))
        writes[-1].start()
    for at in range(2):
        reads[at].wait()
        writes.append(pltpu.make_async_copy(held[at], targets[at], written.at[at]))
        writes[-1].start()
    reads[8].wait()
    vectors_ref, small_to, bias_to = held[8], targets[8:15], targets[15]
    place = lax.axis_index("feat")
    width = vectors_ref.shape[1]
    size = small_to[0].shape[1]
    turned = pltpu.roll(vectors_ref[...], lax.rem(width - place * size, width), 1)
    for row, target in enumerate(small_to):
        target[...] = turned[row : row + 1, :size]
    size = bias_to.shape[1]
    per_row = width // size
    row = vectors_ref[pl.ds(len(small_to) + lax.div(place, per_row), 1), :]
    bias = row[:, :size]
    for at in range(1, per_row):
        bias = jnp.where(lax.rem(place, per_row) == at, row[:, at * size : (at + 1) * size], bias)
    bias_to[...] = bias
    for copy in writes:
        copy.wait()


def fused_body(tokens, cotangent, counts, *shards):
    (
        gain_one, shift_one, project_one, merge_one, gain_two, shift_two, project_two, merge_two,
        gain_three, shift_three, expand, bias_in, shrink, bias_out,
    ) = shards
    groups = lax.axis_size("feat")
    members = lax.axis_size("task")
    place = lax.axis_index("feat")
    tasks, samples, _, width = tokens.shape
    block_rows = samples // groups
    hidden_units = expand.shape[1]
    pairs = width // PAIR

    small = (
        gain_one, shift_one, gain_two, shift_two, gain_three, shift_three, bias_out,
    )
    length = sum(part.shape[0] for part in (bias_in,) + small)
    slots = -(-length // (8 * PAIR)) * 8
    vectors, low = None, 0
    for part in (bias_in,) + small:
        high = slots * PAIR - low - part.shape[0]
        moved = jnp.pad(part.astype(F32), (low, high))
        vectors = moved if vectors is None else vectors + moved
        low += part.shape[0]
    vectors = vectors.reshape(slots, PAIR)

    big = {
        "project_one": project_one, "merge_one": merge_one, "project_two": project_two,
        "merge_two": merge_two, "expand": expand, "shrink": shrink,
    }
    names, operands, specs = [], [], []

    def operand(name, value, spec):
        names.append(name)
        operands.append(value)
        specs.append(spec)

    any_spec = pl.BlockSpec(memory_space=pl.ANY)
    operand("counts", counts, SMEM)
    operand("tokens", tokens.reshape(tasks, samples, width), VMEM)
    operand("upstream", cotangent.reshape(tasks, samples, width), any_spec)
    operand("vectors", vectors, any_spec)
    shapes = {}
    for name, shard in big.items():
        rows, columns = shard.shape[0] // SPLIT, shard.shape[1]
        shapes[name] = (rows, columns)
        operand("s_" + name, shard.reshape(SPLIT, rows, columns), any_spec)

    outs, out_specs = [], []

    def output(name, dims, kind, spec):
        names.append(name)
        outs.append(shape(dims, kind))
        out_specs.append(spec)

    output("layer_out", (tasks, samples, width), BF16, any_spec)
    output("input_grad", (tasks, samples * width // PAIR, PAIR), F32, VMEM)
    for name in big:
        output("o_" + name, (SPLIT,) + shapes[name], BF16, VMEM)
    output("o_vectors", (VECTORS, width), F32, VMEM)

    scratch = []

    def memory(name, dims, kind):
        names.append(name)
        scratch.append(pltpu.VMEM(dims, kind))

    def semaphores(name, dims):
        names.append(name)
        scratch.append(pltpu.SemaphoreType.DMA(dims))

    for name in big:
        memory("w_" + name, (DEPTH, WIDE_Y, SPLIT) + shapes[name], BF16)
    for name in big:
        if name != "project_one":
            memory("t_" + name, (DEPTH, WIDE_Y, SPLIT) + shapes[name], F32)
    rows, columns = shapes["project_one"]
    for name in ("low", "high"):
        memory("t_" + name, (DEPTH, WIDE_Y, SPLIT, rows, columns // 2), F32)
        memory("b_" + name, (DEPTH, WIDE_Y, SPLIT, rows, columns // 2), BF16)
    rows, columns = shapes["shrink"]
    shrink_part = (rows // 2, columns)
    rows, columns = shapes["expand"]
    expand_part = (rows, columns // 2)
    rows, columns = shapes["project_one"]
    half_project = (rows, columns // 2)
    items = (
        (shrink_part, True, False), (shrink_part, True, False),
        (expand_part, False, False), (expand_part, False, False),
        (shapes["project_two"], False, False), (shapes["merge_two"], False, False),
        (shapes["merge_one"], True, True), (half_project, True, True), (half_project, True, True),
    )
    for index, (dims, wide, direct) in enumerate(items):
        count = HALVES if wide else 1
        sizes = {
            "halves": (DEPTH, WIDE_Y, HALVES), "quarters": (DEPTH, WIDE_Y, 1),
            "lines": (DEPTH, count), "outer": (DEPTH - 1 if direct else 2, count),
            "crossed": (2, count), "paired": (count,), "final": (SPLIT,), "twin": (count,),
        }
        unused = {"quarters" if wide else "twin"}
        if direct:
            unused |= {"crossed", "paired"}
        for kind in BUFFERS:
            if kind not in unused:
                memory("m%d_%s" % (index, kind), sizes[kind] + dims, BF16)
    memory("vector_slots", (groups, slots, PAIR), F32)
    memory("params", (VECTORS, width), F32)
    memory("vector_sums", (VECTORS, width), F32)
    memory("vector_back", (groups, VECTORS, width), F32)
    memory("vector_total", (VECTORS, width), F32)
    memory("task_slots", (members, VECTORS, width), F32)
    memory("normed_one", (tasks, samples, width), BF16)
    memory("triple", (tasks, samples, 3 * width), BF16)
    memory("mixed_one", (tasks, samples, width), BF16)
    memory("logs_one", (tasks * pairs * (samples // PAIR), 2 * PAIR), F32)
    memory("grad_mixed", (tasks, samples, width), BF16)
    memory("flow", (tasks, samples, width), BF16)
    memory("hidden_in", (groups, tasks, block_rows, width), BF16)
    memory("upstream_in", (groups, tasks, block_rows, width), BF16)
    memory("part_triple", (256, 3 * width), BF16)
    memory("block_mixed", (256, width), BF16)
    memory("block_grad", (256, width), BF16)
    memory("block_logs", (8, 2 * PAIR), F32)
    memory("key_sum", (samples, PAIR), F32)
    memory("value_sum", (samples, PAIR), F32)
    semaphores("gather_sent", (10, 6))
    semaphores("gather_arrived", (10, 6))
    semaphores("gather_local", (10,))
    semaphores("reduce_sent", (len(items), 8))
    semaphores("reduce_arrived", (len(items), 8))
    for name in ("vector_sent", "vector_arrived"):
        semaphores(name, (3,))
    semaphores("vector_local", (1,))
    for name in ("upstream", "hidden"):
        for kind in ("_sent", "_arrived", "_local"):
            semaphores(name + kind, (tasks,))
    semaphores("flow_sent", (1,))
    semaphores("flow_arrived", (tasks,))
    semaphores("flow_local", (tasks,))
    for kind in ("_sent", "_arrived", "_local"):
        semaphores("out" + kind, (1,))

    results = pl.pallas_call(
        functools.partial(fused_kernel, tuple(names)),
        in_specs=specs,
        out_specs=out_specs,
        out_shape=outs,
        scratch_shapes=scratch,
        compiler_params=pltpu.CompilerParams(
            vmem_limit_bytes=FUSED_LIMIT, collective_id=0, has_side_effects=True
        ),
        name="layer",
    )(*operands)
    outs = [
        shape((tasks, samples, width), BF16),
        shape((tasks, samples * width // PAIR, PAIR), F32),
    ]
    outs += [shape((SPLIT,) + shapes[name], F32) for name in big]
    outs += [shape((1, part.shape[0]), F32) for part in small]
    outs += [shape((1, bias_in.shape[0]), F32)]
    finished = pl.pallas_call(
        finish_kernel,
        in_specs=[any_spec] * len(results),
        out_specs=[any_spec] * (2 + len(big)) + [VMEM] * (len(small) + 1),
        out_shape=outs,
        scratch_shapes=[pltpu.VMEM(result.shape, result.dtype) for result in results]
        + [pltpu.VMEM(out.shape, F32) for out in outs[2 : 2 + len(big)]]
        + [pltpu.SemaphoreType.DMA((len(results),))] * 2,
        compiler_params=pltpu.CompilerParams(vmem_limit_bytes=FINISH_LIMIT),
        name="finish",
    )(*results)
    grads = {
        name: result.reshape(big[name].shape) for name, result in zip(big, finished[2:])
    }
    ends = [part.reshape(-1) for part in finished[2 + len(big):]]
    return (
        finished[0].reshape(tokens.shape), finished[1].reshape(tokens.shape),
        ends[0], ends[1], grads["project_one"], grads["merge_one"],
        ends[2], ends[3], grads["project_two"], grads["merge_two"],
        ends[4], ends[5], grads["expand"], ends[7], grads["shrink"], ends[6],
    )


def solution(mesh):
    wide = P("task", None, "feat", None)
    row, grid = P("feat"), P("feat", None)
    weights = (
        row, row, grid, grid, row, row, grid, grid, row, row, grid, row, grid, row,
    )
    fits = mesh.shape["feat"] == DEPTH * WIDE_Y and mesh.shape["task"] == CORES * HALVES
    return jax.shard_map(
        fused_body if fits else body,
        mesh=mesh,
        in_specs=(wide, wide, P("task")) + weights,
        out_specs=(wide, wide) + weights,
        check_vma=False,
    )
```

```python
import functools
import types

import jax
import jax.numpy as jnp
from jax import lax
from jax.experimental import pallas as pl
from jax.experimental.pallas import tpu as pltpu
from jax.sharding import PartitionSpec as P

HEADS = 8
NORM_EPS = 1e-05
MASKED = -1e30
PAIR = 128
GROUP = 16
F32 = jnp.float32
BF16 = jnp.bfloat16


def nt(left, right):
    return lax.dot_general(left, right, (((1,), (1,)), ((), ())), preferred_element_type=F32)


def tn(left, right):
    return lax.dot_general(left, right, (((0,), (0,)), ((), ())), preferred_element_type=F32)


def nn(left, right):
    return lax.dot_general(left, right, (((1,), (0,)), ((), ())), preferred_element_type=F32)


def normalise(values):
    center = values - jnp.mean(values, axis=-1, keepdims=True)
    spread = jnp.mean(center * center, axis=-1, keepdims=True)
    scale = lax.rsqrt(spread + NORM_EPS)
    return center * scale, scale


def normalise_back(incoming, normed, scale, gain):
    weighted = incoming * gain
    first = jnp.mean(weighted, axis=-1, keepdims=True)
    second = jnp.mean(weighted * normed, axis=-1, keepdims=True)
    return scale * (weighted - first - normed * second)


def head_masks(scale):
    lane = lax.broadcasted_iota(jnp.int32, (1, PAIR), 1)
    low = jnp.where(lane < PAIR // 2, scale, 0.0).astype(BF16)
    high = jnp.where(lane < PAIR // 2, 0.0, scale).astype(BF16)
    return low, high


def two_heads(rows, scale):
    low, high = head_masks(scale)
    return jnp.concatenate([rows * low, rows * high], axis=0)


def join_heads(turned, length):
    half = PAIR // 2
    joined = jnp.concatenate([turned[:half, :length], turned[half:, length:]], axis=0)
    return joined.T


def attend(query, key, value_turned, bias, head_scale):
    scores = nt(key, two_heads(query, head_scale)) + bias
    top = jnp.max(scores, axis=0, keepdims=True)
    expo = jnp.exp(scores - top)
    total = jnp.sum(expo, axis=0, keepdims=True)
    mixed = nn(value_turned, expo.astype(BF16)) * (1.0 / total)
    return join_heads(mixed, query.shape[0]), top + jnp.log(total)


def attend_back(
    query, key, value, key_turned, result, grad_out, log_total, bias, head_scale
):
    half = PAIR // 2
    product = (result.astype(F32) * grad_out.astype(F32)).T
    inner = jnp.concatenate(
        [
            jnp.sum(product[:half], axis=0, keepdims=True),
            jnp.sum(product[half:], axis=0, keepdims=True),
        ],
        axis=1,
    )
    queries = two_heads(query, head_scale)
    grads = two_heads(grad_out, 1.0)
    chances = jnp.exp(nt(key, queries) + bias - log_total)
    grad_scores = (chances * (nt(value, grads) - inner)).astype(BF16)
    grad_value = nn(chances.astype(BF16), grads)
    grad_key = nn(grad_scores, queries)
    grad_query = join_heads(nn(key_turned, grad_scores), query.shape[0]) * head_scale
    return grad_query, grad_key, grad_value


def sample_forward_kernel(
    counts_ref, tokens_ref, gain_ref, shift_ref, project_ref, merge_ref,
    triple_ref, mixed_ref, logs_ref, hidden_ref,
):
    count = counts_ref[pl.program_id(0)]
    samples, width = tokens_ref.shape[1:]
    chunk = min(256, samples)
    gain = gain_ref[...].astype(F32)
    shift = shift_ref[...].astype(F32)
    for start in range(0, samples, chunk):
        rows = tokens_ref[0, pl.ds(start, chunk), :].astype(F32)
        normed = (normalise(rows)[0] * gain + shift).astype(BF16)
        triple_ref[0, pl.ds(start, chunk), :] = nn(normed, project_ref[...]).astype(BF16)
    keys = lax.broadcasted_iota(jnp.int32, (samples, 1), 0)
    bias = jnp.where(keys < count, 0.0, MASKED)
    head_scale = (width // HEADS) ** (-0.5)
    pairs = width // PAIR

    def one_pair(pair, carry):
        lanes = pl.multiple_of(pair * PAIR, PAIR)
        key = triple_ref[0, :, pl.ds(lanes + width, PAIR)]
        value_turned = triple_ref[0, :, pl.ds(lanes + 2 * width, PAIR)].T
        for at in range(samples // PAIR):
            query = triple_ref[0, pl.ds(at * PAIR, PAIR), pl.ds(lanes, PAIR)]
            mixed, log_total = attend(query, key, value_turned, bias, head_scale)
            mixed_ref[0, pl.ds(at * PAIR, PAIR), pl.ds(lanes, PAIR)] = mixed.astype(BF16)
            logs_ref[0, pl.ds(pair * (samples // PAIR) + at, 1), :] = log_total
        return carry

    lax.fori_loop(0, pairs, one_pair, 0)
    for start in range(0, samples, chunk):
        rows = tokens_ref[0, pl.ds(start, chunk), :].astype(F32)
        at = lax.broadcasted_iota(jnp.int32, (chunk, 1), 0) + start
        live = jnp.where(at < count, 1.0, 0.0)
        merged = nn(mixed_ref[0, pl.ds(start, chunk), :], merge_ref[...])
        hidden_ref[0, pl.ds(start, chunk), :] = (rows + live * merged).astype(BF16)


def sample_backward_kernel(
    counts_ref, tokens_ref, gain_ref, shift_ref, project_ref, merge_ref,
    triple_ref, mixed_ref, logs_ref, flow_ref,
    input_grad_ref, project_grad_ref, merge_grad_ref, gain_grad_ref, shift_grad_ref,
    grad_mixed, grad_triple, key_sum, value_sum,
):
    task = pl.program_id(0)
    count = counts_ref[task]
    samples, width = tokens_ref.shape[1:]
    chunk = min(256, samples)
    gain = gain_ref[...].astype(F32)
    shift = shift_ref[...].astype(F32)

    @pl.when(task == 0)
    def _():
        project_grad_ref[...] = jnp.zeros_like(project_grad_ref)
        merge_grad_ref[...] = jnp.zeros_like(merge_grad_ref)
        gain_grad_ref[...] = jnp.zeros_like(gain_grad_ref)
        shift_grad_ref[...] = jnp.zeros_like(shift_grad_ref)

    for start in range(0, samples, chunk):
        at = lax.broadcasted_iota(jnp.int32, (chunk, 1), 0) + start
        live = jnp.where(at < count, 1.0, 0.0)
        branch = (flow_ref[0, pl.ds(start, chunk), :].astype(F32) * live).astype(BF16)
        merge_grad_ref[...] += tn(mixed_ref[0, pl.ds(start, chunk), :], branch)
        grad_mixed[pl.ds(start, chunk), :] = nt(branch, merge_ref[...]).astype(BF16)
    keys = lax.broadcasted_iota(jnp.int32, (samples, 1), 0)
    bias = jnp.where(keys < count, 0.0, MASKED)
    head_scale = (width // HEADS) ** (-0.5)
    pairs = width // PAIR

    def one_pair(pair, carry):
        lanes = pl.multiple_of(pair * PAIR, PAIR)
        key = triple_ref[0, :, pl.ds(lanes + width, PAIR)]
        value = triple_ref[0, :, pl.ds(lanes + 2 * width, PAIR)]
        key_turned = key.T
        for at in range(samples // PAIR):
            query = triple_ref[0, pl.ds(at * PAIR, PAIR), pl.ds(lanes, PAIR)]
            grad_out = grad_mixed[pl.ds(at * PAIR, PAIR), pl.ds(lanes, PAIR)]
            log_total = logs_ref[0, pl.ds(pair * (samples // PAIR) + at, 1), :]
            grad_query, grad_key, grad_value = attend_back(
                query, key, value, key_turned,
                mixed_ref[0, pl.ds(at * PAIR, PAIR), pl.ds(lanes, PAIR)],
                grad_out, log_total, bias, head_scale,
            )
            grad_triple[pl.ds(at * PAIR, PAIR), pl.ds(lanes, PAIR)] = grad_query.astype(BF16)
            if at == 0:
                key_sum[...] = grad_key
                value_sum[...] = grad_value
            else:
                key_sum[...] += grad_key
                value_sum[...] += grad_value
        grad_triple[:, pl.ds(lanes + width, PAIR)] = key_sum[...].astype(BF16)
        grad_triple[:, pl.ds(lanes + 2 * width, PAIR)] = value_sum[...].astype(BF16)
        return carry

    lax.fori_loop(0, pairs, one_pair, 0)
    for start in range(0, samples, chunk):
        rows = tokens_ref[0, pl.ds(start, chunk), :].astype(F32)
        normed, scale = normalise(rows)
        part = grad_triple[pl.ds(start, chunk), :]
        project_grad_ref[...] += tn((normed * gain + shift).astype(BF16), part)
        incoming = nt(part, project_ref[...])
        gain_grad_ref[...] += jnp.sum(incoming * normed, axis=0, keepdims=True)
        shift_grad_ref[...] += jnp.sum(incoming, axis=0, keepdims=True)
        back = normalise_back(incoming, normed, scale, gain)
        input_grad_ref[0, pl.ds(start, chunk), :] = (
            flow_ref[0, pl.ds(start, chunk), :].astype(F32) + back
        )


def block_kernel(
    rows_per_task, blocks,
    counts_ref, hidden_ref, upstream_ref,
    gain_two_ref, shift_two_ref, project_ref, merge_ref,
    gain_three_ref, shift_three_ref, expand_ref, bias_in_ref, shrink_ref, bias_out_ref,
    out_ref, flow_ref,
    gain_two_grad, shift_two_grad, project_grad, merge_grad,
    gain_three_grad, shift_three_grad, expand_grad, bias_in_grad, shrink_grad, bias_out_grad,
    triple, mixed, logs, grad_mixed, grad_triple, key_sum, value_sum,
):
    step = pl.program_id(0)
    place = lax.axis_index("feat")
    feats, _, width = hidden_ref.shape
    size = feats * GROUP
    rows = blocks * size
    hidden_units = expand_ref.shape[1]
    sums = (
        gain_two_grad, shift_two_grad, project_grad, merge_grad, gain_three_grad,
        shift_three_grad, expand_grad, bias_in_grad, shrink_grad, bias_out_grad,
    )

    @pl.when(step == 0)
    def _():
        for ref in sums:
            ref[...] = jnp.zeros_like(ref)

    def load(ref):
        pieces = [
            ref[:, pl.ds(block * GROUP, GROUP), :].reshape(size, width) for block in range(blocks)
        ]
        return pieces[0] if blocks == 1 else jnp.concatenate(pieces, axis=0)

    def store(ref, values):
        for block in range(blocks):
            piece = values[block * size : (block + 1) * size]
            ref[:, pl.ds(block * GROUP, GROUP), :] = piece.reshape(feats, GROUP, width)

    row = lax.broadcasted_iota(jnp.int32, (rows, 1), 0)
    row = (step * blocks + row // size) * GROUP + row % GROUP
    sample = place * rows_per_task + row % rows_per_task
    count = jnp.zeros_like(row)
    for task in range(counts_ref.shape[0]):
        count = jnp.where(row // rows_per_task == task, counts_ref[task], count)
    live = jnp.where(sample < count, 1.0, 0.0)

    gain_two = gain_two_ref[...].astype(F32)
    shift_two = shift_two_ref[...].astype(F32)
    gain_three = gain_three_ref[...].astype(F32)
    shift_three = shift_three_ref[...].astype(F32)
    hidden_one = load(hidden_ref).astype(F32)
    unit_two, scale_two = normalise(hidden_one)
    normed_two = (unit_two * gain_two + shift_two).astype(BF16)
    triple[...] = nn(normed_two, project_ref[...]).astype(BF16)

    reach = min(PAIR, size)
    key_at = lax.broadcasted_iota(jnp.int32, (size, 2 * reach), 0) % GROUP
    query_at = lax.broadcasted_iota(jnp.int32, (size, 2 * reach), 1) % GROUP
    bias = jnp.where(key_at == query_at, 0.0, MASKED)
    head_scale = (width // HEADS) ** (-0.5)
    parts = size // reach
    pairs = width // PAIR
    for block in range(blocks):
        start = block * size
        for pair in range(pairs):
            lanes = pair * PAIR
            key = triple[pl.ds(start, size), pl.ds(width + lanes, PAIR)]
            value_turned = triple[pl.ds(start, size), pl.ds(2 * width + lanes, PAIR)].T
            for part in range(parts):
                at = start + part * reach
                query = triple[pl.ds(at, reach), pl.ds(lanes, PAIR)]
                result, log_total = attend(query, key, value_turned, bias, head_scale)
                mixed[pl.ds(at, reach), pl.ds(lanes, PAIR)] = result.astype(BF16)
                logs[pl.ds((block * pairs + pair) * parts + part, 1), :] = log_total

    hidden_two = hidden_one + live * nn(mixed[...], merge_ref[...])
    unit_three, scale_three = normalise(hidden_two)
    normed_three = (unit_three * gain_three + shift_three).astype(BF16)
    upstream = load(upstream_ref).astype(F32)
    grad_dense = (upstream * live).astype(BF16)
    bias_out_grad[...] += jnp.sum(grad_dense.astype(F32), axis=0, keepdims=True)
    lanes = min(512, hidden_units)
    dense = None
    incoming = None
    for start in range(0, hidden_units, lanes):
        cut = pl.ds(start, lanes)
        expanded = nn(normed_three, expand_ref[:, cut]) + bias_in_ref[:, cut].astype(F32)
        square = expanded * expanded
        steep = 0.7978845608028654
        bend = jnp.tanh(expanded * (steep + (steep * 0.044715) * square))
        half_up = 0.5 + 0.5 * bend
        activated = (expanded * half_up).astype(BF16)
        slope = half_up + (0.5 * expanded) * (1.0 - bend * bend) * (
            steep + (3.0 * steep * 0.044715) * square
        )
        grad_expanded = (slope * nt(grad_dense, shrink_ref[cut, :])).astype(BF16)
        bias_in_grad[:, cut] += jnp.sum(grad_expanded.astype(F32), axis=0, keepdims=True)
        shrink_grad[cut, :] += tn(activated, grad_dense)
        expand_grad[:, cut] += tn(normed_three, grad_expanded)
        up = nn(activated, shrink_ref[cut, :])
        down = nt(grad_expanded, expand_ref[:, cut])
        dense = up if dense is None else dense + up
        incoming = down if incoming is None else incoming + down
    result = hidden_two + live * (dense + bias_out_ref[...].astype(F32))
    store(out_ref, result.astype(BF16))

    gain_three_grad[...] += jnp.sum(incoming * unit_three, axis=0, keepdims=True)
    shift_three_grad[...] += jnp.sum(incoming, axis=0, keepdims=True)
    flow_two = upstream + normalise_back(incoming, unit_three, scale_three, gain_three)
    branch = (flow_two * live).astype(BF16)
    merge_grad[...] += tn(mixed[...], branch)
    grad_mixed[...] = nt(branch, merge_ref[...]).astype(BF16)
    for block in range(blocks):
        start = block * size
        for pair in range(pairs):
            lanes = pair * PAIR
            key = triple[pl.ds(start, size), pl.ds(width + lanes, PAIR)]
            value = triple[pl.ds(start, size), pl.ds(2 * width + lanes, PAIR)]
            key_turned = key.T
            for part in range(parts):
                at = start + part * reach
                query = triple[pl.ds(at, reach), pl.ds(lanes, PAIR)]
                grad_out = grad_mixed[pl.ds(at, reach), pl.ds(lanes, PAIR)]
                log_total = logs[pl.ds((block * pairs + pair) * parts + part, 1), :]
                grad_query, grad_key, grad_value = attend_back(
                    query, key, value, key_turned, mixed[pl.ds(at, reach), pl.ds(lanes, PAIR)],
                    grad_out, log_total, bias, head_scale,
                )
                grad_triple[pl.ds(at, reach), pl.ds(lanes, PAIR)] = grad_query.astype(BF16)
                if part > 0:
                    grad_key += key_sum[...]
                    grad_value += value_sum[...]
                if part == parts - 1:
                    where = pl.ds(start, size)
                    grad_triple[where, pl.ds(width + lanes, PAIR)] = grad_key.astype(BF16)
                    grad_triple[where, pl.ds(2 * width + lanes, PAIR)] = grad_value.astype(BF16)
                else:
                    key_sum[...] = grad_key
                    value_sum[...] = grad_value
    project_grad[...] += tn(normed_two, grad_triple[...])
    incoming = nt(grad_triple[...], project_ref[...])
    gain_two_grad[...] += jnp.sum(incoming * unit_two, axis=0, keepdims=True)
    shift_two_grad[...] += jnp.sum(incoming, axis=0, keepdims=True)
    flow_one = flow_two + normalise_back(incoming, unit_two, scale_two, gain_two)
    store(flow_ref, flow_one.astype(BF16))


VMEM = pl.BlockSpec(memory_space=pltpu.VMEM)
SMEM = pl.BlockSpec(memory_space=pltpu.SMEM)
LIMIT = 56 * 1024 * 1024


def shape(dims, kind):
    return jax.ShapeDtypeStruct(dims, kind)


def by_task(*dims):
    return pl.BlockSpec((1,) + dims, lambda task: (task,) + (0,) * len(dims))


def body(tokens, cotangent, counts, *shards):
    groups = lax.axis_size("feat")
    tasks, samples, local, width = tokens.shape
    rows_per_task = samples // groups
    gathered = [lax.all_gather(part, "feat", axis=0, tiled=True) for part in shards]
    gathered = [part[None, :] if part.ndim == 1 else part for part in gathered]
    (
        gain_one, shift_one, project_one, merge_one, gain_two, shift_two, project_two, merge_two,
        gain_three, shift_three, expand, bias_in, shrink, bias_out,
    ) = gathered
    hidden_units = expand.shape[1]
    source = tokens.reshape(tasks, samples, width)

    def to_blocks(rows):
        rows = rows.reshape(tasks, groups, rows_per_task, width)
        rows = jnp.transpose(rows, (1, 0, 2, 3))
        rows = lax.all_to_all(rows, "feat", split_axis=0, concat_axis=0, tiled=True)
        return rows.reshape(groups, tasks * rows_per_task, width)

    def from_blocks(rows):
        rows = rows.reshape(groups, tasks, rows_per_task, width)
        rows = lax.all_to_all(rows, "feat", split_axis=0, concat_axis=0, tiled=True)
        rows = jnp.transpose(rows, (1, 0, 2, 3))
        return rows.reshape(tasks, samples, width)

    upstream = to_blocks(cotangent.reshape(tasks, samples, width))
    log_rows = samples * width // PAIR // PAIR
    triple, mixed, logs, hidden = pl.pallas_call(
        sample_forward_kernel,
        grid=(tasks,),
        in_specs=[SMEM, by_task(samples, width), VMEM, VMEM, VMEM, VMEM],
        out_specs=[
            by_task(samples, 3 * width), by_task(samples, width),
            by_task(log_rows, 2 * PAIR), by_task(samples, width),
        ],
        out_shape=[
            shape((tasks, samples, 3 * width), BF16),
            shape((tasks, samples, width), BF16),
            shape((tasks, log_rows, 2 * PAIR), F32),
            shape((tasks, samples, width), BF16),
        ],
        compiler_params=pltpu.CompilerParams(vmem_limit_bytes=LIMIT),
        name="sample_forward",
    )(counts, source, gain_one, shift_one, project_one, merge_one)

    hidden = to_blocks(hidden)
    all_rows = tasks * rows_per_task
    size = groups * GROUP
    blocks = max(1, min(all_rows // GROUP, 256 // size))
    steps = all_rows // (GROUP * blocks)
    rows = blocks * size
    slab = pl.BlockSpec((groups, GROUP * blocks, width), lambda step: (0, step, 0))
    reach = min(PAIR, size)
    pieces = blocks * (width // PAIR) * (size // reach)
    grads = [
        shape((1, width), F32), shape((1, width), F32),
        shape((width, 3 * width), F32), shape((width, width), F32),
        shape((1, width), F32), shape((1, width), F32),
        shape((width, hidden_units), F32), shape((1, hidden_units), F32),
        shape((hidden_units, width), F32), shape((1, width), F32),
    ]
    results = pl.pallas_call(
        functools.partial(block_kernel, rows_per_task, blocks),
        grid=(steps,),
        in_specs=[SMEM, slab, slab] + [VMEM] * 10,
        out_specs=[slab, slab] + [VMEM] * 10,
        out_shape=[shape((groups, all_rows, width), BF16)] * 2 + grads,
        scratch_shapes=[
            pltpu.VMEM((rows, 3 * width), BF16),
            pltpu.VMEM((rows, width), BF16),
            pltpu.VMEM((pieces, 2 * reach), F32),
            pltpu.VMEM((rows, width), BF16),
            pltpu.VMEM((rows, 3 * width), BF16),
            pltpu.VMEM((size, PAIR), F32),
            pltpu.VMEM((size, PAIR), F32),
        ],
        compiler_params=pltpu.CompilerParams(vmem_limit_bytes=LIMIT),
        name="block_layer",
    )(
        counts, hidden, upstream, gain_two, shift_two, project_two, merge_two,
        gain_three, shift_three, expand, bias_in, shrink, bias_out,
    )
    layer_out = from_blocks(results[0])
    flow = from_blocks(results[1])

    first = pl.pallas_call(
        sample_backward_kernel,
        grid=(tasks,),
        in_specs=[
            SMEM, by_task(samples, width), VMEM, VMEM, VMEM, VMEM,
            by_task(samples, 3 * width), by_task(samples, width),
            by_task(log_rows, 2 * PAIR), by_task(samples, width),
        ],
        out_specs=[by_task(samples, width), VMEM, VMEM, VMEM, VMEM],
        out_shape=[
            shape((tasks, samples, width), F32),
            shape((width, 3 * width), F32), shape((width, width), F32),
            shape((1, width), F32), shape((1, width), F32),
        ],
        scratch_shapes=[
            pltpu.VMEM((samples, width), BF16),
            pltpu.VMEM((samples, 3 * width), BF16),
            pltpu.VMEM((samples, PAIR), F32),
            pltpu.VMEM((samples, PAIR), F32),
        ],
        compiler_params=pltpu.CompilerParams(vmem_limit_bytes=LIMIT),
        name="sample_backward",
    )(
        counts, source, gain_one, shift_one, project_one, merge_one, triple, mixed, logs, flow,
    )
    (
        gain_two_grad, shift_two_grad, project_two_grad, merge_two_grad, gain_three_grad,
        shift_three_grad, expand_grad, bias_in_grad, shrink_grad, bias_out_grad,
    ) = results[2:]
    totals = (
        first[3], first[4], first[1], first[2], gain_two_grad, shift_two_grad, project_two_grad,
        merge_two_grad, gain_three_grad, shift_three_grad, expand_grad, bias_in_grad,
        shrink_grad, bias_out_grad,
    )
    totals = [part[0] if part.shape[0] == 1 else part for part in totals]
    totals = tuple(part.astype(BF16) for part in totals)
    totals = lax.psum_scatter(totals, "feat", scatter_dimension=0, tiled=True)
    totals = lax.psum(totals, "task")
    return (
        layer_out.reshape(tokens.shape),
        first[0].reshape(tokens.shape),
    ) + tuple(part.astype(F32) for part in totals)


FUSED_LIMIT = 62 * 1024 * 1024

MESH = pl.DeviceIdType.MESH
DEPTH, WIDE_Y, CORES, HALVES = 4, 2, 2, 2
SPLIT = CORES * HALVES
VECTORS = 16
FINISH_LIMIT = 56 * 1024 * 1024
BUFFERS = ("halves", "quarters", "lines", "outer", "crossed", "paired", "final", "twin")


def remote(source, target, sent, arrived, device):
    return pltpu.make_async_remote_copy(
        src_ref=source, dst_ref=target, send_sem=sent, recv_sem=arrived,
        device_id=device, device_id_type=MESH,
    )


class Place:
    def __init__(self):
        self.feat = lax.axis_index("feat")
        self.task = lax.axis_index("task")
        self.z = lax.div(self.feat, WIDE_Y)
        self.y = lax.rem(self.feat, WIDE_Y)
        self.x = lax.div(self.task, CORES)
        self.c = lax.rem(self.task, CORES)
        self.mine = HALVES * self.c + self.x
        self.theirs = HALVES * self.c + 1 - self.x
        self.below = HALVES * self.c
        self.other = HALVES * (1 - self.c)
        self.along_y = (self.task, WIDE_Y * self.z + 1 - self.y)
        self.along_x = (CORES * (1 - self.x) + self.c, self.feat)
        self.sibling = (CORES * self.x + 1 - self.c, self.feat)
        self.across = DEPTH - 1 - self.z
        self.near_low = 2 * lax.div(self.z, 2)
        self.far_low = 2 - self.near_low
        self.pair = 2 * self.near_low + 1 - self.z
        self.inner = jnp.logical_or(self.z == 1, self.z == 2)

    def along_z(self, shift):
        return lax.rem(self.z + shift, DEPTH)

    def at_z(self, z):
        return (self.task, WIDE_Y * z + self.y)

    def peer(self, shift, groups):
        return lax.rem(self.feat + shift, groups)


class Moves:
    def __init__(self, place, index, wide, sent, arrived, stages):
        self.place, self.wide = place, wide
        self.rows = pl.ds(place.below, HALVES) if wide else pl.ds(place.mine, 1)
        self.sent = [sent.at[index, stage] for stage in range(stages)]
        self.arrived = [arrived.at[index, stage] for stage in range(stages)]

    def move(self, stage, source, target, device):
        return remote(source, target, self.sent[stage], self.arrived[stage], device)


class Gather(Moves):
    def __init__(self, place, index, shard, weight, sent, arrived, local, wide=False, direct=False):
        super().__init__(place, index, wide, sent, arrived, 6)
        self.shard, self.weight, self.local, self.direct = shard, weight, local.at[index], direct

    def _own(self):
        p = self.place
        return pltpu.make_async_copy(
            self.shard.at[self.rows], self.weight.at[p.z, p.y, self.rows], self.local
        )

    def _pair(self, z_count):
        p = self.place
        part = self.weight.at[pl.ds(0, z_count), p.y, self.rows]
        return self.move(0, part, part, p.at_z(p.pair))

    def _far(self, stage, low, device):
        part = self.weight.at[pl.ds(low, 2), self.place.y, self.rows]
        return self.move(stage, part, part, device)

    def _along_y(self):
        p = self.place
        part = self.weight.at[:, p.y, self.rows]
        return self.move(3, part, part, p.along_y)

    def _along_x(self):
        p = self.place
        part = self.weight.at[:, :, self.rows]
        return self.move(4, part, part, p.along_x)

    def _across(self):
        p = self.place
        part = self.weight.at[:, :, pl.ds(p.below, HALVES)]
        return self.move(5, part, part, p.sibling)

    def start(self):
        p = self.place
        self._own().start()
        targets = [p.along_z(shift) for shift in range(1, DEPTH)] if self.direct else [p.pair]
        for z in targets:
            self.move(
                0, self.shard.at[self.rows], self.weight.at[p.z, p.y, self.rows], p.at_z(z)
            ).start()

    def middle(self):
        if self.direct:
            return
        p = self.place

        @pl.when(p.inner)
        def _():
            self._own().wait()
            self._pair(1).wait_recv()
            self._far(1, p.near_low, p.at_z(p.across)).start()

    def outward(self):
        if self.direct:
            return
        p = self.place

        @pl.when(p.inner)
        def _():
            self._far(1, p.far_low, p.at_z(p.across)).wait_recv()
            self._far(2, p.far_low, p.at_z(p.pair)).start()

    def along_y(self):
        p = self.place
        if self.direct:
            self._own().wait()
            self._pair(DEPTH - 1).wait_recv()
        else:
            @pl.when(jnp.logical_not(p.inner))
            def _():
                self._own().wait()
                self._pair(1).wait_recv()
                self._far(2, p.far_low, p.at_z(p.pair)).wait_recv()

        self._along_y().start()

    def along_x(self):
        if not self.wide:
            self._along_y().wait_recv()
            self._along_x().start()

    def core(self):
        if self.wide:
            self._along_y().wait_recv()
        else:
            self._along_x().wait_recv()
        self._across().start()

    def done(self):
        self._across().wait_recv()

    def finish(self):
        p = self.place
        if self.direct:
            self._pair(DEPTH - 1).wait_send()
        else:
            self._pair(1).wait_send()

            @pl.when(p.inner)
            def _():
                self._far(1, p.near_low, p.at_z(p.across)).wait_send()
                self._far(2, p.far_low, p.at_z(p.pair)).wait_send()

        self._along_y().wait_send()
        if not self.wide:
            self._along_x().wait_send()
        self._across().wait_send()


class Reduce(Moves):
    def __init__(
        self, place, index, total, staged, memory, sent, arrived, wide=False, direct=False
    ):
        super().__init__(place, index, wide, sent, arrived, 8)
        self.total, self.staged, self.direct = total, staged, direct
        (
            self.halves, self.quarters, self.lines, self.outer, self.crossed, self.paired,
            self.final, self.twin,
        ) = memory

    def _core(self):
        p = self.place
        return self.move(
            0, self.staged.at[:, :, pl.ds(p.other, HALVES)], self.halves, p.sibling
        )

    def _x(self):
        p = self.place
        return self.move(1, self.staged.at[:, :, pl.ds(p.theirs, 1)], self.quarters, p.along_x)

    def _y(self):
        p = self.place
        return self.move(2, self.staged.at[:, 1 - p.y, self.rows], self.lines, p.along_y)

    def _inward(self):
        p = self.place
        if self.direct:
            return self.move(3, self.outer, self.outer, p.at_z(p.pair))
        return self.move(
            3, self.staged.at[pl.ds(p.far_low, 2), p.y, self.rows], self.outer, p.at_z(p.pair)
        )

    def _over(self):
        p = self.place
        return self.move(
            4, self.staged.at[pl.ds(p.far_low, 2), p.y, self.rows], self.crossed, p.at_z(p.across)
        )

    def _pair(self):
        p = self.place
        return self.move(5, self.staged.at[p.pair, p.y, self.rows], self.paired, p.at_z(p.pair))

    def _twin(self):
        p = self.place
        part = self.final.at[self.rows]
        return self.move(6, part, self.twin if self.wide else part, p.along_x)

    def _across(self):
        p = self.place
        part = self.final.at[pl.ds(p.below, HALVES)]
        return self.move(7, part, part, p.sibling)

    def core(self):
        p = self.place

        def one(z, carry):
            cut = pl.ds(p.other, HALVES)
            self.staged[z, :, cut] = self.total[z, :, cut].astype(BF16)
            return carry

        lax.fori_loop(0, DEPTH, one, 0)
        self._core().start()

    def x(self):
        p = self.place
        if self.wide:
            return
        self._core().wait_recv()

        def one(z, carry):
            summed = self.total[z, :, p.theirs] + self.halves[z, :, 1 - p.x].astype(F32)
            self.staged[z, :, p.theirs] = summed.astype(BF16)
            return carry

        lax.fori_loop(0, DEPTH, one, 0)
        self._x().start()

    def y(self):
        p = self.place
        if self.wide:
            self._core().wait_recv()
        else:
            self._x().wait_recv()

        def one(z, carry):
            if self.wide:
                summed = self.total[z, :, self.rows] + self.halves[z].astype(F32)
            else:
                summed = self.total[z, :, self.rows] + self.halves[z, :, pl.ds(p.x, 1)].astype(F32)
                summed = summed + self.quarters[z].astype(F32)
            self.staged[z, :, self.rows] = summed.astype(BF16)
            return carry

        lax.fori_loop(0, DEPTH, one, 0)
        self._y().start()

    def inward(self):
        p = self.place
        self._y().wait_recv()

        def one(z, carry):
            summed = self.staged[z, p.y, self.rows].astype(F32) + self.lines[z].astype(F32)
            self.staged[z, p.y, self.rows] = summed.astype(BF16)
            return carry

        lax.fori_loop(0, DEPTH, one, 0)
        if self.direct:
            for shift in range(1, DEPTH):
                z = p.along_z(shift)
                self.move(
                    3, self.staged.at[z, p.y, self.rows], self.outer.at[shift - 1], p.at_z(z)
                ).start()
            return

        @pl.when(jnp.logical_not(p.inner))
        def _():
            self._inward().start()

    def over(self):
        p = self.place

        @pl.when(p.inner)
        def _():
            self._inward().wait_recv()
            for at in range(2):
                z = p.far_low + at
                summed = self.staged[z, p.y, self.rows].astype(F32) + self.outer[at].astype(F32)
                self.staged[z, p.y, self.rows] = summed.astype(BF16)
            self._over().start()

    def pair(self):
        p = self.place

        @pl.when(p.inner)
        def _():
            self._over().wait_recv()
            for at in range(2):
                z = p.near_low + at
                summed = self.staged[z, p.y, self.rows].astype(F32) + self.crossed[at].astype(F32)
                self.staged[z, p.y, self.rows] = summed.astype(BF16)

        self._pair().start()

    def twins(self):
        p = self.place
        summed = self.staged[p.z, p.y, self.rows].astype(F32)
        if self.direct:
            self._inward().wait_recv()
            for shift in range(DEPTH - 1):
                summed = summed + self.outer[shift].astype(F32)
        else:
            self._pair().wait_recv()
            summed = summed + self.paired[...].astype(F32)
        self.final[self.rows] = summed.astype(BF16)
        self._twin().start()

    def share(self):
        self._twin().wait_recv()
        if self.wide:
            self._twin().wait_send()
            summed = self.final[self.rows].astype(F32) + self.twin[...].astype(F32)
            self.final[self.rows] = summed.astype(BF16)
        self._across().start()

    def done(self):
        self._across().wait_recv()

    def finish(self):
        p = self.place
        self._core().wait_send()
        if not self.wide:
            self._x().wait_send()
            self._twin().wait_send()
        self._y().wait_send()
        self._across().wait_send()
        if self.direct:
            self._inward().wait_send()
            return

        @pl.when(p.inner)
        def _():
            self._over().wait_send()

        @pl.when(jnp.logical_not(p.inner))
        def _():
            self._inward().wait_send()

        self._pair().wait_send()


class Vectors:
    def __init__(self, place, r):
        self.place, self.r = place, r

    def _within(self):
        r = self.r
        most = r.vector_back.at[pl.ds(0, r.vector_back.shape[0] - 1)]
        return remote(
            most, most, r.vector_sent.at[1], r.vector_arrived.at[1], self.place.along_y
        )

    def _between(self):
        r = self.r
        most = r.task_slots.at[pl.ds(0, r.task_slots.shape[0] - 1)]
        return remote(
            most, most, r.vector_sent.at[2], r.vector_arrived.at[2], self.place.sibling
        )

    def spread(self):
        p, r = self.place, self.r
        groups = r.vector_back.shape[0]
        r.vector_back[p.feat] = r.vector_sums[...]
        for shift in range(1, groups):
            remote(
                r.vector_sums, r.vector_back.at[p.feat],
                r.vector_sent.at[1], r.vector_arrived.at[1], (p.task, p.peer(shift, groups)),
            ).start()

    def gather(self):
        p, r = self.place, self.r
        self._within().wait_recv()
        total = r.vector_back[0]
        for index in range(1, r.vector_back.shape[0]):
            total = total + r.vector_back[index]
        r.vector_total[...] = total
        r.task_slots[p.task] = total
        for device in (p.sibling, p.along_x, (CORES * (1 - p.x) + 1 - p.c, p.feat)):
            remote(
                r.vector_total, r.task_slots.at[p.task],
                r.vector_sent.at[2], r.vector_arrived.at[2], device,
            ).start()

    def done(self):
        r = self.r
        self._between().wait_recv()
        total = r.task_slots[0]
        for index in range(1, r.task_slots.shape[0]):
            total = total + r.task_slots[index]
        r.o_vectors[...] = total

    def finish(self):
        self._within().wait_send()
        self._between().wait_send()


(
    START, ZERO0, ZERO, PARAMS, NORM0, NORM1, NEED_QUERY, NEED_KEY, NEED_VALUE, PROJ0, PROJ1,
    PROJ2, PROJT1, PAIR00, PAIR01, PAIR02, PAIR03, NEED_MERGE, MERGE0, PAIR10, PAIR11, PAIR12,
    PAIR13, MERGE1, NEED_PROJECT, NEED_MERGE_TWO, DENSE, NEED_EXPAND_LOW, NEED_SHRINK_LOW,
    NEED_SHRINK_HIGH, NEED_EXPAND_HIGH, DENSE_GRADS, FEATURE_GRADS, LAYER_END, MERGED0,
    BACK00, BACK01, BACK02, BACK03, MERGED1, BACK10, BACK11, BACK12, BACK13, LOW_GRADS,
    HIGH_GRADS, FIRST0, FIRST1, FIRST2, FIRST3, VECTORS_READY, END,
) = range(52)
NORM_POINTS = (NORM0, NORM1)
PROJECT_POINTS = (PROJ0, PROJ1, PROJ2)
UNTIL_POINTS = (NEED_QUERY, NEED_KEY, NEED_VALUE)
MERGE_POINTS = (MERGE0, MERGE1)
MERGED_POINTS = (MERGED0, MERGED1)
PAIR_POINTS = ((PAIR00, PAIR01, PAIR02, PAIR03), (PAIR10, PAIR11, PAIR12, PAIR13))
BACK_POINTS = ((BACK00, BACK01, BACK02, BACK03), (BACK10, BACK11, BACK12, BACK13))
FIRST_POINTS = (FIRST0, FIRST1, FIRST2, FIRST3)
QUERY, KEY, VALUE, MERGE_ONE, MERGE_TWO, PROJECT_TWO = range(6)
EXPAND_LOW, EXPAND_HIGH, SHRINK_LOW, SHRINK_HIGH = range(6, 10)
D_SHRINK_LOW, D_SHRINK_HIGH, D_EXPAND_LOW, D_EXPAND_HIGH = range(10, 14)
D_PROJECT_TWO, D_MERGE_TWO, D_MERGE_ONE, D_PROJECT_LOW, D_PROJECT_HIGH = range(14, 19)
VECTOR_SUMS = 19
WIDE = {
    KEY, MERGE_TWO, EXPAND_LOW, D_SHRINK_HIGH, D_EXPAND_LOW,
}
DIRECT = {
    QUERY, KEY, VALUE, SHRINK_HIGH, D_EXPAND_HIGH, D_PROJECT_TWO, D_PROJECT_LOW,
    D_PROJECT_HIGH,
}
UPSTREAM = {0: (0, 0), 1: (1, 9)}
SCHEDULE = {
    START: (
        (QUERY, Gather.start),
        (VALUE, Gather.start),
        (MERGE_ONE, Gather.start),
        (EXPAND_HIGH, Gather.start),
        (PROJECT_TWO, Gather.start),
        (SHRINK_LOW, Gather.start),
        (KEY, Gather.start),
        (SHRINK_HIGH, Gather.start),
        (MERGE_TWO, Gather.start),
        (EXPAND_LOW, Gather.start),
    ),
    ZERO: (
        (QUERY, Gather.along_y),
    ),
    PARAMS: (
        (VALUE, Gather.along_y),
        (MERGE_ONE, Gather.middle),
    ),
    NORM0: (
        (EXPAND_HIGH, Gather.middle),
    ),
    NORM1: (
        (PROJECT_TWO, Gather.middle),
    ),
    NEED_QUERY: (
        (SHRINK_LOW, Gather.middle),
        (QUERY, Gather.along_x),
        (VALUE, Gather.along_x),
        (KEY, Gather.along_y),
        (MERGE_ONE, Gather.outward),
        (SHRINK_HIGH, Gather.along_y),
        (MERGE_TWO, Gather.middle),
        (QUERY, Gather.core),
        (EXPAND_HIGH, Gather.outward),
        (EXPAND_LOW, Gather.middle),
    ),
    NEED_KEY: (
        (PROJECT_TWO, Gather.outward),
        (VALUE, Gather.core),
    ),
    NEED_VALUE: (
        (SHRINK_LOW, Gather.outward),
    ),
    PROJ0: (
        (MERGE_ONE, Gather.along_y),
        (KEY, Gather.core),
    ),
    PROJ1: (
        (EXPAND_HIGH, Gather.along_y),
    ),
    PROJ2: (
        (SHRINK_HIGH, Gather.along_x),
    ),
    PROJT1: (
        (PROJECT_TWO, Gather.along_x),
        (MERGE_TWO, Gather.along_y),
    ),
    PAIR00: (
        (MERGE_ONE, Gather.along_x),
        (MERGE_TWO, Gather.outward),
    ),
    PAIR01: (
        (PROJECT_TWO, Gather.along_y),
    ),
    PAIR02: (
        (EXPAND_HIGH, Gather.along_x),
        (SHRINK_LOW, Gather.along_y),
        (EXPAND_LOW, Gather.outward),
    ),
    NEED_MERGE: (
        (SHRINK_HIGH, Gather.core),
        (MERGE_ONE, Gather.core),
    ),
    PAIR11: (
        (EXPAND_HIGH, Gather.core),
        (SHRINK_LOW, Gather.along_x),
        (EXPAND_LOW, Gather.along_y),
    ),
    NEED_PROJECT: (
        (PROJECT_TWO, Gather.core),
        (MERGE_TWO, Gather.core),
    ),
    NEED_EXPAND_LOW: (
        (SHRINK_LOW, Gather.core),
        (EXPAND_LOW, Gather.core),
    ),
    DENSE_GRADS: (
        (D_EXPAND_LOW, Reduce.core),
        (D_SHRINK_LOW, Reduce.core),
        (D_SHRINK_HIGH, Reduce.core),
        (D_EXPAND_HIGH, Reduce.core),
    ),
    FEATURE_GRADS: (
        (D_EXPAND_LOW, Reduce.y),
    ),
    LAYER_END: (
        (D_PROJECT_TWO, Reduce.core),
        (D_MERGE_TWO, Reduce.core),
        (D_SHRINK_LOW, Reduce.x),
        (D_EXPAND_HIGH, Reduce.x),
        (D_SHRINK_HIGH, Reduce.y),
    ),
    BACK00: (
        (D_MERGE_TWO, Reduce.x),
        (D_PROJECT_TWO, Reduce.x),
    ),
    BACK01: (
        (D_EXPAND_LOW, Reduce.inward),
    ),
    BACK03: (
        (D_SHRINK_LOW, Reduce.y),
    ),
    MERGED1: (
        (D_MERGE_ONE, Reduce.core),
    ),
    BACK10: (
        (D_MERGE_ONE, Reduce.x),
    ),
    BACK12: (
        (D_PROJECT_LOW, Reduce.x),
        (D_EXPAND_LOW, Reduce.over),
    ),
    LOW_GRADS: (
        (D_PROJECT_LOW, Reduce.core),
        (D_EXPAND_HIGH, Reduce.y),
        (D_SHRINK_HIGH, Reduce.inward),
        (D_MERGE_TWO, Reduce.y),
    ),
    HIGH_GRADS: (
        (D_PROJECT_HIGH, Reduce.core),
    ),
    FIRST0: (
        (D_SHRINK_LOW, Reduce.inward),
        (D_SHRINK_HIGH, Reduce.over),
        (D_PROJECT_HIGH, Reduce.x),
    ),
    FIRST1: (
        (D_PROJECT_TWO, Reduce.y),
        (D_EXPAND_LOW, Reduce.pair),
        (D_EXPAND_HIGH, Reduce.inward),
    ),
    FIRST2: (
        (D_MERGE_TWO, Reduce.inward),
        (D_SHRINK_LOW, Reduce.over),
        (D_MERGE_ONE, Reduce.y),
    ),
    FIRST3: (
        (D_SHRINK_HIGH, Reduce.pair),
        (D_EXPAND_LOW, Reduce.twins),
    ),
    VECTORS_READY: ((VECTOR_SUMS, Vectors.spread),),
    END: (
        (VECTOR_SUMS, Vectors.gather),
        (D_MERGE_TWO, Reduce.over),
        (D_SHRINK_LOW, Reduce.pair),
        (D_EXPAND_HIGH, Reduce.twins),
        (D_MERGE_ONE, Reduce.inward),
        (D_SHRINK_HIGH, Reduce.twins),
        (D_PROJECT_TWO, Reduce.inward),
        (D_PROJECT_LOW, Reduce.y),
        (D_PROJECT_HIGH, Reduce.y),
        (D_MERGE_TWO, Reduce.pair),
        (D_SHRINK_LOW, Reduce.twins),
        (D_EXPAND_LOW, Reduce.share),
        (D_MERGE_ONE, Reduce.over),
        (D_EXPAND_HIGH, Reduce.share),
        (D_PROJECT_LOW, Reduce.inward),
        (D_SHRINK_HIGH, Reduce.share),
        (D_SHRINK_LOW, Reduce.share),
        (D_PROJECT_TWO, Reduce.twins),
        (D_MERGE_TWO, Reduce.twins),
        (D_PROJECT_HIGH, Reduce.inward),
        (D_MERGE_ONE, Reduce.pair),
        (D_PROJECT_LOW, Reduce.twins),
        (D_PROJECT_TWO, Reduce.share),
        (D_MERGE_TWO, Reduce.share),
        (D_MERGE_ONE, Reduce.twins),
        (D_PROJECT_HIGH, Reduce.twins),
        (D_PROJECT_LOW, Reduce.share),
        (D_MERGE_ONE, Reduce.share),
        (D_PROJECT_HIGH, Reduce.share),
    ),
}


def flat(ref):
    return ref[...].reshape(-1, ref.shape[-1])


def fused_kernel(names, *refs):
    r = types.SimpleNamespace(**dict(zip(names, refs)))
    p = Place()
    tasks, samples, width = r.tokens.shape
    groups = r.hidden_in.shape[0]
    members = r.task_slots.shape[0]
    block_rows = samples // groups
    hidden_units = r.w_expand.shape[-1]
    chunk = 256
    head_scale = (width // HEADS) ** (-0.5)
    pairs = width // PAIR
    parts = samples // PAIR

    entry = pltpu.get_barrier_semaphore()
    for shift in range(1, groups):
        pl.semaphore_signal(
            entry, inc=1, device_id=(p.task, p.peer(shift, groups)), device_id_type=MESH
        )
    for shift in range(1, members):
        pl.semaphore_signal(
            entry, inc=1, device_id=(lax.rem(p.task + shift, members), p.feat),
            device_id_type=MESH,
        )
    pl.semaphore_wait(entry, groups + members - 2)

    third = width
    gathers = []

    def gather(name, rows=None, columns=None, wide=False, direct=False):
        shard, weight = getattr(r, "s_" + name), getattr(r, "w_" + name)
        if rows is not None:
            shard, weight = shard.at[:, pl.ds(*rows), :], weight.at[:, :, :, pl.ds(*rows), :]
        if columns is not None:
            shard = shard.at[:, :, pl.ds(*columns)]
            weight = weight.at[:, :, :, :, pl.ds(*columns)]
        item = Gather(
            p, len(gathers), shard, weight, r.gather_sent, r.gather_arrived, r.gather_local,
            wide, direct,
        )
        gathers.append(item)
        return item

    deep = r.w_shrink.shape[3] // 2
    half_units = hidden_units // 2
    items = {}
    for index, name, rows, columns in (
        (QUERY, "project_one", None, (0, third)),
        (KEY, "project_one", None, (third, third)),
        (VALUE, "project_one", None, (2 * third, third)),
        (MERGE_ONE, "merge_one", None, None),
        (MERGE_TWO, "merge_two", None, None),
        (PROJECT_TWO, "project_two", None, None),
        (EXPAND_LOW, "expand", None, (0, half_units)),
        (EXPAND_HIGH, "expand", None, (half_units, half_units)),
        (SHRINK_LOW, "shrink", (0, deep), None),
        (SHRINK_HIGH, "shrink", (deep, deep), None),
    ):
        items[index] = gather(name, rows, columns, index in WIDE, index in DIRECT)
    dense_items = (EXPAND_LOW, SHRINK_LOW, SHRINK_HIGH, EXPAND_HIGH)

    def run(point):
        for name, stage in SCHEDULE.get(point, ()):
            stage(items[name])

    def vectors_in():
        most = r.vector_slots.at[pl.ds(0, groups - 1)]
        return remote(most, most, r.vector_sent.at[0], r.vector_arrived.at[0], p.along_y)

    own_vectors = pltpu.make_async_copy(
        r.vectors, r.vector_slots.at[p.feat], r.vector_local.at[0]
    )
    own_vectors.start()
    for shift in range(1, groups):
        remote(
            r.vectors, r.vector_slots.at[p.feat], r.vector_sent.at[0], r.vector_arrived.at[0],
            (p.task, p.peer(shift, groups)),
        ).start()
    run(START)

    def spread(source, target, task, sent, arrived, local):
        def own():
            return pltpu.make_async_copy(
                source.at[task, pl.ds(p.feat * block_rows, block_rows)],
                target.at[p.feat, task], local.at[task],
            )

        def all_of():
            most = target.at[pl.ds(0, groups - 1), task]
            return remote(most, most, sent.at[task], arrived.at[task], p.along_y)

        def start():
            own().start()
            for shift in range(1, groups):
                peer = p.peer(shift, groups)
                remote(
                    source.at[task, pl.ds(peer * block_rows, block_rows)],
                    target.at[p.feat, task], sent.at[task], arrived.at[task], (p.task, peer),
                ).start()

        def wait():
            own().wait()
            all_of().wait_recv()

        def finish():
            all_of().wait_send()

        return types.SimpleNamespace(start=start, wait=wait, finish=finish)

    upstream = [
        spread(
            r.upstream, r.upstream_in, task, r.upstream_sent, r.upstream_arrived,
            r.upstream_local,
        )
        for task in range(tasks)
    ]
    hidden = [
        spread(
            r.grad_mixed, r.hidden_in, task, r.hidden_sent, r.hidden_arrived, r.hidden_local
        )
        for task in range(tasks)
    ]

    for ref in (r.t_project_two, r.t_merge_two, r.vector_sums, r.t_expand, r.t_shrink):
        ref[...] = jnp.zeros_like(ref)
        if ref is r.vector_sums:
            run(ZERO0)
    run(ZERO)
    own_vectors.wait()
    vectors_in().wait_recv()
    lane = lax.broadcasted_iota(jnp.int32, (1, PAIR), 1)
    per_slot = r.vector_slots.shape[1:]
    turned = [pltpu.roll(r.vector_slots[index], PAIR // 2, 1) for index in range(groups)]
    whole = [r.vector_slots[index] for index in range(groups)]
    bias_tiles = hidden_units // groups // PAIR
    for row in range(7):
        tile = bias_tiles + row // 2
        for at in range(groups // 2):
            first = (turned if row % 2 else whole)[2 * at][tile : tile + 1]
            second = (whole if row % 2 else turned)[2 * at + 1][tile : tile + 1]
            r.params[pl.ds(row, 1), pl.ds(at * PAIR, PAIR)] = jnp.where(
                lane < PAIR // 2, first, second
            )
    for at in range(groups * bias_tiles):
        row, tile = divmod(at, width // PAIR)
        r.params[pl.ds(7 + row, 1), pl.ds(tile * PAIR, PAIR)] = whole[at // bias_tiles][
            at % bias_tiles : at % bias_tiles + 1
        ]
    run(PARAMS)

    def param(row):
        return r.params[pl.ds(row, 1), :]

    def add_vector(row, value):
        r.vector_sums[pl.ds(row, 1), :] += jnp.sum(value, axis=0, keepdims=True)

    def norm_one(task):
        for start in range(0, samples, chunk):
            rows = r.tokens[task, pl.ds(start, chunk), :].astype(F32)
            normed = normalise(rows)[0] * param(0) + param(1)
            r.normed_one[task, pl.ds(start, chunk), :] = normed.astype(BF16)

    for task in range(tasks):
        norm_one(task)
        run(NORM_POINTS[task])

    def key_bias(task):
        keys = lax.broadcasted_iota(jnp.int32, (samples, 1), 0)
        return jnp.where(keys < r.counts[task], 0.0, MASKED)

    def live_rows(task, start):
        at = lax.broadcasted_iota(jnp.int32, (chunk, 1), 0) + start
        return jnp.where(at < r.counts[task], 1.0, 0.0)

    def at_pair(pair, points):
        for at, point in enumerate(points):
            if point in SCHEDULE:
                pl.when(pair == at)(functools.partial(run, point))

    def attend_pairs(task, points):
        bias = key_bias(task)

        def one_pair(pair, carry):
            lanes = pl.multiple_of(pair * PAIR, PAIR)
            key = r.triple[task, :, pl.ds(lanes + width, PAIR)]
            value_turned = r.triple[task, :, pl.ds(lanes + 2 * width, PAIR)].T
            for at in range(parts):
                query = r.triple[task, pl.ds(at * PAIR, PAIR), pl.ds(lanes, PAIR)]
                mixed, log_total = attend(query, key, value_turned, bias, head_scale)
                r.mixed_one[task, pl.ds(at * PAIR, PAIR), pl.ds(lanes, PAIR)] = mixed.astype(BF16)
                r.logs_one[pl.ds((task * pairs + pair) * parts + at, 1), :] = log_total
            for later, (on, at) in UPSTREAM.items():
                if on == task and at < pairs:
                    pl.when(pair == at)(upstream[later].start)
            at_pair(pair, points)
            return carry

        lax.fori_loop(0, pairs, one_pair, 0)

    def project(task, part):
        weight = r.w_project_one[:, :, :, :, pl.ds(part * width, width)].reshape(width, width)
        for start in range(0, samples, chunk):
            normed = r.normed_one[task, pl.ds(start, chunk), :]
            r.triple[task, pl.ds(start, chunk), pl.ds(part * width, width)] = nn(
                normed, weight
            ).astype(BF16)

    for name, part in ((QUERY, 0), (KEY, 1), (VALUE, 2)):
        run(UNTIL_POINTS[part])
        items[name].done()
        project(0, part)
        run(PROJECT_POINTS[part])
    for task in range(tasks):
        if task > 0:
            for part in range(3):
                project(task, part)
            run(PROJT1)
        attend_pairs(task, PAIR_POINTS[task])
        if task == 0:
            run(NEED_MERGE)
            items[MERGE_ONE].done()
        for start in range(0, samples, chunk):
            rows = r.tokens[task, pl.ds(start, chunk), :].astype(F32)
            merged = nn(r.mixed_one[task, pl.ds(start, chunk), :], flat(r.w_merge_one))
            summed = rows + live_rows(task, start) * merged
            r.grad_mixed[task, pl.ds(start, chunk), :] = summed.astype(BF16)
        hidden[task].start()
        for later, (on, at) in UPSTREAM.items():
            if on == task and at >= pairs:
                upstream[later].start()
        run(MERGE_POINTS[task])

    size = groups * GROUP
    blocks = chunk // size
    piece = blocks * GROUP
    per_task = block_rows // piece

    def own_piece(source, target, task, start, semaphore):
        return pltpu.make_async_copy(
            source.at[p.feat, task, pl.ds(start, piece)],
            target.at[task, pl.ds(p.feat * block_rows + start, piece)], semaphore,
        )

    def send_back(source, target, task, start, sent, arrived, local):
        own_piece(source, target, task, start, local).start()
        for shift in range(1, groups):
            peer = p.peer(shift, groups)
            remote(
                source.at[peer, task, pl.ds(start, piece)],
                target.at[task, pl.ds(p.feat * block_rows + start, piece)],
                sent, arrived, (p.task, peer),
            ).start()

    def send_out(task, begin):
        send_back(
            r.upstream_in, r.layer_out, task, begin,
            r.out_sent.at[0], r.out_arrived.at[0], r.out_local.at[0],
        )

    reductions = []

    def reduction(name, total, staged):
        index = len(reductions)
        item = Reduce(
            p, index, total, staged,
            [getattr(r, "m%d_%s" % (index, kind), None) for kind in BUFFERS],
            r.reduce_sent, r.reduce_arrived, name in WIDE, name in DIRECT,
        )
        reductions.append(item)
        return item

    def part_of(ref, rows=None, columns=None):
        if rows is not None:
            return ref.at[:, :, :, pl.ds(*rows), :]
        return ref.at[:, :, :, :, pl.ds(*columns)]

    for at, index in enumerate((D_SHRINK_LOW, D_SHRINK_HIGH)):
        cut = (at * deep, deep)
        items[index] = reduction(index, part_of(r.t_shrink, cut), part_of(r.w_shrink, cut))
    for at, index in enumerate((D_EXPAND_LOW, D_EXPAND_HIGH)):
        cut = (at * half_units, half_units)
        items[index] = reduction(
            index, part_of(r.t_expand, None, cut), part_of(r.w_expand, None, cut)
        )
    for index, total, staged in (
        (D_PROJECT_TWO, r.t_project_two, r.w_project_two),
        (D_MERGE_TWO, r.t_merge_two, r.w_merge_two),
        (D_MERGE_ONE, r.t_merge_one, r.w_merge_one),
        (D_PROJECT_LOW, r.t_low, r.b_low), (D_PROJECT_HIGH, r.t_high, r.b_high),
    ):
        items[index] = reduction(index, total, staged)

    def layer_chunk(step, carry):
        task = lax.div(step, per_task)
        begin = pl.multiple_of(lax.rem(step, per_task) * piece, piece)

        first = step == 0
        final = step == tasks * per_task - 1

        @pl.when(first)
        def _():
            run(NEED_PROJECT)
            items[PROJECT_TWO].done()
            hidden[0].wait()

        for later in range(1, tasks):
            @pl.when(step == later * per_task)
            def _():
                hidden[later].wait()

        def load(ref):
            pieces = [
                ref[:, task, pl.ds(begin + block * GROUP, GROUP), :].reshape(size, width)
                for block in range(blocks)
            ]
            return pieces[0] if blocks == 1 else jnp.concatenate(pieces, axis=0)

        def store(ref, values):
            for block in range(blocks):
                part = values[block * size : (block + 1) * size].reshape(groups, GROUP, width)
                ref[:, task, pl.ds(begin + block * GROUP, GROUP), :] = part

        row = lax.broadcasted_iota(jnp.int32, (chunk, 1), 0)
        row = (row // size) * GROUP + row % GROUP + begin + p.feat * block_rows
        live = jnp.where(row < r.counts[task], 1.0, 0.0)

        hidden_one = load(r.hidden_in).astype(F32)
        unit_two, scale_two = normalise(hidden_one)
        normed_two = (unit_two * param(2) + param(3)).astype(BF16)
        r.part_triple[...] = nn(normed_two, flat(r.w_project_two)).astype(BF16)
        reach = min(PAIR, size)
        key_at = lax.broadcasted_iota(jnp.int32, (size, 2 * reach), 0) % GROUP
        query_at = lax.broadcasted_iota(jnp.int32, (size, 2 * reach), 1) % GROUP
        bias = jnp.where(key_at == query_at, 0.0, MASKED)
        for block in range(blocks):
            where = pl.ds(block * size, size)
            for pair in range(pairs):
                lanes = pair * PAIR
                key = r.part_triple[where, pl.ds(width + lanes, PAIR)]
                value_turned = r.part_triple[where, pl.ds(2 * width + lanes, PAIR)].T
                query = r.part_triple[where, pl.ds(lanes, PAIR)]
                result, log_total = attend(query, key, value_turned, bias, head_scale)
                r.block_mixed[where, pl.ds(lanes, PAIR)] = result.astype(BF16)
                r.block_logs[pl.ds(block * pairs + pair, 1), :] = log_total

        @pl.when(first)
        def _():
            run(NEED_MERGE_TWO)
            items[MERGE_TWO].done()

        hidden_two = hidden_one + live * nn(r.block_mixed[...], flat(r.w_merge_two))
        unit_three, scale_three = normalise(hidden_two)
        normed_three = (unit_three * param(4) + param(5)).astype(BF16)
        @pl.when(first)
        def _():
            run(DENSE)
            upstream[0].wait()

        for later in range(1, tasks):
            @pl.when(step == later * per_task)
            def _():
                upstream[later].wait()

        flow = load(r.upstream_in).astype(F32)
        grad_dense = (flow * live).astype(BF16)
        add_vector(6, grad_dense.astype(F32))

        @pl.when(first)
        def _():
            run(NEED_EXPAND_LOW)
            items[EXPAND_LOW].done()
            run(NEED_SHRINK_LOW)
            items[SHRINK_LOW].done()
            run(NEED_SHRINK_HIGH)
            items[SHRINK_HIGH].done()

        dense = None
        incoming = None
        lanes = hidden_units // DEPTH
        for turn in range(DEPTH):
            cut = pl.ds(turn * lanes, lanes)
            if turn == DEPTH // 2:
                @pl.when(first)
                def _():
                    run(NEED_EXPAND_HIGH)
                    items[EXPAND_HIGH].done()

            up_weight = r.w_expand[:, :, :, :, cut].reshape(width, lanes)
            down_weight = r.w_shrink[turn].reshape(lanes, width)
            expanded = nn(normed_three, up_weight) + param(7 + turn)
            square = expanded * expanded
            steep = 0.7978845608028654
            bend = jnp.tanh(expanded * (steep + (steep * 0.044715) * square))
            half_up = 0.5 + 0.5 * bend
            activated = (expanded * half_up).astype(BF16)
            slope = half_up + (0.5 * expanded) * (1.0 - bend * bend) * (
                steep + (3.0 * steep * 0.044715) * square
            )
            grad_expanded = (slope * nt(grad_dense, down_weight)).astype(BF16)
            add_vector(7 + turn, grad_expanded.astype(F32))
            r.t_shrink[turn] += tn(activated, grad_dense).reshape(r.t_shrink.shape[1:])
            r.t_expand[:, :, :, :, cut] += tn(normed_three, grad_expanded).reshape(
                r.t_expand.shape[:4] + (lanes,)
            )
            up = nn(activated, down_weight)
            down = nt(grad_expanded, up_weight)
            dense = up if dense is None else dense + up
            incoming = down if incoming is None else incoming + down
        @pl.when(final)
        def _():
            for name in dense_items:
                items[name].finish()
            run(DENSE_GRADS)

        result = hidden_two + live * (dense + param(6))
        store(r.upstream_in, result.astype(BF16))

        add_vector(4, incoming * unit_three)
        add_vector(5, incoming)
        flow = flow + normalise_back(incoming, unit_three, scale_three, param(4))
        branch = (flow * live).astype(BF16)
        r.t_merge_two[...] += tn(r.block_mixed[...], branch).reshape(r.t_merge_two.shape)
        r.block_grad[...] = nt(branch, flat(r.w_merge_two)).astype(BF16)

        @pl.when(final)
        def _():
            run(FEATURE_GRADS)

        for block in range(blocks):
            where = pl.ds(block * size, size)
            for pair in range(pairs):
                lanes = pair * PAIR
                key = r.part_triple[where, pl.ds(width + lanes, PAIR)]
                value = r.part_triple[where, pl.ds(2 * width + lanes, PAIR)]
                query = r.part_triple[where, pl.ds(lanes, PAIR)]
                grad_query, grad_key, grad_value = attend_back(
                    query, key, value, key.T, r.block_mixed[where, pl.ds(lanes, PAIR)],
                    r.block_grad[where, pl.ds(lanes, PAIR)], r.block_logs[pl.ds(block * pairs + pair, 1), :], bias, head_scale,
                )
                r.part_triple[where, pl.ds(lanes, PAIR)] = grad_query.astype(BF16)
                r.part_triple[where, pl.ds(width + lanes, PAIR)] = grad_key.astype(BF16)
                r.part_triple[where, pl.ds(2 * width + lanes, PAIR)] = grad_value.astype(BF16)
        grad_triple = r.part_triple[...]
        r.t_project_two[...] += tn(normed_two, grad_triple).reshape(r.t_project_two.shape)
        incoming = nt(grad_triple, flat(r.w_project_two))
        add_vector(2, incoming * unit_two)
        add_vector(3, incoming)
        flow = flow + normalise_back(incoming, unit_two, scale_two, param(2))
        store(r.hidden_in, flow.astype(BF16))
        send_back(
            r.hidden_in, r.flow, task, begin,
            r.flow_sent.at[0], r.flow_arrived.at[task], r.flow_local.at[task],
        )

        @pl.when(task < tasks - 1)
        def _():
            send_out(task, begin)

        return carry

    lax.fori_loop(0, tasks * per_task, layer_chunk, 0)

    for name in (QUERY, KEY, VALUE, MERGE_ONE, PROJECT_TWO, MERGE_TWO):
        items[name].finish()
    for task in range(tasks):
        hidden[task].finish()
    run(LAYER_END)

    def flow_in(task):
        most = r.flow.at[task, pl.ds(0, samples - block_rows)]
        return remote(most, most, r.flow_sent.at[0], r.flow_arrived.at[task], p.along_y)

    def wait_flow(task):
        flow_in(task).wait_recv()
        own = r.flow.at[task, pl.ds(0, block_rows)]
        pltpu.make_async_copy(own, own, r.flow_local.at[task]).wait()

    def merge_back(task):
        for start in range(0, samples, chunk):
            live = live_rows(task, start)
            branch = (r.flow[task, pl.ds(start, chunk), :].astype(F32) * live).astype(BF16)
            part = tn(r.mixed_one[task, pl.ds(start, chunk), :], branch)
            part = part.reshape(r.t_merge_one.shape)
            if task == 0 and start == 0:
                r.t_merge_one[...] = part
            else:
                r.t_merge_one[...] += part
            r.grad_mixed[task, pl.ds(start, chunk), :] = nt(branch, flat(r.w_merge_one)).astype(BF16)

    def attend_pairs_back(task, points):
        bias = key_bias(task)

        def one_pair(pair, carry):
            lanes = pl.multiple_of(pair * PAIR, PAIR)
            key = r.triple[task, :, pl.ds(lanes + width, PAIR)]
            value = r.triple[task, :, pl.ds(lanes + 2 * width, PAIR)]
            key_turned = key.T
            for at in range(parts):
                query = r.triple[task, pl.ds(at * PAIR, PAIR), pl.ds(lanes, PAIR)]
                grad_out = r.grad_mixed[task, pl.ds(at * PAIR, PAIR), pl.ds(lanes, PAIR)]
                log_total = r.logs_one[pl.ds((task * pairs + pair) * parts + at, 1), :]
                grad_query, grad_key, grad_value = attend_back(
                    query, key, value, key_turned,
                    r.mixed_one[task, pl.ds(at * PAIR, PAIR), pl.ds(lanes, PAIR)],
                    grad_out, log_total, bias, head_scale,
                )
                r.triple[task, pl.ds(at * PAIR, PAIR), pl.ds(lanes, PAIR)] = grad_query.astype(BF16)
                if at == 0:
                    r.slab[0, pl.ds(0, samples), :] = grad_key
                    r.slab[1, pl.ds(0, samples), :] = grad_value
                else:
                    r.slab[0, pl.ds(0, samples), :] += grad_key
                    r.slab[1, pl.ds(0, samples), :] += grad_value
            r.triple[task, :, pl.ds(lanes + width, PAIR)] = r.slab[0, pl.ds(0, samples), :].astype(BF16)
            r.triple[task, :, pl.ds(lanes + 2 * width, PAIR)] = r.slab[1, pl.ds(0, samples), :].astype(BF16)
            at_pair(pair, points)
            if task == tasks - 1:
                @pl.when(pair == half - 1)
                def _():
                    project_weight(0)
                    run(LOW_GRADS)

            return carry

        lax.fori_loop(0, pairs, one_pair, 0)

    def project_weight(which):
        ref = (r.t_low, r.t_high)[which]
        lanes = width // 2
        for third in range(3):
            cut = pl.ds(third * width + which * lanes, lanes)
            part = None
            for task in range(tasks):
                one = tn(r.normed_one[task], r.triple[task, :, cut])
                part = one if part is None else part + one
            ref[:, :, :, :, pl.ds(third * lanes, lanes)] = part.reshape(ref.shape[:4] + (lanes,))

    slabs = []

    def project_back(task, start):
        rows = r.tokens[task, pl.ds(start, chunk), :].astype(F32)
        normed, scale = normalise(rows)
        incoming = nt(r.triple[task, pl.ds(start, chunk), :], flat(r.w_project_one))
        add_vector(0, incoming * normed)
        add_vector(1, incoming)
        back = normalise_back(incoming, normed, scale, param(0))
        back = r.flow[task, pl.ds(start, chunk), :].astype(F32) + back
        tiles = width // PAIR
        slot = len(slabs) % 2
        if len(slabs) > 1:
            slabs[-2].wait()
        for tile in range(tiles):
            r.slab[slot, pl.ds(tile, chunk, stride=tiles), :] = back[
                :, tile * PAIR : (tile + 1) * PAIR
            ]
        copy = pltpu.make_async_copy(
            r.slab.at[slot], r.input_grad.at[task, pl.ds(start * tiles, chunk * tiles)],
            r.o_done.at[len(slabs)],
        )
        copy.start()
        slabs.append(copy)

    half = pairs // 2
    for task in range(tasks):
        wait_flow(task)
        merge_back(task)
        if task == 0:
            for start in range(0, block_rows, piece):
                send_out(tasks - 1, start)
        run(MERGED_POINTS[task])
        attend_pairs_back(task, BACK_POINTS[task])
    project_weight(1)
    run(HIGH_GRADS)
    for task in range(tasks):
        for start in range(0, samples, chunk):
            project_back(task, start)
            run(FIRST_POINTS[task * (samples // chunk) + start // chunk])

    items[VECTOR_SUMS] = Vectors(p, r)
    run(VECTORS_READY)
    run(END)
    written = list(slabs)

    def write(source, target):
        copy = pltpu.make_async_copy(source, target, r.o_done.at[len(written)])
        copy.start()
        written.append(copy)

    for name, target in (
        (D_SHRINK_LOW, r.o_shrink.at[:, pl.ds(0, deep), :]),
        (D_SHRINK_HIGH, r.o_shrink.at[:, pl.ds(deep, deep), :]),
        (D_EXPAND_LOW, r.o_expand.at[:, :, pl.ds(0, half_units)]),
        (D_EXPAND_HIGH, r.o_expand.at[:, :, pl.ds(half_units, half_units)]),
        (D_PROJECT_TWO, r.o_project_two), (D_MERGE_TWO, r.o_merge_two),
        (D_MERGE_ONE, r.o_merge_one),
    ):
        items[name].done()
        write(items[name].final, target)
    items[VECTOR_SUMS].done()
    lanes = width // 2
    for which in range(2):
        item = items[(D_PROJECT_LOW, D_PROJECT_HIGH)[which]]
        item.done()
        for part in range(3):
            write(
                item.final.at[:, :, pl.ds(part * lanes, lanes)],
                r.o_project_one.at[:, :, pl.ds(part * width + which * lanes, lanes)],
            )
    for copy in written[len(slabs) - 2 :]:
        copy.wait()

    vectors_in().wait_send()
    items[VECTOR_SUMS].finish()
    for task in range(tasks):
        upstream[task].finish()
    everywhere = r.flow.at[:, pl.ds(0, samples - block_rows)]
    remote(everywhere, everywhere, r.flow_sent.at[0], r.flow_arrived.at[0], p.along_y).wait_send()
    everywhere = r.layer_out.at[:, pl.ds(0, samples - block_rows)]
    both = remote(everywhere, everywhere, r.out_sent.at[0], r.out_arrived.at[0], p.along_y)
    both.wait_send()
    both.wait_recv()
    own = r.layer_out.at[:, pl.ds(0, block_rows)]
    pltpu.make_async_copy(own, own, r.out_local.at[0]).wait()
    for item in reductions:
        item.finish()


def finish_kernel(*refs):
    count = 9
    sources, targets = refs[:count], refs[count : count + 16]
    held = refs[count + 16 : 2 * count + 16]
    made = refs[2 * count + 16 : 2 * count + 22]
    read, written = refs[2 * count + 22 :]
    reads = [
        pltpu.make_async_copy(source, memory, read.at[at])
        for at, (source, memory) in enumerate(zip(sources, held))
    ]
    for copy in reads:
        copy.start()
    writes = []
    for at in range(2, 8):
        reads[at].wait()
        made[at - 2][...] = held[at][...].astype(F32)
        writes.append(pltpu.make_async_copy(made[at - 2], targets[at], written.at[at]))
        writes[-1].start()
    for at in range(2):
        reads[at].wait()
        writes.append(pltpu.make_async_copy(held[at], targets[at], written.at[at]))
        writes[-1].start()
    reads[8].wait()
    vectors_ref, small_to, bias_to = held[8], targets[8:15], targets[15]
    place = lax.axis_index("feat")
    width = vectors_ref.shape[1]
    size = small_to[0].shape[1]
    turned = pltpu.roll(vectors_ref[...], lax.rem(width - place * size, width), 1)
    for row, target in enumerate(small_to):
        target[...] = turned[row : row + 1, :size]
    size = bias_to.shape[1]
    per_row = width // size
    row = vectors_ref[pl.ds(len(small_to) + lax.div(place, per_row), 1), :]
    bias = row[:, :size]
    for at in range(1, per_row):
        bias = jnp.where(lax.rem(place, per_row) == at, row[:, at * size : (at + 1) * size], bias)
    bias_to[...] = bias
    for copy in writes:
        copy.wait()


def fused_body(tokens, cotangent, counts, *shards):
    (
        gain_one, shift_one, project_one, merge_one, gain_two, shift_two, project_two, merge_two,
        gain_three, shift_three, expand, bias_in, shrink, bias_out,
    ) = shards
    groups = lax.axis_size("feat")
    members = lax.axis_size("task")
    place = lax.axis_index("feat")
    tasks, samples, _, width = tokens.shape
    block_rows = samples // groups
    hidden_units = expand.shape[1]
    pairs = width // PAIR

    small = (
        gain_one, shift_one, gain_two, shift_two, gain_three, shift_three, bias_out,
    )
    length = sum(part.shape[0] for part in (bias_in,) + small)
    slots = -(-length // (8 * PAIR)) * 8
    vectors, low = None, 0
    for part in (bias_in,) + small:
        high = slots * PAIR - low - part.shape[0]
        moved = jnp.pad(part.astype(F32), (low, high))
        vectors = moved if vectors is None else vectors + moved
        low += part.shape[0]
    vectors = vectors.reshape(slots, PAIR)

    big = {
        "project_one": project_one, "merge_one": merge_one, "project_two": project_two,
        "merge_two": merge_two, "expand": expand, "shrink": shrink,
    }
    names, operands, specs = [], [], []

    def operand(name, value, spec):
        names.append(name)
        operands.append(value)
        specs.append(spec)

    any_spec = pl.BlockSpec(memory_space=pl.ANY)
    operand("counts", counts, SMEM)
    operand("tokens", tokens.reshape(tasks, samples, width), VMEM)
    operand("upstream", cotangent.reshape(tasks, samples, width), any_spec)
    operand("vectors", vectors, any_spec)
    shapes = {}
    for name, shard in big.items():
        rows, columns = shard.shape[0] // SPLIT, shard.shape[1]
        shapes[name] = (rows, columns)
        operand("s_" + name, shard.reshape(SPLIT, rows, columns), any_spec)

    outs, out_specs = [], []

    def output(name, dims, kind, spec):
        names.append(name)
        outs.append(shape(dims, kind))
        out_specs.append(spec)

    output("layer_out", (tasks, samples, width), BF16, any_spec)
    output("input_grad", (tasks, samples * width // PAIR, PAIR), F32, any_spec)
    for name in big:
        output("o_" + name, (SPLIT,) + shapes[name], BF16, any_spec)
    output("o_vectors", (VECTORS, width), F32, VMEM)

    scratch = []

    def memory(name, dims, kind):
        names.append(name)
        scratch.append(pltpu.VMEM(dims, kind))

    def semaphores(name, dims):
        names.append(name)
        scratch.append(pltpu.SemaphoreType.DMA(dims))

    for name in big:
        memory("w_" + name, (DEPTH, WIDE_Y, SPLIT) + shapes[name], BF16)
    for name in big:
        if name != "project_one":
            memory("t_" + name, (DEPTH, WIDE_Y, SPLIT) + shapes[name], F32)
    rows, columns = shapes["project_one"]
    for name in ("low", "high"):
        memory("t_" + name, (DEPTH, WIDE_Y, SPLIT, rows, columns // 2), F32)
        memory("b_" + name, (DEPTH, WIDE_Y, SPLIT, rows, columns // 2), BF16)
    rows, columns = shapes["shrink"]
    shrink_part = (rows // 2, columns)
    rows, columns = shapes["expand"]
    expand_part = (rows, columns // 2)
    rows, columns = shapes["project_one"]
    half_project = (rows, columns // 2)
    items = (
        (shrink_part, D_SHRINK_LOW), (shrink_part, D_SHRINK_HIGH),
        (expand_part, D_EXPAND_LOW), (expand_part, D_EXPAND_HIGH),
        (shapes["project_two"], D_PROJECT_TWO), (shapes["merge_two"], D_MERGE_TWO),
        (shapes["merge_one"], D_MERGE_ONE), (half_project, D_PROJECT_LOW),
        (half_project, D_PROJECT_HIGH),
    )
    for index, (dims, name) in enumerate(items):
        wide, direct = name in WIDE, name in DIRECT
        count = HALVES if wide else 1
        sizes = {
            "halves": (DEPTH, WIDE_Y, HALVES), "quarters": (DEPTH, WIDE_Y, 1),
            "lines": (DEPTH, count), "outer": (DEPTH - 1 if direct else 2, count),
            "crossed": (2, count), "paired": (count,), "final": (SPLIT,), "twin": (count,),
        }
        unused = {"quarters" if wide else "twin"}
        if direct:
            unused |= {"crossed", "paired"}
        for kind in BUFFERS:
            if kind not in unused:
                memory("m%d_%s" % (index, kind), sizes[kind] + dims, BF16)
    memory("vector_slots", (groups, slots, PAIR), F32)
    memory("params", (VECTORS, width), F32)
    memory("vector_sums", (VECTORS, width), F32)
    memory("vector_back", (groups, VECTORS, width), F32)
    memory("vector_total", (VECTORS, width), F32)
    memory("task_slots", (members, VECTORS, width), F32)
    memory("normed_one", (tasks, samples, width), BF16)
    memory("triple", (tasks, samples, 3 * width), BF16)
    memory("mixed_one", (tasks, samples, width), BF16)
    memory("logs_one", (tasks * pairs * (samples // PAIR), 2 * PAIR), F32)
    memory("grad_mixed", (tasks, samples, width), BF16)
    memory("flow", (tasks, samples, width), BF16)
    memory("hidden_in", (groups, tasks, block_rows, width), BF16)
    memory("upstream_in", (groups, tasks, block_rows, width), BF16)
    memory("part_triple", (256, 3 * width), BF16)
    memory("block_mixed", (256, width), BF16)
    memory("block_grad", (256, width), BF16)
    memory("block_logs", (8, 2 * PAIR), F32)
    memory("slab", (2, 256 * width // PAIR, PAIR), F32)
    semaphores("gather_sent", (10, 6))
    semaphores("gather_arrived", (10, 6))
    semaphores("gather_local", (10,))
    semaphores("reduce_sent", (len(items), 8))
    semaphores("reduce_arrived", (len(items), 8))
    for name in ("vector_sent", "vector_arrived"):
        semaphores(name, (3,))
    semaphores("vector_local", (1,))
    semaphores("o_done", (tasks * samples // 256 + 13,))
    for name in ("upstream", "hidden"):
        for kind in ("_sent", "_arrived", "_local"):
            semaphores(name + kind, (tasks,))
    semaphores("flow_sent", (1,))
    semaphores("flow_arrived", (tasks,))
    semaphores("flow_local", (tasks,))
    for kind in ("_sent", "_arrived", "_local"):
        semaphores("out" + kind, (1,))

    results = pl.pallas_call(
        functools.partial(fused_kernel, tuple(names)),
        in_specs=specs,
        out_specs=out_specs,
        out_shape=outs,
        scratch_shapes=scratch,
        compiler_params=pltpu.CompilerParams(
            vmem_limit_bytes=FUSED_LIMIT, collective_id=0, has_side_effects=True
        ),
        name="layer",
    )(*operands)
    outs = [
        shape((tasks, samples, width), BF16),
        shape((tasks, samples * width // PAIR, PAIR), F32),
    ]
    outs += [shape((SPLIT,) + shapes[name], F32) for name in big]
    outs += [shape((1, part.shape[0]), F32) for part in small]
    outs += [shape((1, bias_in.shape[0]), F32)]
    finished = pl.pallas_call(
        finish_kernel,
        in_specs=[any_spec] * len(results),
        out_specs=[any_spec] * (2 + len(big)) + [VMEM] * (len(small) + 1),
        out_shape=outs,
        scratch_shapes=[pltpu.VMEM(result.shape, result.dtype) for result in results]
        + [pltpu.VMEM(out.shape, F32) for out in outs[2 : 2 + len(big)]]
        + [pltpu.SemaphoreType.DMA((len(results),))] * 2,
        compiler_params=pltpu.CompilerParams(vmem_limit_bytes=FINISH_LIMIT),
        name="finish",
    )(*results)
    grads = {
        name: result.reshape(big[name].shape) for name, result in zip(big, finished[2:])
    }
    ends = [part.reshape(-1) for part in finished[2 + len(big):]]
    return (
        finished[0].reshape(tokens.shape), finished[1].reshape(tokens.shape),
        ends[0], ends[1], grads["project_one"], grads["merge_one"],
        ends[2], ends[3], grads["project_two"], grads["merge_two"],
        ends[4], ends[5], grads["expand"], ends[7], grads["shrink"], ends[6],
    )


def solution(mesh):
    wide = P("task", None, "feat", None)
    row, grid = P("feat"), P("feat", None)
    weights = (
        row, row, grid, grid, row, row, grid, grid, row, row, grid, row, grid, row,
    )
    fits = mesh.shape["feat"] == DEPTH * WIDE_Y and mesh.shape["task"] == CORES * HALVES
    return jax.shard_map(
        fused_body if fits else body,
        mesh=mesh,
        in_specs=(wide, wide, P("task")) + weights,
        out_specs=(wide, wide) + weights,
        check_vma=False,
    )
```

```python
import functools
import types

import jax
import jax.numpy as jnp
from jax import lax
from jax.experimental import pallas as pl
from jax.experimental.pallas import tpu as pltpu
from jax.sharding import PartitionSpec as P

HEADS = 8
NORM_EPS = 1e-05
MASKED = -1e30
PAIR = 128
GROUP = 16
F32 = jnp.float32
BF16 = jnp.bfloat16


def nt(left, right):
    return lax.dot_general(left, right, (((1,), (1,)), ((), ())), preferred_element_type=F32)


def tn(left, right):
    return lax.dot_general(left, right, (((0,), (0,)), ((), ())), preferred_element_type=F32)


def nn(left, right):
    return lax.dot_general(left, right, (((1,), (0,)), ((), ())), preferred_element_type=F32)


def normalise(values):
    center = values - jnp.mean(values, axis=-1, keepdims=True)
    spread = jnp.mean(center * center, axis=-1, keepdims=True)
    scale = lax.rsqrt(spread + NORM_EPS)
    return center * scale, scale


def normalise_back(incoming, normed, scale, gain):
    weighted = incoming * gain
    first = jnp.mean(weighted, axis=-1, keepdims=True)
    second = jnp.mean(weighted * normed, axis=-1, keepdims=True)
    return scale * (weighted - first - normed * second)


def head_masks(scale):
    lane = lax.broadcasted_iota(jnp.int32, (1, PAIR), 1)
    low = jnp.where(lane < PAIR // 2, scale, 0.0).astype(BF16)
    high = jnp.where(lane < PAIR // 2, 0.0, scale).astype(BF16)
    return low, high


def two_heads(rows, scale):
    low, high = head_masks(scale)
    return jnp.concatenate([rows * low, rows * high], axis=0)


def join_heads(turned, length):
    half = PAIR // 2
    joined = jnp.concatenate([turned[:half, :length], turned[half:, length:]], axis=0)
    return joined.T


def attend(query, key, value_turned, bias, head_scale):
    scores = nt(key, two_heads(query, head_scale)) + bias
    top = jnp.max(scores, axis=0, keepdims=True)
    expo = jnp.exp(scores - top)
    total = jnp.sum(expo, axis=0, keepdims=True)
    mixed = nn(value_turned, expo.astype(BF16)) * (1.0 / total)
    return join_heads(mixed, query.shape[0]), top + jnp.log(total)


def attend_back(
    query, key, value, key_turned, result, grad_out, log_total, bias, head_scale
):
    half = PAIR // 2
    product = (result.astype(F32) * grad_out.astype(F32)).T
    inner = jnp.concatenate(
        [
            jnp.sum(product[:half], axis=0, keepdims=True),
            jnp.sum(product[half:], axis=0, keepdims=True),
        ],
        axis=1,
    )
    queries = two_heads(query, head_scale)
    grads = two_heads(grad_out, 1.0)
    chances = jnp.exp(nt(key, queries) + bias - log_total)
    grad_scores = (chances * (nt(value, grads) - inner)).astype(BF16)
    grad_value = nn(chances.astype(BF16), grads)
    grad_key = nn(grad_scores, queries)
    grad_query = join_heads(nn(key_turned, grad_scores), query.shape[0]) * head_scale
    return grad_query, grad_key, grad_value


def sample_forward_kernel(
    counts_ref, tokens_ref, gain_ref, shift_ref, project_ref, merge_ref,
    triple_ref, mixed_ref, logs_ref, hidden_ref,
):
    count = counts_ref[pl.program_id(0)]
    samples, width = tokens_ref.shape[1:]
    chunk = min(256, samples)
    gain = gain_ref[...].astype(F32)
    shift = shift_ref[...].astype(F32)
    for start in range(0, samples, chunk):
        rows = tokens_ref[0, pl.ds(start, chunk), :].astype(F32)
        normed = (normalise(rows)[0] * gain + shift).astype(BF16)
        triple_ref[0, pl.ds(start, chunk), :] = nn(normed, project_ref[...]).astype(BF16)
    keys = lax.broadcasted_iota(jnp.int32, (samples, 1), 0)
    bias = jnp.where(keys < count, 0.0, MASKED)
    head_scale = (width // HEADS) ** (-0.5)
    pairs = width // PAIR

    def one_pair(pair, carry):
        lanes = pl.multiple_of(pair * PAIR, PAIR)
        key = triple_ref[0, :, pl.ds(lanes + width, PAIR)]
        value_turned = triple_ref[0, :, pl.ds(lanes + 2 * width, PAIR)].T
        for at in range(samples // PAIR):
            query = triple_ref[0, pl.ds(at * PAIR, PAIR), pl.ds(lanes, PAIR)]
            mixed, log_total = attend(query, key, value_turned, bias, head_scale)
            mixed_ref[0, pl.ds(at * PAIR, PAIR), pl.ds(lanes, PAIR)] = mixed.astype(BF16)
            logs_ref[0, pl.ds(pair * (samples // PAIR) + at, 1), :] = log_total
        return carry

    lax.fori_loop(0, pairs, one_pair, 0)
    for start in range(0, samples, chunk):
        rows = tokens_ref[0, pl.ds(start, chunk), :].astype(F32)
        at = lax.broadcasted_iota(jnp.int32, (chunk, 1), 0) + start
        live = jnp.where(at < count, 1.0, 0.0)
        merged = nn(mixed_ref[0, pl.ds(start, chunk), :], merge_ref[...])
        hidden_ref[0, pl.ds(start, chunk), :] = (rows + live * merged).astype(BF16)


def sample_backward_kernel(
    counts_ref, tokens_ref, gain_ref, shift_ref, project_ref, merge_ref,
    triple_ref, mixed_ref, logs_ref, flow_ref,
    input_grad_ref, project_grad_ref, merge_grad_ref, gain_grad_ref, shift_grad_ref,
    grad_mixed, grad_triple, key_sum, value_sum,
):
    task = pl.program_id(0)
    count = counts_ref[task]
    samples, width = tokens_ref.shape[1:]
    chunk = min(256, samples)
    gain = gain_ref[...].astype(F32)
    shift = shift_ref[...].astype(F32)

    @pl.when(task == 0)
    def _():
        project_grad_ref[...] = jnp.zeros_like(project_grad_ref)
        merge_grad_ref[...] = jnp.zeros_like(merge_grad_ref)
        gain_grad_ref[...] = jnp.zeros_like(gain_grad_ref)
        shift_grad_ref[...] = jnp.zeros_like(shift_grad_ref)

    for start in range(0, samples, chunk):
        at = lax.broadcasted_iota(jnp.int32, (chunk, 1), 0) + start
        live = jnp.where(at < count, 1.0, 0.0)
        branch = (flow_ref[0, pl.ds(start, chunk), :].astype(F32) * live).astype(BF16)
        merge_grad_ref[...] += tn(mixed_ref[0, pl.ds(start, chunk), :], branch)
        grad_mixed[pl.ds(start, chunk), :] = nt(branch, merge_ref[...]).astype(BF16)
    keys = lax.broadcasted_iota(jnp.int32, (samples, 1), 0)
    bias = jnp.where(keys < count, 0.0, MASKED)
    head_scale = (width // HEADS) ** (-0.5)
    pairs = width // PAIR

    def one_pair(pair, carry):
        lanes = pl.multiple_of(pair * PAIR, PAIR)
        key = triple_ref[0, :, pl.ds(lanes + width, PAIR)]
        value = triple_ref[0, :, pl.ds(lanes + 2 * width, PAIR)]
        key_turned = key.T
        for at in range(samples // PAIR):
            query = triple_ref[0, pl.ds(at * PAIR, PAIR), pl.ds(lanes, PAIR)]
            grad_out = grad_mixed[pl.ds(at * PAIR, PAIR), pl.ds(lanes, PAIR)]
            log_total = logs_ref[0, pl.ds(pair * (samples // PAIR) + at, 1), :]
            grad_query, grad_key, grad_value = attend_back(
                query, key, value, key_turned,
                mixed_ref[0, pl.ds(at * PAIR, PAIR), pl.ds(lanes, PAIR)],
                grad_out, log_total, bias, head_scale,
            )
            grad_triple[pl.ds(at * PAIR, PAIR), pl.ds(lanes, PAIR)] = grad_query.astype(BF16)
            if at == 0:
                key_sum[...] = grad_key
                value_sum[...] = grad_value
            else:
                key_sum[...] += grad_key
                value_sum[...] += grad_value
        grad_triple[:, pl.ds(lanes + width, PAIR)] = key_sum[...].astype(BF16)
        grad_triple[:, pl.ds(lanes + 2 * width, PAIR)] = value_sum[...].astype(BF16)
        return carry

    lax.fori_loop(0, pairs, one_pair, 0)
    for start in range(0, samples, chunk):
        rows = tokens_ref[0, pl.ds(start, chunk), :].astype(F32)
        normed, scale = normalise(rows)
        part = grad_triple[pl.ds(start, chunk), :]
        project_grad_ref[...] += tn((normed * gain + shift).astype(BF16), part)
        incoming = nt(part, project_ref[...])
        gain_grad_ref[...] += jnp.sum(incoming * normed, axis=0, keepdims=True)
        shift_grad_ref[...] += jnp.sum(incoming, axis=0, keepdims=True)
        back = normalise_back(incoming, normed, scale, gain)
        input_grad_ref[0, pl.ds(start, chunk), :] = (
            flow_ref[0, pl.ds(start, chunk), :].astype(F32) + back
        )


def block_kernel(
    rows_per_task, blocks,
    counts_ref, hidden_ref, upstream_ref,
    gain_two_ref, shift_two_ref, project_ref, merge_ref,
    gain_three_ref, shift_three_ref, expand_ref, bias_in_ref, shrink_ref, bias_out_ref,
    out_ref, flow_ref,
    gain_two_grad, shift_two_grad, project_grad, merge_grad,
    gain_three_grad, shift_three_grad, expand_grad, bias_in_grad, shrink_grad, bias_out_grad,
    triple, mixed, logs, grad_mixed, grad_triple, key_sum, value_sum,
):
    step = pl.program_id(0)
    place = lax.axis_index("feat")
    feats, _, width = hidden_ref.shape
    size = feats * GROUP
    rows = blocks * size
    hidden_units = expand_ref.shape[1]
    sums = (
        gain_two_grad, shift_two_grad, project_grad, merge_grad, gain_three_grad,
        shift_three_grad, expand_grad, bias_in_grad, shrink_grad, bias_out_grad,
    )

    @pl.when(step == 0)
    def _():
        for ref in sums:
            ref[...] = jnp.zeros_like(ref)

    def load(ref):
        pieces = [
            ref[:, pl.ds(block * GROUP, GROUP), :].reshape(size, width) for block in range(blocks)
        ]
        return pieces[0] if blocks == 1 else jnp.concatenate(pieces, axis=0)

    def store(ref, values):
        for block in range(blocks):
            piece = values[block * size : (block + 1) * size]
            ref[:, pl.ds(block * GROUP, GROUP), :] = piece.reshape(feats, GROUP, width)

    row = lax.broadcasted_iota(jnp.int32, (rows, 1), 0)
    row = (step * blocks + row // size) * GROUP + row % GROUP
    sample = place * rows_per_task + row % rows_per_task
    count = jnp.zeros_like(row)
    for task in range(counts_ref.shape[0]):
        count = jnp.where(row // rows_per_task == task, counts_ref[task], count)
    live = jnp.where(sample < count, 1.0, 0.0)

    gain_two = gain_two_ref[...].astype(F32)
    shift_two = shift_two_ref[...].astype(F32)
    gain_three = gain_three_ref[...].astype(F32)
    shift_three = shift_three_ref[...].astype(F32)
    hidden_one = load(hidden_ref).astype(F32)
    unit_two, scale_two = normalise(hidden_one)
    normed_two = (unit_two * gain_two + shift_two).astype(BF16)
    triple[...] = nn(normed_two, project_ref[...]).astype(BF16)

    reach = min(PAIR, size)
    key_at = lax.broadcasted_iota(jnp.int32, (size, 2 * reach), 0) % GROUP
    query_at = lax.broadcasted_iota(jnp.int32, (size, 2 * reach), 1) % GROUP
    bias = jnp.where(key_at == query_at, 0.0, MASKED)
    head_scale = (width // HEADS) ** (-0.5)
    parts = size // reach
    pairs = width // PAIR
    for block in range(blocks):
        start = block * size
        for pair in range(pairs):
            lanes = pair * PAIR
            key = triple[pl.ds(start, size), pl.ds(width + lanes, PAIR)]
            value_turned = triple[pl.ds(start, size), pl.ds(2 * width + lanes, PAIR)].T
            for part in range(parts):
                at = start + part * reach
                query = triple[pl.ds(at, reach), pl.ds(lanes, PAIR)]
                result, log_total = attend(query, key, value_turned, bias, head_scale)
                mixed[pl.ds(at, reach), pl.ds(lanes, PAIR)] = result.astype(BF16)
                logs[pl.ds((block * pairs + pair) * parts + part, 1), :] = log_total

    hidden_two = hidden_one + live * nn(mixed[...], merge_ref[...])
    unit_three, scale_three = normalise(hidden_two)
    normed_three = (unit_three * gain_three + shift_three).astype(BF16)
    upstream = load(upstream_ref).astype(F32)
    grad_dense = (upstream * live).astype(BF16)
    bias_out_grad[...] += jnp.sum(grad_dense.astype(F32), axis=0, keepdims=True)
    lanes = min(512, hidden_units)
    dense = None
    incoming = None
    for start in range(0, hidden_units, lanes):
        cut = pl.ds(start, lanes)
        expanded = nn(normed_three, expand_ref[:, cut]) + bias_in_ref[:, cut].astype(F32)
        square = expanded * expanded
        steep = 0.7978845608028654
        bend = jnp.tanh(expanded * (steep + (steep * 0.044715) * square))
        half_up = 0.5 + 0.5 * bend
        activated = (expanded * half_up).astype(BF16)
        slope = half_up + (0.5 * expanded) * (1.0 - bend * bend) * (
            steep + (3.0 * steep * 0.044715) * square
        )
        grad_expanded = (slope * nt(grad_dense, shrink_ref[cut, :])).astype(BF16)
        bias_in_grad[:, cut] += jnp.sum(grad_expanded.astype(F32), axis=0, keepdims=True)
        shrink_grad[cut, :] += tn(activated, grad_dense)
        expand_grad[:, cut] += tn(normed_three, grad_expanded)
        up = nn(activated, shrink_ref[cut, :])
        down = nt(grad_expanded, expand_ref[:, cut])
        dense = up if dense is None else dense + up
        incoming = down if incoming is None else incoming + down
    result = hidden_two + live * (dense + bias_out_ref[...].astype(F32))
    store(out_ref, result.astype(BF16))

    gain_three_grad[...] += jnp.sum(incoming * unit_three, axis=0, keepdims=True)
    shift_three_grad[...] += jnp.sum(incoming, axis=0, keepdims=True)
    flow_two = upstream + normalise_back(incoming, unit_three, scale_three, gain_three)
    branch = (flow_two * live).astype(BF16)
    merge_grad[...] += tn(mixed[...], branch)
    grad_mixed[...] = nt(branch, merge_ref[...]).astype(BF16)
    for block in range(blocks):
        start = block * size
        for pair in range(pairs):
            lanes = pair * PAIR
            key = triple[pl.ds(start, size), pl.ds(width + lanes, PAIR)]
            value = triple[pl.ds(start, size), pl.ds(2 * width + lanes, PAIR)]
            key_turned = key.T
            for part in range(parts):
                at = start + part * reach
                query = triple[pl.ds(at, reach), pl.ds(lanes, PAIR)]
                grad_out = grad_mixed[pl.ds(at, reach), pl.ds(lanes, PAIR)]
                log_total = logs[pl.ds((block * pairs + pair) * parts + part, 1), :]
                grad_query, grad_key, grad_value = attend_back(
                    query, key, value, key_turned, mixed[pl.ds(at, reach), pl.ds(lanes, PAIR)],
                    grad_out, log_total, bias, head_scale,
                )
                grad_triple[pl.ds(at, reach), pl.ds(lanes, PAIR)] = grad_query.astype(BF16)
                if part > 0:
                    grad_key += key_sum[...]
                    grad_value += value_sum[...]
                if part == parts - 1:
                    where = pl.ds(start, size)
                    grad_triple[where, pl.ds(width + lanes, PAIR)] = grad_key.astype(BF16)
                    grad_triple[where, pl.ds(2 * width + lanes, PAIR)] = grad_value.astype(BF16)
                else:
                    key_sum[...] = grad_key
                    value_sum[...] = grad_value
    project_grad[...] += tn(normed_two, grad_triple[...])
    incoming = nt(grad_triple[...], project_ref[...])
    gain_two_grad[...] += jnp.sum(incoming * unit_two, axis=0, keepdims=True)
    shift_two_grad[...] += jnp.sum(incoming, axis=0, keepdims=True)
    flow_one = flow_two + normalise_back(incoming, unit_two, scale_two, gain_two)
    store(flow_ref, flow_one.astype(BF16))


VMEM = pl.BlockSpec(memory_space=pltpu.VMEM)
SMEM = pl.BlockSpec(memory_space=pltpu.SMEM)
LIMIT = 56 * 1024 * 1024


def shape(dims, kind):
    return jax.ShapeDtypeStruct(dims, kind)


def by_task(*dims):
    return pl.BlockSpec((1,) + dims, lambda task: (task,) + (0,) * len(dims))


def body(tokens, cotangent, counts, *shards):
    groups = lax.axis_size("feat")
    tasks, samples, local, width = tokens.shape
    rows_per_task = samples // groups
    gathered = [lax.all_gather(part, "feat", axis=0, tiled=True) for part in shards]
    gathered = [part[None, :] if part.ndim == 1 else part for part in gathered]
    (
        gain_one, shift_one, project_one, merge_one, gain_two, shift_two, project_two, merge_two,
        gain_three, shift_three, expand, bias_in, shrink, bias_out,
    ) = gathered
    hidden_units = expand.shape[1]
    source = tokens.reshape(tasks, samples, width)

    def to_blocks(rows):
        rows = rows.reshape(tasks, groups, rows_per_task, width)
        rows = jnp.transpose(rows, (1, 0, 2, 3))
        rows = lax.all_to_all(rows, "feat", split_axis=0, concat_axis=0, tiled=True)
        return rows.reshape(groups, tasks * rows_per_task, width)

    def from_blocks(rows):
        rows = rows.reshape(groups, tasks, rows_per_task, width)
        rows = lax.all_to_all(rows, "feat", split_axis=0, concat_axis=0, tiled=True)
        rows = jnp.transpose(rows, (1, 0, 2, 3))
        return rows.reshape(tasks, samples, width)

    upstream = to_blocks(cotangent.reshape(tasks, samples, width))
    log_rows = samples * width // PAIR // PAIR
    triple, mixed, logs, hidden = pl.pallas_call(
        sample_forward_kernel,
        grid=(tasks,),
        in_specs=[SMEM, by_task(samples, width), VMEM, VMEM, VMEM, VMEM],
        out_specs=[
            by_task(samples, 3 * width), by_task(samples, width),
            by_task(log_rows, 2 * PAIR), by_task(samples, width),
        ],
        out_shape=[
            shape((tasks, samples, 3 * width), BF16),
            shape((tasks, samples, width), BF16),
            shape((tasks, log_rows, 2 * PAIR), F32),
            shape((tasks, samples, width), BF16),
        ],
        compiler_params=pltpu.CompilerParams(vmem_limit_bytes=LIMIT),
        name="sample_forward",
    )(counts, source, gain_one, shift_one, project_one, merge_one)

    hidden = to_blocks(hidden)
    all_rows = tasks * rows_per_task
    size = groups * GROUP
    blocks = max(1, min(all_rows // GROUP, 256 // size))
    steps = all_rows // (GROUP * blocks)
    rows = blocks * size
    slab = pl.BlockSpec((groups, GROUP * blocks, width), lambda step: (0, step, 0))
    reach = min(PAIR, size)
    pieces = blocks * (width // PAIR) * (size // reach)
    grads = [
        shape((1, width), F32), shape((1, width), F32),
        shape((width, 3 * width), F32), shape((width, width), F32),
        shape((1, width), F32), shape((1, width), F32),
        shape((width, hidden_units), F32), shape((1, hidden_units), F32),
        shape((hidden_units, width), F32), shape((1, width), F32),
    ]
    results = pl.pallas_call(
        functools.partial(block_kernel, rows_per_task, blocks),
        grid=(steps,),
        in_specs=[SMEM, slab, slab] + [VMEM] * 10,
        out_specs=[slab, slab] + [VMEM] * 10,
        out_shape=[shape((groups, all_rows, width), BF16)] * 2 + grads,
        scratch_shapes=[
            pltpu.VMEM((rows, 3 * width), BF16),
            pltpu.VMEM((rows, width), BF16),
            pltpu.VMEM((pieces, 2 * reach), F32),
            pltpu.VMEM((rows, width), BF16),
            pltpu.VMEM((rows, 3 * width), BF16),
            pltpu.VMEM((size, PAIR), F32),
            pltpu.VMEM((size, PAIR), F32),
        ],
        compiler_params=pltpu.CompilerParams(vmem_limit_bytes=LIMIT),
        name="block_layer",
    )(
        counts, hidden, upstream, gain_two, shift_two, project_two, merge_two,
        gain_three, shift_three, expand, bias_in, shrink, bias_out,
    )
    layer_out = from_blocks(results[0])
    flow = from_blocks(results[1])

    first = pl.pallas_call(
        sample_backward_kernel,
        grid=(tasks,),
        in_specs=[
            SMEM, by_task(samples, width), VMEM, VMEM, VMEM, VMEM,
            by_task(samples, 3 * width), by_task(samples, width),
            by_task(log_rows, 2 * PAIR), by_task(samples, width),
        ],
        out_specs=[by_task(samples, width), VMEM, VMEM, VMEM, VMEM],
        out_shape=[
            shape((tasks, samples, width), F32),
            shape((width, 3 * width), F32), shape((width, width), F32),
            shape((1, width), F32), shape((1, width), F32),
        ],
        scratch_shapes=[
            pltpu.VMEM((samples, width), BF16),
            pltpu.VMEM((samples, 3 * width), BF16),
            pltpu.VMEM((samples, PAIR), F32),
            pltpu.VMEM((samples, PAIR), F32),
        ],
        compiler_params=pltpu.CompilerParams(vmem_limit_bytes=LIMIT),
        name="sample_backward",
    )(
        counts, source, gain_one, shift_one, project_one, merge_one, triple, mixed, logs, flow,
    )
    (
        gain_two_grad, shift_two_grad, project_two_grad, merge_two_grad, gain_three_grad,
        shift_three_grad, expand_grad, bias_in_grad, shrink_grad, bias_out_grad,
    ) = results[2:]
    totals = (
        first[3], first[4], first[1], first[2], gain_two_grad, shift_two_grad, project_two_grad,
        merge_two_grad, gain_three_grad, shift_three_grad, expand_grad, bias_in_grad,
        shrink_grad, bias_out_grad,
    )
    totals = [part[0] if part.shape[0] == 1 else part for part in totals]
    totals = tuple(part.astype(BF16) for part in totals)
    totals = lax.psum_scatter(totals, "feat", scatter_dimension=0, tiled=True)
    totals = lax.psum(totals, "task")
    return (
        layer_out.reshape(tokens.shape),
        first[0].reshape(tokens.shape),
    ) + tuple(part.astype(F32) for part in totals)


FUSED_LIMIT = 62 * 1024 * 1024

MESH = pl.DeviceIdType.MESH
DEPTH, WIDE_Y, CORES, HALVES = 4, 2, 2, 2
SPLIT = CORES * HALVES
VECTORS = 16
FINISH_LIMIT = 56 * 1024 * 1024
BUFFERS = ("halves", "quarters", "lines", "outer", "crossed", "paired", "final", "twin")


def remote(source, target, sent, arrived, device):
    return pltpu.make_async_remote_copy(
        src_ref=source, dst_ref=target, send_sem=sent, recv_sem=arrived,
        device_id=device, device_id_type=MESH,
    )


class Place:
    def __init__(self):
        self.feat = lax.axis_index("feat")
        self.task = lax.axis_index("task")
        self.z = lax.div(self.feat, WIDE_Y)
        self.y = lax.rem(self.feat, WIDE_Y)
        self.x = lax.div(self.task, CORES)
        self.c = lax.rem(self.task, CORES)
        self.mine = HALVES * self.c + self.x
        self.theirs = HALVES * self.c + 1 - self.x
        self.below = HALVES * self.c
        self.other = HALVES * (1 - self.c)
        self.along_y = (self.task, WIDE_Y * self.z + 1 - self.y)
        self.along_x = (CORES * (1 - self.x) + self.c, self.feat)
        self.sibling = (CORES * self.x + 1 - self.c, self.feat)
        self.across = DEPTH - 1 - self.z
        self.near_low = 2 * lax.div(self.z, 2)
        self.far_low = 2 - self.near_low
        self.pair = 2 * self.near_low + 1 - self.z
        self.inner = jnp.logical_or(self.z == 1, self.z == 2)

    def along_z(self, shift):
        return lax.rem(self.z + shift, DEPTH)

    def at_z(self, z):
        return (self.task, WIDE_Y * z + self.y)

    def peer(self, shift, groups):
        return lax.rem(self.feat + shift, groups)


class Moves:
    def __init__(self, place, index, wide, sent, arrived, stages):
        self.place, self.wide = place, wide
        self.rows = pl.ds(place.below, HALVES) if wide else pl.ds(place.mine, 1)
        self.sent = [sent.at[index, stage] for stage in range(stages)]
        self.arrived = [arrived.at[index, stage] for stage in range(stages)]

    def move(self, stage, source, target, device):
        return remote(source, target, self.sent[stage], self.arrived[stage], device)


class Gather(Moves):
    def __init__(self, place, index, shard, weight, sent, arrived, local, wide=False, direct=False):
        super().__init__(place, index, wide, sent, arrived, 6)
        self.shard, self.weight, self.local, self.direct = shard, weight, local.at[index], direct

    def _own(self):
        p = self.place
        return pltpu.make_async_copy(
            self.shard.at[self.rows], self.weight.at[p.z, p.y, self.rows], self.local
        )

    def _pair(self, z_count):
        p = self.place
        part = self.weight.at[pl.ds(0, z_count), p.y, self.rows]
        return self.move(0, part, part, p.at_z(p.pair))

    def _far(self, stage, low, device):
        part = self.weight.at[pl.ds(low, 2), self.place.y, self.rows]
        return self.move(stage, part, part, device)

    def _along_y(self):
        p = self.place
        part = self.weight.at[:, p.y, self.rows]
        return self.move(3, part, part, p.along_y)

    def _along_x(self):
        p = self.place
        part = self.weight.at[:, :, self.rows]
        return self.move(4, part, part, p.along_x)

    def _across(self):
        p = self.place
        part = self.weight.at[:, :, pl.ds(p.below, HALVES)]
        return self.move(5, part, part, p.sibling)

    def start(self):
        p = self.place
        self._own().start()
        targets = [p.along_z(shift) for shift in range(1, DEPTH)] if self.direct else [p.pair]
        for z in targets:
            self.move(
                0, self.shard.at[self.rows], self.weight.at[p.z, p.y, self.rows], p.at_z(z)
            ).start()

    def middle(self):
        if self.direct:
            return
        p = self.place

        @pl.when(p.inner)
        def _():
            self._own().wait()
            self._pair(1).wait_recv()
            self._far(1, p.near_low, p.at_z(p.across)).start()

    def outward(self):
        if self.direct:
            return
        p = self.place

        @pl.when(p.inner)
        def _():
            self._far(1, p.far_low, p.at_z(p.across)).wait_recv()
            self._far(2, p.far_low, p.at_z(p.pair)).start()

    def along_y(self):
        p = self.place
        if self.direct:
            self._own().wait()
            self._pair(DEPTH - 1).wait_recv()
        else:
            @pl.when(jnp.logical_not(p.inner))
            def _():
                self._own().wait()
                self._pair(1).wait_recv()
                self._far(2, p.far_low, p.at_z(p.pair)).wait_recv()

        self._along_y().start()

    def along_x(self):
        if not self.wide:
            self._along_y().wait_recv()
            self._along_x().start()

    def core(self):
        if self.wide:
            self._along_y().wait_recv()
        else:
            self._along_x().wait_recv()
        self._across().start()

    def done(self):
        self._across().wait_recv()

    def finish(self):
        p = self.place
        if self.direct:
            self._pair(DEPTH - 1).wait_send()
        else:
            self._pair(1).wait_send()

            @pl.when(p.inner)
            def _():
                self._far(1, p.near_low, p.at_z(p.across)).wait_send()
                self._far(2, p.far_low, p.at_z(p.pair)).wait_send()

        self._along_y().wait_send()
        if not self.wide:
            self._along_x().wait_send()
        self._across().wait_send()


class Reduce(Moves):
    def __init__(
        self, place, index, total, staged, memory, sent, arrived, wide=False, direct=False
    ):
        super().__init__(place, index, wide, sent, arrived, 8)
        self.total, self.staged, self.direct = total, staged, direct
        (
            self.halves, self.quarters, self.lines, self.outer, self.crossed, self.paired,
            self.final, self.twin,
        ) = memory

    def _core(self):
        p = self.place
        return self.move(
            0, self.staged.at[:, :, pl.ds(p.other, HALVES)], self.halves, p.sibling
        )

    def _x(self):
        p = self.place
        return self.move(1, self.staged.at[:, :, pl.ds(p.theirs, 1)], self.quarters, p.along_x)

    def _y(self):
        p = self.place
        return self.move(2, self.staged.at[:, 1 - p.y, self.rows], self.lines, p.along_y)

    def _inward(self):
        p = self.place
        if self.direct:
            return self.move(3, self.outer, self.outer, p.at_z(p.pair))
        return self.move(
            3, self.staged.at[pl.ds(p.far_low, 2), p.y, self.rows], self.outer, p.at_z(p.pair)
        )

    def _over(self):
        p = self.place
        return self.move(
            4, self.staged.at[pl.ds(p.far_low, 2), p.y, self.rows], self.crossed, p.at_z(p.across)
        )

    def _pair(self):
        p = self.place
        return self.move(5, self.staged.at[p.pair, p.y, self.rows], self.paired, p.at_z(p.pair))

    def _twin(self):
        p = self.place
        part = self.final.at[self.rows]
        return self.move(6, part, self.twin if self.wide else part, p.along_x)

    def _across(self):
        p = self.place
        part = self.final.at[pl.ds(p.below, HALVES)]
        return self.move(7, part, part, p.sibling)

    def core(self):
        p = self.place

        def one(z, carry):
            cut = pl.ds(p.other, HALVES)
            self.staged[z, :, cut] = self.total[z, :, cut].astype(BF16)
            return carry

        lax.fori_loop(0, DEPTH, one, 0)
        self._core().start()

    def x(self):
        p = self.place
        if self.wide:
            return
        self._core().wait_recv()

        def one(z, carry):
            summed = self.total[z, :, p.theirs] + self.halves[z, :, 1 - p.x].astype(F32)
            self.staged[z, :, p.theirs] = summed.astype(BF16)
            return carry

        lax.fori_loop(0, DEPTH, one, 0)
        self._x().start()

    def y(self):
        p = self.place
        if self.wide:
            self._core().wait_recv()
        else:
            self._x().wait_recv()

        def one(z, carry):
            if self.wide:
                summed = self.total[z, :, self.rows] + self.halves[z].astype(F32)
            else:
                summed = self.total[z, :, self.rows] + self.halves[z, :, pl.ds(p.x, 1)].astype(F32)
                summed = summed + self.quarters[z].astype(F32)
            self.staged[z, :, self.rows] = summed.astype(BF16)
            return carry

        lax.fori_loop(0, DEPTH, one, 0)
        self._y().start()

    def inward(self):
        p = self.place
        self._y().wait_recv()

        def one(z, carry):
            summed = self.staged[z, p.y, self.rows].astype(F32) + self.lines[z].astype(F32)
            self.staged[z, p.y, self.rows] = summed.astype(BF16)
            return carry

        lax.fori_loop(0, DEPTH, one, 0)
        if self.direct:
            for shift in range(1, DEPTH):
                z = p.along_z(shift)
                self.move(
                    3, self.staged.at[z, p.y, self.rows], self.outer.at[shift - 1], p.at_z(z)
                ).start()
            return

        @pl.when(jnp.logical_not(p.inner))
        def _():
            self._inward().start()

    def over(self):
        p = self.place

        @pl.when(p.inner)
        def _():
            self._inward().wait_recv()
            for at in range(2):
                z = p.far_low + at
                summed = self.staged[z, p.y, self.rows].astype(F32) + self.outer[at].astype(F32)
                self.staged[z, p.y, self.rows] = summed.astype(BF16)
            self._over().start()

    def pair(self):
        p = self.place

        @pl.when(p.inner)
        def _():
            self._over().wait_recv()
            for at in range(2):
                z = p.near_low + at
                summed = self.staged[z, p.y, self.rows].astype(F32) + self.crossed[at].astype(F32)
                self.staged[z, p.y, self.rows] = summed.astype(BF16)

        self._pair().start()

    def twins(self):
        p = self.place
        summed = self.staged[p.z, p.y, self.rows].astype(F32)
        if self.direct:
            self._inward().wait_recv()
            for shift in range(DEPTH - 1):
                summed = summed + self.outer[shift].astype(F32)
        else:
            self._pair().wait_recv()
            summed = summed + self.paired[...].astype(F32)
        self.final[self.rows] = summed.astype(BF16)
        self._twin().start()

    def share(self):
        self._twin().wait_recv()
        if self.wide:
            self._twin().wait_send()
            summed = self.final[self.rows].astype(F32) + self.twin[...].astype(F32)
            self.final[self.rows] = summed.astype(BF16)
        self._across().start()

    def done(self):
        self._across().wait_recv()

    def finish(self):
        p = self.place
        self._core().wait_send()
        if not self.wide:
            self._x().wait_send()
            self._twin().wait_send()
        self._y().wait_send()
        self._across().wait_send()
        if self.direct:
            self._inward().wait_send()
            return

        @pl.when(p.inner)
        def _():
            self._over().wait_send()

        @pl.when(jnp.logical_not(p.inner))
        def _():
            self._inward().wait_send()

        self._pair().wait_send()


class Vectors:
    def __init__(self, place, r):
        self.place, self.r = place, r

    def _within(self):
        r = self.r
        most = r.vector_back.at[pl.ds(0, r.vector_back.shape[0] - 1)]
        return remote(
            most, most, r.vector_sent.at[1], r.vector_arrived.at[1], self.place.along_y
        )

    def _between(self):
        r = self.r
        most = r.task_slots.at[pl.ds(0, r.task_slots.shape[0] - 1)]
        return remote(
            most, most, r.vector_sent.at[2], r.vector_arrived.at[2], self.place.sibling
        )

    def spread(self):
        p, r = self.place, self.r
        groups = r.vector_back.shape[0]
        r.vector_back[p.feat] = r.vector_sums[...]
        for shift in range(1, groups):
            remote(
                r.vector_sums, r.vector_back.at[p.feat],
                r.vector_sent.at[1], r.vector_arrived.at[1], (p.task, p.peer(shift, groups)),
            ).start()

    def gather(self):
        p, r = self.place, self.r
        self._within().wait_recv()
        total = r.vector_back[0]
        for index in range(1, r.vector_back.shape[0]):
            total = total + r.vector_back[index]
        r.vector_total[...] = total
        r.task_slots[p.task] = total
        for device in (p.sibling, p.along_x, (CORES * (1 - p.x) + 1 - p.c, p.feat)):
            remote(
                r.vector_total, r.task_slots.at[p.task],
                r.vector_sent.at[2], r.vector_arrived.at[2], device,
            ).start()

    def done(self):
        r = self.r
        self._between().wait_recv()
        total = r.task_slots[0]
        for index in range(1, r.task_slots.shape[0]):
            total = total + r.task_slots[index]
        r.o_vectors[...] = total

    def finish(self):
        self._within().wait_send()
        self._between().wait_send()


(
    START, ZERO0, ZERO, PARAMS, NORM0, NORM1, NEED_QUERY, NEED_KEY, NEED_VALUE, PROJ0, PROJ1,
    PROJ2, PROJT1, PAIR00, PAIR01, PAIR02, PAIR03, NEED_MERGE, MERGE0, PAIR10, PAIR11, PAIR12,
    PAIR13, MERGE1, NEED_PROJECT, NEED_MERGE_TWO, DENSE, NEED_EXPAND_LOW, NEED_SHRINK_LOW,
    NEED_SHRINK_HIGH, NEED_EXPAND_HIGH, DENSE_GRADS, FEATURE_GRADS, LAYER_END, MERGED0,
    BACK00, BACK01, BACK02, BACK03, MERGED1, BACK10, BACK11, BACK12, BACK13, LOW_GRADS,
    HIGH_GRADS, FIRST0, FIRST1, FIRST2, FIRST3, VECTORS_READY, END,
) = range(52)
NORM_POINTS = (NORM0, NORM1)
PROJECT_POINTS = (PROJ0, PROJ1, PROJ2)
UNTIL_POINTS = (NEED_QUERY, NEED_KEY, NEED_VALUE)
MERGE_POINTS = (MERGE0, MERGE1)
MERGED_POINTS = (MERGED0, MERGED1)
PAIR_POINTS = ((PAIR00, PAIR01, PAIR02, PAIR03), (PAIR10, PAIR11, PAIR12, PAIR13))
BACK_POINTS = ((BACK00, BACK01, BACK02, BACK03), (BACK10, BACK11, BACK12, BACK13))
FIRST_POINTS = (FIRST0, FIRST1, FIRST2, FIRST3)
QUERY, KEY, VALUE, MERGE_ONE, MERGE_TWO, PROJECT_TWO = range(6)
EXPAND_LOW, EXPAND_HIGH, SHRINK_LOW, SHRINK_HIGH = range(6, 10)
D_SHRINK_LOW, D_SHRINK_HIGH, D_EXPAND_LOW, D_EXPAND_HIGH = range(10, 14)
D_PROJECT_TWO, D_PROJECT_TWO_HIGH, D_MERGE_TWO, D_MERGE_ONE = range(14, 18)
D_PROJECT_LOW, D_PROJECT_HIGH, VECTOR_SUMS = range(18, 21)
WIDE = {
    KEY, MERGE_TWO, EXPAND_HIGH, D_SHRINK_LOW, D_SHRINK_HIGH,
}
DIRECT = {
    QUERY, KEY, VALUE, EXPAND_LOW, D_MERGE_TWO, D_MERGE_ONE, D_PROJECT_LOW, D_PROJECT_HIGH,
}
UPSTREAM = {0: (0, 0), 1: (1, 9)}
SCHEDULE = {
    START: (
        (VALUE, Gather.start),
        (QUERY, Gather.start),
        (MERGE_ONE, Gather.start),
        (KEY, Gather.start),
        (SHRINK_HIGH, Gather.start),
        (PROJECT_TWO, Gather.start),
        (MERGE_TWO, Gather.start),
        (EXPAND_LOW, Gather.start),
        (SHRINK_LOW, Gather.start),
        (EXPAND_HIGH, Gather.start),
    ),
    PARAMS: (
        (VALUE, Gather.along_y),
    ),
    NORM1: (
        (QUERY, Gather.along_y),
        (MERGE_ONE, Gather.middle),
    ),
    NEED_QUERY: (
        (SHRINK_HIGH, Gather.middle),
        (VALUE, Gather.along_x),
        (KEY, Gather.along_y),
        (PROJECT_TWO, Gather.middle),
        (MERGE_TWO, Gather.middle),
        (QUERY, Gather.along_x),
        (MERGE_ONE, Gather.outward),
        (EXPAND_LOW, Gather.along_y),
        (SHRINK_LOW, Gather.middle),
        (VALUE, Gather.core),
        (SHRINK_HIGH, Gather.outward),
        (KEY, Gather.core),
        (EXPAND_HIGH, Gather.middle),
        (MERGE_ONE, Gather.along_y),
        (PROJECT_TWO, Gather.outward),
        (QUERY, Gather.core),
        (MERGE_TWO, Gather.outward),
        (SHRINK_HIGH, Gather.along_y),
        (EXPAND_LOW, Gather.along_x),
    ),
    PROJ2: (
        (SHRINK_LOW, Gather.outward),
        (MERGE_ONE, Gather.along_x),
    ),
    PAIR00: (
        (PROJECT_TWO, Gather.along_y),
    ),
    PAIR01: (
        (MERGE_TWO, Gather.along_y),
        (EXPAND_HIGH, Gather.outward),
    ),
    PAIR02: (
        (SHRINK_HIGH, Gather.along_x),
        (SHRINK_LOW, Gather.along_y),
    ),
    NEED_MERGE: (
        (EXPAND_LOW, Gather.core),
        (MERGE_ONE, Gather.core),
    ),
    PAIR10: (
        (PROJECT_TWO, Gather.along_x),
    ),
    PAIR11: (
        (SHRINK_HIGH, Gather.core),
    ),
    PAIR12: (
        (EXPAND_HIGH, Gather.along_y),
        (MERGE_TWO, Gather.core),
    ),
    NEED_PROJECT: (
        (SHRINK_LOW, Gather.along_x),
        (PROJECT_TWO, Gather.core),
    ),
    NEED_SHRINK_LOW: (
        (SHRINK_LOW, Gather.core),
        (EXPAND_HIGH, Gather.core),
    ),
    DENSE_GRADS: (
        (D_EXPAND_LOW, Reduce.core),
        (D_SHRINK_LOW, Reduce.core),
        (D_SHRINK_HIGH, Reduce.core),
        (D_EXPAND_HIGH, Reduce.core),
    ),
    LAYER_END: (
        (D_PROJECT_TWO, Reduce.core),
        (D_PROJECT_TWO_HIGH, Reduce.core),
        (D_MERGE_TWO, Reduce.core),
        (D_EXPAND_LOW, Reduce.x),
        (D_SHRINK_LOW, Reduce.y),
        (D_SHRINK_HIGH, Reduce.y),
    ),
    MERGED0: (
        (D_PROJECT_TWO, Reduce.x),
        (D_EXPAND_HIGH, Reduce.x),
        (D_PROJECT_TWO_HIGH, Reduce.x),
        (D_MERGE_TWO, Reduce.x),
    ),
    MERGED1: (
        (D_MERGE_ONE, Reduce.core),
        (D_EXPAND_LOW, Reduce.y),
        (D_PROJECT_TWO, Reduce.y),
        (D_SHRINK_LOW, Reduce.inward),
    ),
    BACK10: (
        (D_MERGE_ONE, Reduce.x),
    ),
    BACK12: (
        (D_EXPAND_HIGH, Reduce.y),
        (D_PROJECT_LOW, Reduce.x),
        (D_SHRINK_LOW, Reduce.over),
    ),
    LOW_GRADS: (
        (D_PROJECT_LOW, Reduce.core),
        (D_SHRINK_HIGH, Reduce.inward),
    ),
    HIGH_GRADS: (
        (D_PROJECT_HIGH, Reduce.core),
    ),
    FIRST0: (
        (D_SHRINK_HIGH, Reduce.over),
        (D_PROJECT_TWO_HIGH, Reduce.y),
    ),
    FIRST1: (
        (D_EXPAND_LOW, Reduce.inward),
        (D_PROJECT_HIGH, Reduce.x),
    ),
    FIRST2: (
        (D_MERGE_TWO, Reduce.y),
        (D_SHRINK_LOW, Reduce.pair),
    ),
    FIRST3: (
        (D_PROJECT_TWO, Reduce.inward),
        (D_MERGE_ONE, Reduce.y),
    ),
    VECTORS_READY: (
        (VECTOR_SUMS, Vectors.spread),
        (D_EXPAND_LOW, Reduce.over),
        (D_SHRINK_HIGH, Reduce.pair),
    ),
    END: (
        (D_EXPAND_HIGH, Reduce.inward),
        (D_SHRINK_LOW, Reduce.twins),
        (D_PROJECT_TWO_HIGH, Reduce.inward),
        (D_PROJECT_TWO, Reduce.over),
        (D_PROJECT_LOW, Reduce.y),
        (D_MERGE_TWO, Reduce.inward),
        (D_EXPAND_LOW, Reduce.pair),
        (D_SHRINK_HIGH, Reduce.twins),
        (D_MERGE_ONE, Reduce.inward),
        (VECTOR_SUMS, Vectors.gather),
        (D_PROJECT_TWO, Reduce.pair),
        (D_EXPAND_HIGH, Reduce.over),
        (D_PROJECT_HIGH, Reduce.y),
        (D_PROJECT_TWO_HIGH, Reduce.over),
        (D_PROJECT_LOW, Reduce.inward),
        (D_MERGE_TWO, Reduce.twins),
        (D_SHRINK_LOW, Reduce.share),
        (D_EXPAND_LOW, Reduce.twins),
        (D_SHRINK_HIGH, Reduce.share),
        (D_MERGE_ONE, Reduce.twins),
        (D_EXPAND_HIGH, Reduce.pair),
        (D_PROJECT_TWO, Reduce.twins),
        (D_MERGE_TWO, Reduce.share),
        (D_PROJECT_TWO_HIGH, Reduce.pair),
        (D_PROJECT_HIGH, Reduce.inward),
        (D_EXPAND_LOW, Reduce.share),
        (D_MERGE_ONE, Reduce.share),
        (D_EXPAND_HIGH, Reduce.twins),
        (D_PROJECT_LOW, Reduce.twins),
        (D_PROJECT_TWO, Reduce.share),
        (D_PROJECT_TWO_HIGH, Reduce.twins),
        (D_PROJECT_HIGH, Reduce.twins),
        (D_EXPAND_HIGH, Reduce.share),
        (D_PROJECT_LOW, Reduce.share),
        (D_PROJECT_TWO_HIGH, Reduce.share),
        (D_PROJECT_HIGH, Reduce.share),
    ),
}


def flat(ref):
    return ref[...].reshape(-1, ref.shape[-1])


def fused_kernel(names, *refs):
    r = types.SimpleNamespace(**dict(zip(names, refs)))
    p = Place()
    tasks, samples, width = r.tokens.shape
    groups = r.hidden_in.shape[0]
    members = r.task_slots.shape[0]
    block_rows = samples // groups
    hidden_units = r.w_expand.shape[-1]
    chunk = 256
    head_scale = (width // HEADS) ** (-0.5)
    pairs = width // PAIR
    parts = samples // PAIR

    held = pltpu.make_async_copy(r.source, r.tokens, r.vector_local.at[1])
    held.start()
    entry = pltpu.get_barrier_semaphore()
    for shift in range(1, groups):
        pl.semaphore_signal(
            entry, inc=1, device_id=(p.task, p.peer(shift, groups)), device_id_type=MESH
        )
    for shift in range(1, members):
        pl.semaphore_signal(
            entry, inc=1, device_id=(lax.rem(p.task + shift, members), p.feat),
            device_id_type=MESH,
        )
    pl.semaphore_wait(entry, groups + members - 2)

    third = width
    gathers = []

    def gather(name, rows=None, columns=None, wide=False, direct=False):
        shard, weight = getattr(r, "s_" + name), getattr(r, "w_" + name)
        if rows is not None:
            shard, weight = shard.at[:, pl.ds(*rows), :], weight.at[:, :, :, pl.ds(*rows), :]
        if columns is not None:
            shard = shard.at[:, :, pl.ds(*columns)]
            weight = weight.at[:, :, :, :, pl.ds(*columns)]
        item = Gather(
            p, len(gathers), shard, weight, r.gather_sent, r.gather_arrived, r.gather_local,
            wide, direct,
        )
        gathers.append(item)
        return item

    deep = r.w_shrink.shape[3] // 2
    half_units = hidden_units // 2
    items = {}
    for index, name, rows, columns in (
        (QUERY, "project_one", None, (0, third)),
        (KEY, "project_one", None, (third, third)),
        (VALUE, "project_one", None, (2 * third, third)),
        (MERGE_ONE, "merge_one", None, None),
        (MERGE_TWO, "merge_two", None, None),
        (PROJECT_TWO, "project_two", None, None),
        (EXPAND_LOW, "expand", None, (0, half_units)),
        (EXPAND_HIGH, "expand", None, (half_units, half_units)),
        (SHRINK_LOW, "shrink", (0, deep), None),
        (SHRINK_HIGH, "shrink", (deep, deep), None),
    ):
        items[index] = gather(name, rows, columns, index in WIDE, index in DIRECT)
    dense_items = (EXPAND_LOW, SHRINK_LOW, SHRINK_HIGH, EXPAND_HIGH)

    def run(point):
        for name, stage in SCHEDULE.get(point, ()):
            stage(items[name])

    def vectors_in():
        most = r.vector_slots.at[pl.ds(0, groups - 1)]
        return remote(most, most, r.vector_sent.at[0], r.vector_arrived.at[0], p.along_y)

    own_vectors = pltpu.make_async_copy(
        r.vectors, r.vector_slots.at[p.feat], r.vector_local.at[0]
    )
    own_vectors.start()
    for shift in range(1, groups):
        remote(
            r.vectors, r.vector_slots.at[p.feat], r.vector_sent.at[0], r.vector_arrived.at[0],
            (p.task, p.peer(shift, groups)),
        ).start()
    run(START)

    def spread(source, target, task, sent, arrived, local):
        def own():
            return pltpu.make_async_copy(
                source.at[task, pl.ds(p.feat * block_rows, block_rows)],
                target.at[p.feat, task], local.at[task],
            )

        def all_of():
            most = target.at[pl.ds(0, groups - 1), task]
            return remote(most, most, sent.at[task], arrived.at[task], p.along_y)

        def start():
            own().start()
            for shift in range(1, groups):
                peer = p.peer(shift, groups)
                remote(
                    source.at[task, pl.ds(peer * block_rows, block_rows)],
                    target.at[p.feat, task], sent.at[task], arrived.at[task], (p.task, peer),
                ).start()

        def wait():
            own().wait()
            all_of().wait_recv()

        def finish():
            all_of().wait_send()

        return types.SimpleNamespace(start=start, wait=wait, finish=finish)

    upstream = [
        spread(
            r.upstream, r.upstream_in, task, r.upstream_sent, r.upstream_arrived,
            r.upstream_local,
        )
        for task in range(tasks)
    ]
    hidden = [
        spread(
            r.grad_mixed, r.hidden_in, task, r.hidden_sent, r.hidden_arrived, r.hidden_local
        )
        for task in range(tasks)
    ]

    for later, (on, at) in UPSTREAM.items():
        if on == -2:
            upstream[later].start()
    for ref in (r.t_project_two, r.t_merge_two, r.vector_sums, r.t_expand, r.t_shrink):
        ref[...] = jnp.zeros_like(ref)
        if ref is r.vector_sums:
            run(ZERO0)
    run(ZERO)
    own_vectors.wait()
    vectors_in().wait_recv()
    lane = lax.broadcasted_iota(jnp.int32, (1, PAIR), 1)
    per_slot = r.vector_slots.shape[1:]
    turned = [pltpu.roll(r.vector_slots[index], PAIR // 2, 1) for index in range(groups)]
    whole = [r.vector_slots[index] for index in range(groups)]
    bias_tiles = hidden_units // groups // PAIR
    for row in range(7):
        tile = bias_tiles + row // 2
        for at in range(groups // 2):
            first = (turned if row % 2 else whole)[2 * at][tile : tile + 1]
            second = (whole if row % 2 else turned)[2 * at + 1][tile : tile + 1]
            r.params[pl.ds(row, 1), pl.ds(at * PAIR, PAIR)] = jnp.where(
                lane < PAIR // 2, first, second
            )
    for at in range(groups * bias_tiles):
        row, tile = divmod(at, width // PAIR)
        r.params[pl.ds(7 + row, 1), pl.ds(tile * PAIR, PAIR)] = whole[at // bias_tiles][
            at % bias_tiles : at % bias_tiles + 1
        ]
    run(PARAMS)
    held.wait()

    def param(row):
        return r.params[pl.ds(row, 1), :]

    def add_vector(row, value):
        r.vector_sums[pl.ds(row, 1), :] += jnp.sum(value, axis=0, keepdims=True)

    def norm_one(task):
        for start in range(0, samples, chunk):
            rows = r.tokens[task, pl.ds(start, chunk), :].astype(F32)
            normed = normalise(rows)[0] * param(0) + param(1)
            r.normed_one[task, pl.ds(start, chunk), :] = normed.astype(BF16)

    for task in range(tasks):
        norm_one(task)
        for later, (on, at) in UPSTREAM.items():
            if on == -1 and at == task:
                upstream[later].start()
        run(NORM_POINTS[task])

    def key_bias(task):
        keys = lax.broadcasted_iota(jnp.int32, (samples, 1), 0)
        return jnp.where(keys < r.counts[task], 0.0, MASKED)

    def live_rows(task, start):
        at = lax.broadcasted_iota(jnp.int32, (chunk, 1), 0) + start
        return jnp.where(at < r.counts[task], 1.0, 0.0)

    def at_pair(pair, points):
        for at, point in enumerate(points):
            if point in SCHEDULE:
                pl.when(pair == at)(functools.partial(run, point))

    def attend_pairs(task, points):
        bias = key_bias(task)

        def one_pair(pair, carry):
            lanes = pl.multiple_of(pair * PAIR, PAIR)
            key = r.triple[task, :, pl.ds(lanes + width, PAIR)]
            value_turned = r.triple[task, :, pl.ds(lanes + 2 * width, PAIR)].T
            for at in range(parts):
                query = r.triple[task, pl.ds(at * PAIR, PAIR), pl.ds(lanes, PAIR)]
                mixed, log_total = attend(query, key, value_turned, bias, head_scale)
                r.mixed_one[task, pl.ds(at * PAIR, PAIR), pl.ds(lanes, PAIR)] = mixed.astype(BF16)
                r.logs_one[pl.ds((task * pairs + pair) * parts + at, 1), :] = log_total
            for later, (on, at) in UPSTREAM.items():
                if on == task and at < pairs:
                    pl.when(pair == at)(upstream[later].start)
            at_pair(pair, points)
            return carry

        lax.fori_loop(0, pairs, one_pair, 0)

    def project(task, part):
        weight = r.w_project_one[:, :, :, :, pl.ds(part * width, width)].reshape(width, width)
        for start in range(0, samples, chunk):
            normed = r.normed_one[task, pl.ds(start, chunk), :]
            r.triple[task, pl.ds(start, chunk), pl.ds(part * width, width)] = nn(
                normed, weight
            ).astype(BF16)

    for name, part in ((QUERY, 0), (KEY, 1), (VALUE, 2)):
        run(UNTIL_POINTS[part])
        items[name].done()
        project(0, part)
        run(PROJECT_POINTS[part])
    for task in range(tasks):
        if task > 0:
            for part in range(3):
                project(task, part)
            run(PROJT1)
        attend_pairs(task, PAIR_POINTS[task])
        if task == 0:
            run(NEED_MERGE)
            items[MERGE_ONE].done()
        for start in range(0, samples, chunk):
            rows = r.tokens[task, pl.ds(start, chunk), :].astype(F32)
            merged = nn(r.mixed_one[task, pl.ds(start, chunk), :], flat(r.w_merge_one))
            summed = rows + live_rows(task, start) * merged
            r.grad_mixed[task, pl.ds(start, chunk), :] = summed.astype(BF16)
        hidden[task].start()
        for later, (on, at) in UPSTREAM.items():
            if on == task and at >= pairs:
                upstream[later].start()
        run(MERGE_POINTS[task])

    for task in range(tasks):
        r.turned_one[task] = r.normed_one[task].T
    size = groups * GROUP
    blocks = chunk // size
    piece = blocks * GROUP
    per_task = block_rows // piece

    def own_piece(source, target, task, start, semaphore):
        return pltpu.make_async_copy(
            source.at[p.feat, task, pl.ds(start, piece)],
            target.at[task, pl.ds(p.feat * block_rows + start, piece)], semaphore,
        )

    def send_back(source, target, task, start, sent, arrived, local):
        own_piece(source, target, task, start, local).start()
        for shift in range(1, groups):
            peer = p.peer(shift, groups)
            remote(
                source.at[peer, task, pl.ds(start, piece)],
                target.at[task, pl.ds(p.feat * block_rows + start, piece)],
                sent, arrived, (p.task, peer),
            ).start()

    def send_out(task, begin):
        send_back(
            r.upstream_in, r.layer_out, task, begin,
            r.out_sent.at[0], r.out_arrived.at[0], r.out_local.at[0],
        )

    reductions = []

    def reduction(name, total, staged):
        index = len(reductions)
        item = Reduce(
            p, index, total, staged,
            [getattr(r, "m%d_%s" % (index, kind), None) for kind in BUFFERS],
            r.reduce_sent, r.reduce_arrived, name in WIDE, name in DIRECT,
        )
        reductions.append(item)
        return item

    def part_of(ref, rows=None, columns=None):
        if rows is not None:
            return ref.at[:, :, :, pl.ds(*rows), :]
        return ref.at[:, :, :, :, pl.ds(*columns)]

    for at, index in enumerate((D_SHRINK_LOW, D_SHRINK_HIGH)):
        cut = (at * deep, deep)
        items[index] = reduction(index, part_of(r.t_shrink, cut), part_of(r.w_shrink, cut))
    for at, index in enumerate((D_EXPAND_LOW, D_EXPAND_HIGH)):
        cut = (at * half_units, half_units)
        items[index] = reduction(
            index, part_of(r.t_expand, None, cut), part_of(r.w_expand, None, cut)
        )
    wide_half = 3 * width // 2
    low_half, high_half = (0, wide_half), (wide_half, wide_half)
    for index, total, staged in (
        (D_PROJECT_TWO, part_of(r.t_project_two, None, low_half), part_of(r.w_project_two, None, low_half)),
        (D_PROJECT_TWO_HIGH, part_of(r.t_project_two, None, high_half), part_of(r.w_project_two, None, high_half)),
        (D_MERGE_TWO, r.t_merge_two, r.w_merge_two),
        (D_MERGE_ONE, r.t_merge_one, r.w_merge_one),
        (D_PROJECT_LOW, r.t_low, r.b_low), (D_PROJECT_HIGH, r.t_high, r.b_high),
    ):
        items[index] = reduction(index, total, staged)

    def layer_chunk(step, carry):
        task = lax.div(step, per_task)
        begin = pl.multiple_of(lax.rem(step, per_task) * piece, piece)

        first = step == 0
        final = step == tasks * per_task - 1

        @pl.when(first)
        def _():
            run(NEED_PROJECT)
            items[PROJECT_TWO].done()
            hidden[0].wait()

        for later in range(1, tasks):
            @pl.when(step == later * per_task)
            def _():
                hidden[later].wait()

        def load(ref):
            pieces = [
                ref[:, task, pl.ds(begin + block * GROUP, GROUP), :].reshape(size, width)
                for block in range(blocks)
            ]
            return pieces[0] if blocks == 1 else jnp.concatenate(pieces, axis=0)

        def store(ref, values):
            for block in range(blocks):
                part = values[block * size : (block + 1) * size].reshape(groups, GROUP, width)
                ref[:, task, pl.ds(begin + block * GROUP, GROUP), :] = part

        row = lax.broadcasted_iota(jnp.int32, (chunk, 1), 0)
        row = (row // size) * GROUP + row % GROUP + begin + p.feat * block_rows
        live = jnp.where(row < r.counts[task], 1.0, 0.0)

        hidden_one = load(r.hidden_in).astype(F32)
        unit_two, scale_two = normalise(hidden_one)
        normed_two = (unit_two * param(2) + param(3)).astype(BF16)
        r.part_triple[...] = nn(normed_two, flat(r.w_project_two)).astype(BF16)
        reach = min(PAIR, size)
        key_at = lax.broadcasted_iota(jnp.int32, (size, 2 * reach), 0) % GROUP
        query_at = lax.broadcasted_iota(jnp.int32, (size, 2 * reach), 1) % GROUP
        bias = jnp.where(key_at == query_at, 0.0, MASKED)
        for block in range(blocks):
            where = pl.ds(block * size, size)
            for pair in range(pairs):
                lanes = pair * PAIR
                key = r.part_triple[where, pl.ds(width + lanes, PAIR)]
                value_turned = r.part_triple[where, pl.ds(2 * width + lanes, PAIR)].T
                query = r.part_triple[where, pl.ds(lanes, PAIR)]
                result, log_total = attend(query, key, value_turned, bias, head_scale)
                r.block_mixed[where, pl.ds(lanes, PAIR)] = result.astype(BF16)
                r.block_logs[pl.ds(block * pairs + pair, 1), :] = log_total

        @pl.when(first)
        def _():
            run(NEED_MERGE_TWO)
            items[MERGE_TWO].done()

        hidden_two = hidden_one + live * nn(r.block_mixed[...], flat(r.w_merge_two))
        unit_three, scale_three = normalise(hidden_two)
        normed_three = (unit_three * param(4) + param(5)).astype(BF16)
        @pl.when(first)
        def _():
            run(DENSE)
            upstream[0].wait()

        for later in range(1, tasks):
            @pl.when(step == later * per_task)
            def _():
                upstream[later].wait()

        flow = load(r.upstream_in).astype(F32)
        grad_dense = (flow * live).astype(BF16)
        add_vector(6, grad_dense.astype(F32))

        @pl.when(first)
        def _():
            run(NEED_EXPAND_LOW)
            items[EXPAND_LOW].done()
            run(NEED_SHRINK_LOW)
            items[SHRINK_LOW].done()
            run(NEED_SHRINK_HIGH)
            items[SHRINK_HIGH].done()

        turned_three = normed_three.T
        dense = None
        incoming = None
        lanes = hidden_units // DEPTH
        for turn in range(DEPTH):
            cut = pl.ds(turn * lanes, lanes)
            if turn == DEPTH // 2:
                @pl.when(first)
                def _():
                    run(NEED_EXPAND_HIGH)
                    items[EXPAND_HIGH].done()

            up_weight = r.w_expand[:, :, :, :, cut].reshape(width, lanes)
            down_weight = r.w_shrink[turn].reshape(lanes, width)
            expanded = nn(normed_three, up_weight) + param(7 + turn)
            square = expanded * expanded
            steep = 0.7978845608028654
            bend = jnp.tanh(expanded * (steep + (steep * 0.044715) * square))
            half_up = 0.5 + 0.5 * bend
            activated = (expanded * half_up).astype(BF16)
            slope = half_up + (0.5 * expanded) * (1.0 - bend * bend) * (
                steep + (3.0 * steep * 0.044715) * square
            )
            grad_expanded = (slope * nt(grad_dense, down_weight)).astype(BF16)
            add_vector(7 + turn, grad_expanded.astype(F32))
            r.t_shrink[turn] += tn(activated, grad_dense).reshape(r.t_shrink.shape[1:])
            r.t_expand[:, :, :, :, cut] += nn(turned_three, grad_expanded).reshape(
                r.t_expand.shape[:4] + (lanes,)
            )
            up = nn(activated, down_weight)
            down = nt(grad_expanded, up_weight)
            dense = up if dense is None else dense + up
            incoming = down if incoming is None else incoming + down
        @pl.when(final)
        def _():
            for name in dense_items:
                items[name].finish()
            run(DENSE_GRADS)

        result = hidden_two + live * (dense + param(6))
        store(r.upstream_in, result.astype(BF16))

        add_vector(4, incoming * unit_three)
        add_vector(5, incoming)
        flow = flow + normalise_back(incoming, unit_three, scale_three, param(4))
        branch = (flow * live).astype(BF16)
        r.t_merge_two[...] += tn(r.block_mixed[...], branch).reshape(r.t_merge_two.shape)
        r.block_grad[...] = nt(branch, flat(r.w_merge_two)).astype(BF16)

        @pl.when(final)
        def _():
            run(FEATURE_GRADS)

        for block in range(blocks):
            where = pl.ds(block * size, size)
            for pair in range(pairs):
                lanes = pair * PAIR
                key = r.part_triple[where, pl.ds(width + lanes, PAIR)]
                value = r.part_triple[where, pl.ds(2 * width + lanes, PAIR)]
                query = r.part_triple[where, pl.ds(lanes, PAIR)]
                grad_query, grad_key, grad_value = attend_back(
                    query, key, value, key.T, r.block_mixed[where, pl.ds(lanes, PAIR)],
                    r.block_grad[where, pl.ds(lanes, PAIR)], r.block_logs[pl.ds(block * pairs + pair, 1), :], bias, head_scale,
                )
                r.part_triple[where, pl.ds(lanes, PAIR)] = grad_query.astype(BF16)
                r.part_triple[where, pl.ds(width + lanes, PAIR)] = grad_key.astype(BF16)
                r.part_triple[where, pl.ds(2 * width + lanes, PAIR)] = grad_value.astype(BF16)
        grad_triple = r.part_triple[...]
        r.t_project_two[...] += tn(normed_two, grad_triple).reshape(r.t_project_two.shape)
        incoming = nt(grad_triple, flat(r.w_project_two))
        add_vector(2, incoming * unit_two)
        add_vector(3, incoming)
        flow = flow + normalise_back(incoming, unit_two, scale_two, param(2))
        store(r.hidden_in, flow.astype(BF16))
        send_back(
            r.hidden_in, r.flow, task, begin,
            r.flow_sent.at[0], r.flow_arrived.at[task], r.flow_local.at[task],
        )

        @pl.when(task < tasks - 1)
        def _():
            send_out(task, begin)

        return carry

    lax.fori_loop(0, tasks * per_task, layer_chunk, 0)

    for name in (QUERY, KEY, VALUE, MERGE_ONE, PROJECT_TWO, MERGE_TWO):
        items[name].finish()
    for task in range(tasks):
        hidden[task].finish()
    run(LAYER_END)

    def flow_in(task):
        most = r.flow.at[task, pl.ds(0, samples - block_rows)]
        return remote(most, most, r.flow_sent.at[0], r.flow_arrived.at[task], p.along_y)

    def wait_flow(task):
        flow_in(task).wait_recv()
        own = r.flow.at[task, pl.ds(0, block_rows)]
        pltpu.make_async_copy(own, own, r.flow_local.at[task]).wait()

    def merge_back(task):
        for start in range(0, samples, chunk):
            live = live_rows(task, start)
            branch = (r.flow[task, pl.ds(start, chunk), :].astype(F32) * live).astype(BF16)
            part = tn(r.mixed_one[task, pl.ds(start, chunk), :], branch)
            part = part.reshape(r.t_merge_one.shape)
            if task == 0 and start == 0:
                r.t_merge_one[...] = part
            else:
                r.t_merge_one[...] += part
            r.grad_mixed[task, pl.ds(start, chunk), :] = nt(branch, flat(r.w_merge_one)).astype(BF16)

    def attend_pairs_back(task, points):
        bias = key_bias(task)

        def one_pair(pair, carry):
            lanes = pl.multiple_of(pair * PAIR, PAIR)
            key = r.triple[task, :, pl.ds(lanes + width, PAIR)]
            value = r.triple[task, :, pl.ds(lanes + 2 * width, PAIR)]
            key_turned = key.T
            for at in range(parts):
                query = r.triple[task, pl.ds(at * PAIR, PAIR), pl.ds(lanes, PAIR)]
                grad_out = r.grad_mixed[task, pl.ds(at * PAIR, PAIR), pl.ds(lanes, PAIR)]
                log_total = r.logs_one[pl.ds((task * pairs + pair) * parts + at, 1), :]
                grad_query, grad_key, grad_value = attend_back(
                    query, key, value, key_turned,
                    r.mixed_one[task, pl.ds(at * PAIR, PAIR), pl.ds(lanes, PAIR)],
                    grad_out, log_total, bias, head_scale,
                )
                r.triple[task, pl.ds(at * PAIR, PAIR), pl.ds(lanes, PAIR)] = grad_query.astype(BF16)
                if at == 0:
                    r.slab[0, pl.ds(0, samples), :] = grad_key
                    r.slab[1, pl.ds(0, samples), :] = grad_value
                else:
                    r.slab[0, pl.ds(0, samples), :] += grad_key
                    r.slab[1, pl.ds(0, samples), :] += grad_value
            r.triple[task, :, pl.ds(lanes + width, PAIR)] = r.slab[0, pl.ds(0, samples), :].astype(BF16)
            r.triple[task, :, pl.ds(lanes + 2 * width, PAIR)] = r.slab[1, pl.ds(0, samples), :].astype(BF16)
            at_pair(pair, points)
            if task == tasks - 1:
                @pl.when(pair == half - 1)
                def _():
                    project_weight(0)
                    run(LOW_GRADS)

            return carry

        lax.fori_loop(0, pairs, one_pair, 0)

    def project_weight(which):
        ref = (r.t_low, r.t_high)[which]
        lanes = width // 2
        for third in range(3):
            cut = pl.ds(third * width + which * lanes, lanes)
            part = None
            for task in range(tasks):
                one = nn(r.turned_one[task], r.triple[task, :, cut])
                part = one if part is None else part + one
            ref[:, :, :, :, pl.ds(third * lanes, lanes)] = part.reshape(ref.shape[:4] + (lanes,))

    slabs = []

    def project_back(task, start):
        rows = r.tokens[task, pl.ds(start, chunk), :].astype(F32)
        normed, scale = normalise(rows)
        incoming = nt(r.triple[task, pl.ds(start, chunk), :], flat(r.w_project_one))
        add_vector(0, incoming * normed)
        add_vector(1, incoming)
        back = normalise_back(incoming, normed, scale, param(0))
        back = r.flow[task, pl.ds(start, chunk), :].astype(F32) + back
        tiles = width // PAIR
        slot = len(slabs) % 2
        if len(slabs) > 1:
            slabs[-2].wait()
        for tile in range(tiles):
            r.slab[slot, pl.ds(tile, chunk, stride=tiles), :] = back[
                :, tile * PAIR : (tile + 1) * PAIR
            ]
        copy = pltpu.make_async_copy(
            r.slab.at[slot], r.input_grad.at[task, pl.ds(start * tiles, chunk * tiles)],
            r.o_done.at[len(slabs)],
        )
        copy.start()
        slabs.append(copy)

    half = pairs // 2
    for task in range(tasks):
        wait_flow(task)
        merge_back(task)
        if task == 0:
            for start in range(0, block_rows, piece):
                send_out(tasks - 1, start)
        run(MERGED_POINTS[task])
        attend_pairs_back(task, BACK_POINTS[task])
    project_weight(1)
    run(HIGH_GRADS)
    for task in range(tasks):
        for start in range(0, samples, chunk):
            project_back(task, start)
            run(FIRST_POINTS[task * (samples // chunk) + start // chunk])

    items[VECTOR_SUMS] = Vectors(p, r)
    run(VECTORS_READY)
    run(END)
    written = list(slabs)

    def write(source, target):
        copy = pltpu.make_async_copy(source, target, r.o_done.at[len(written)])
        copy.start()
        written.append(copy)

    for name, target in (
        (D_SHRINK_LOW, r.o_shrink.at[:, pl.ds(0, deep), :]),
        (D_SHRINK_HIGH, r.o_shrink.at[:, pl.ds(deep, deep), :]),
        (D_EXPAND_LOW, r.o_expand.at[:, :, pl.ds(0, half_units)]),
        (D_EXPAND_HIGH, r.o_expand.at[:, :, pl.ds(half_units, half_units)]),
        (D_PROJECT_TWO, r.o_project_two.at[:, :, pl.ds(0, wide_half)]),
        (D_PROJECT_TWO_HIGH, r.o_project_two.at[:, :, pl.ds(wide_half, wide_half)]),
        (D_MERGE_TWO, r.o_merge_two),
        (D_MERGE_ONE, r.o_merge_one),
    ):
        items[name].done()
        write(items[name].final, target)
    items[VECTOR_SUMS].done()
    lanes = width // 2
    for which in range(2):
        item = items[(D_PROJECT_LOW, D_PROJECT_HIGH)[which]]
        item.done()
        for part in range(3):
            write(
                item.final.at[:, :, pl.ds(part * lanes, lanes)],
                r.o_project_one.at[:, :, pl.ds(part * width + which * lanes, lanes)],
            )
    for copy in written[len(slabs) - 2 :]:
        copy.wait()

    vectors_in().wait_send()
    items[VECTOR_SUMS].finish()
    for task in range(tasks):
        upstream[task].finish()
    everywhere = r.flow.at[:, pl.ds(0, samples - block_rows)]
    remote(everywhere, everywhere, r.flow_sent.at[0], r.flow_arrived.at[0], p.along_y).wait_send()
    everywhere = r.layer_out.at[:, pl.ds(0, samples - block_rows)]
    both = remote(everywhere, everywhere, r.out_sent.at[0], r.out_arrived.at[0], p.along_y)
    both.wait_send()
    both.wait_recv()
    own = r.layer_out.at[:, pl.ds(0, block_rows)]
    pltpu.make_async_copy(own, own, r.out_local.at[0]).wait()
    for item in reductions:
        item.finish()


def finish_kernel(*refs):
    count = 9
    sources, targets = refs[:count], refs[count : count + 16]
    held = refs[count + 16 : 2 * count + 16]
    made = refs[2 * count + 16 : 2 * count + 22]
    read, written = refs[2 * count + 22 :]
    reads = [
        pltpu.make_async_copy(source, memory, read.at[at])
        for at, (source, memory) in enumerate(zip(sources, held))
    ]
    for copy in reads:
        copy.start()
    writes = []
    for at in range(2):
        reads[at].wait()
        writes.append(pltpu.make_async_copy(held[at], targets[at], written.at[at]))
        writes[-1].start()
    for at in range(2, 8):
        reads[at].wait()
        made[at - 2][...] = held[at][...].astype(F32)
        writes.append(pltpu.make_async_copy(made[at - 2], targets[at], written.at[at]))
        writes[-1].start()
    reads[8].wait()
    vectors_ref, small_to, bias_to = held[8], targets[8:15], targets[15]
    place = lax.axis_index("feat")
    width = vectors_ref.shape[1]
    size = small_to[0].shape[1]
    turned = pltpu.roll(vectors_ref[...], lax.rem(width - place * size, width), 1)
    for row, target in enumerate(small_to):
        target[...] = turned[row : row + 1, :size]
    size = bias_to.shape[1]
    per_row = width // size
    row = vectors_ref[pl.ds(len(small_to) + lax.div(place, per_row), 1), :]
    bias = row[:, :size]
    for at in range(1, per_row):
        bias = jnp.where(lax.rem(place, per_row) == at, row[:, at * size : (at + 1) * size], bias)
    bias_to[...] = bias
    for copy in writes:
        copy.wait()


def fused_body(tokens, cotangent, counts, *shards):
    (
        gain_one, shift_one, project_one, merge_one, gain_two, shift_two, project_two, merge_two,
        gain_three, shift_three, expand, bias_in, shrink, bias_out,
    ) = shards
    groups = lax.axis_size("feat")
    members = lax.axis_size("task")
    place = lax.axis_index("feat")
    tasks, samples, _, width = tokens.shape
    block_rows = samples // groups
    hidden_units = expand.shape[1]
    pairs = width // PAIR

    small = (
        gain_one, shift_one, gain_two, shift_two, gain_three, shift_three, bias_out,
    )
    length = sum(part.shape[0] for part in (bias_in,) + small)
    slots = -(-length // (8 * PAIR)) * 8
    vectors, low = None, 0
    for part in (bias_in,) + small:
        high = slots * PAIR - low - part.shape[0]
        moved = jnp.pad(part.astype(F32), (low, high))
        vectors = moved if vectors is None else vectors + moved
        low += part.shape[0]
    vectors = vectors.reshape(slots, PAIR)

    big = {
        "project_one": project_one, "merge_one": merge_one, "project_two": project_two,
        "merge_two": merge_two, "expand": expand, "shrink": shrink,
    }
    names, operands, specs = [], [], []

    def operand(name, value, spec):
        names.append(name)
        operands.append(value)
        specs.append(spec)

    any_spec = pl.BlockSpec(memory_space=pl.ANY)
    operand("counts", counts, SMEM)
    operand("source", tokens.reshape(tasks, samples, width), any_spec)
    operand("upstream", cotangent.reshape(tasks, samples, width), any_spec)
    operand("vectors", vectors, any_spec)
    shapes = {}
    for name, shard in big.items():
        rows, columns = shard.shape[0] // SPLIT, shard.shape[1]
        shapes[name] = (rows, columns)
        operand("s_" + name, shard.reshape(SPLIT, rows, columns), any_spec)

    outs, out_specs = [], []

    def output(name, dims, kind, spec):
        names.append(name)
        outs.append(shape(dims, kind))
        out_specs.append(spec)

    output("layer_out", (tasks, samples, width), BF16, any_spec)
    output("input_grad", (tasks, samples * width // PAIR, PAIR), F32, any_spec)
    for name in big:
        output("o_" + name, (SPLIT,) + shapes[name], BF16, any_spec)
    output("o_vectors", (VECTORS, width), F32, VMEM)

    scratch = []

    def memory(name, dims, kind):
        names.append(name)
        scratch.append(pltpu.VMEM(dims, kind))

    def semaphores(name, dims):
        names.append(name)
        scratch.append(pltpu.SemaphoreType.DMA(dims))

    for name in big:
        memory("w_" + name, (DEPTH, WIDE_Y, SPLIT) + shapes[name], BF16)
    for name in big:
        if name != "project_one":
            memory("t_" + name, (DEPTH, WIDE_Y, SPLIT) + shapes[name], F32)
    rows, columns = shapes["project_one"]
    for name in ("low", "high"):
        memory("t_" + name, (DEPTH, WIDE_Y, SPLIT, rows, columns // 2), F32)
        memory("b_" + name, (DEPTH, WIDE_Y, SPLIT, rows, columns // 2), BF16)
    rows, columns = shapes["shrink"]
    shrink_part = (rows // 2, columns)
    rows, columns = shapes["expand"]
    expand_part = (rows, columns // 2)
    rows, columns = shapes["project_one"]
    half_project = (rows, columns // 2)
    items = (
        (shrink_part, D_SHRINK_LOW), (shrink_part, D_SHRINK_HIGH),
        (expand_part, D_EXPAND_LOW), (expand_part, D_EXPAND_HIGH),
        (half_project, D_PROJECT_TWO), (half_project, D_PROJECT_TWO_HIGH), (shapes["merge_two"], D_MERGE_TWO),
        (shapes["merge_one"], D_MERGE_ONE), (half_project, D_PROJECT_LOW),
        (half_project, D_PROJECT_HIGH),
    )
    for index, (dims, name) in enumerate(items):
        wide, direct = name in WIDE, name in DIRECT
        count = HALVES if wide else 1
        sizes = {
            "halves": (DEPTH, WIDE_Y, HALVES), "quarters": (DEPTH, WIDE_Y, 1),
            "lines": (DEPTH, count), "outer": (DEPTH - 1 if direct else 2, count),
            "crossed": (2, count), "paired": (count,), "final": (SPLIT,), "twin": (count,),
        }
        unused = {"quarters" if wide else "twin"}
        if direct:
            unused |= {"crossed", "paired"}
        for kind in BUFFERS:
            if kind not in unused:
                memory("m%d_%s" % (index, kind), sizes[kind] + dims, BF16)
    memory("vector_slots", (groups, slots, PAIR), F32)
    memory("params", (VECTORS, width), F32)
    memory("vector_sums", (VECTORS, width), F32)
    memory("vector_back", (groups, VECTORS, width), F32)
    memory("vector_total", (VECTORS, width), F32)
    memory("task_slots", (members, VECTORS, width), F32)
    memory("tokens", (tasks, samples, width), BF16)
    memory("normed_one", (tasks, samples, width), BF16)
    memory("turned_one", (tasks, width, samples), BF16)
    memory("triple", (tasks, samples, 3 * width), BF16)
    memory("mixed_one", (tasks, samples, width), BF16)
    memory("logs_one", (tasks * pairs * (samples // PAIR), 2 * PAIR), F32)
    memory("grad_mixed", (tasks, samples, width), BF16)
    memory("flow", (tasks, samples, width), BF16)
    memory("hidden_in", (groups, tasks, block_rows, width), BF16)
    memory("upstream_in", (groups, tasks, block_rows, width), BF16)
    memory("part_triple", (256, 3 * width), BF16)
    memory("block_mixed", (256, width), BF16)
    memory("block_grad", (256, width), BF16)
    memory("block_logs", (8, 2 * PAIR), F32)
    memory("slab", (2, 256 * width // PAIR, PAIR), F32)
    semaphores("gather_sent", (10, 6))
    semaphores("gather_arrived", (10, 6))
    semaphores("gather_local", (10,))
    semaphores("reduce_sent", (len(items), 8))
    semaphores("reduce_arrived", (len(items), 8))
    for name in ("vector_sent", "vector_arrived"):
        semaphores(name, (3,))
    semaphores("vector_local", (2,))
    semaphores("o_done", (tasks * samples // 256 + 14,))
    for name in ("upstream", "hidden"):
        for kind in ("_sent", "_arrived", "_local"):
            semaphores(name + kind, (tasks,))
    semaphores("flow_sent", (1,))
    semaphores("flow_arrived", (tasks,))
    semaphores("flow_local", (tasks,))
    for kind in ("_sent", "_arrived", "_local"):
        semaphores("out" + kind, (1,))

    results = pl.pallas_call(
        functools.partial(fused_kernel, tuple(names)),
        in_specs=specs,
        out_specs=out_specs,
        out_shape=outs,
        scratch_shapes=scratch,
        compiler_params=pltpu.CompilerParams(
            vmem_limit_bytes=FUSED_LIMIT, collective_id=0, has_side_effects=True
        ),
        name="layer",
    )(*operands)
    outs = [
        shape((tasks, samples, width), BF16),
        shape((tasks, samples * width // PAIR, PAIR), F32),
    ]
    outs += [shape((SPLIT,) + shapes[name], F32) for name in big]
    outs += [shape((1, part.shape[0]), F32) for part in small]
    outs += [shape((1, bias_in.shape[0]), F32)]
    finished = pl.pallas_call(
        finish_kernel,
        in_specs=[any_spec] * len(results),
        out_specs=[any_spec] * (2 + len(big)) + [VMEM] * (len(small) + 1),
        out_shape=outs,
        scratch_shapes=[pltpu.VMEM(result.shape, result.dtype) for result in results]
        + [pltpu.VMEM(out.shape, F32) for out in outs[2 : 2 + len(big)]]
        + [pltpu.SemaphoreType.DMA((len(results),))] * 2,
        compiler_params=pltpu.CompilerParams(vmem_limit_bytes=FINISH_LIMIT),
        name="finish",
    )(*results)
    grads = {
        name: result.reshape(big[name].shape) for name, result in zip(big, finished[2:])
    }
    ends = [part.reshape(-1) for part in finished[2 + len(big):]]
    return (
        finished[0].reshape(tokens.shape), finished[1].reshape(tokens.shape),
        ends[0], ends[1], grads["project_one"], grads["merge_one"],
        ends[2], ends[3], grads["project_two"], grads["merge_two"],
        ends[4], ends[5], grads["expand"], ends[7], grads["shrink"], ends[6],
    )


def solution(mesh):
    wide = P("task", None, "feat", None)
    row, grid = P("feat"), P("feat", None)
    weights = (
        row, row, grid, grid, row, row, grid, grid, row, row, grid, row, grid, row,
    )
    fits = mesh.shape["feat"] == DEPTH * WIDE_Y and mesh.shape["task"] == CORES * HALVES
    return jax.shard_map(
        fused_body if fits else body,
        mesh=mesh,
        in_specs=(wide, wide, P("task")) + weights,
        out_specs=(wide, wide) + weights,
        check_vma=False,
    )
```
